32 devices in a mesh: frames: 8 (over z, x), rows: 4 (over y, core).
Axes of the slice: x: 2, y: 2, z: 4, core: 2. Of those that a mesh axis runs over, the one named last changes fastest.
Arguments:
- frames_in: bfloat16 [448, 197, 768], P(('frames', 'rows')), may hold values from -6 to 6
- cotangent: bfloat16 [448, 197, 768], P(('frames', 'rows')), may hold values from -6 to 6
- video_ids: int32 [448], P(('frames', 'rows')), may hold values from 0 to 511, as said below
- frame_device: int32 [448], P(('frames', 'rows')), may hold values from 0 to 7, as said below
- msg_weight: bfloat16 [768, 768], replicated, may hold values from -0.21875 to 0.21875
- msg_gain: float32 [768], replicated, may hold values from 0.5 to 1.5
- msg_qkv: bfloat16 [768, 2304], replicated, may hold values from -0.21875 to 0.21875
- msg_out: bfloat16 [768, 768], replicated, may hold values from -0.625 to 0.625
- attn_gain: float32 [768], replicated, may hold values from 0.5 to 1.5
- attn_qkv: bfloat16 [768, 2304], replicated, may hold values from -0.21875 to 0.21875
- attn_out: bfloat16 [768, 768], replicated, may hold values from -1.75 to 1.75
- mlp_gain: float32 [768], replicated, may hold values from 0.5 to 1.5
- up_weight: bfloat16 [768, 3072], replicated, may hold values from -0.21875 to 0.21875
- down_weight: bfloat16 [3072, 768], replicated, may hold values from -0.109375 to 0.109375
Outputs:
- output: bfloat16 [448, 197, 768], P(('frames', 'rows'))
- grad_in: bfloat16 [448, 197, 768], P(('frames', 'rows'))
- grad_msg_weight: float32 [768, 768], P('frames', 'rows')
- grad_msg_gain: float32 [768], P('frames')
- grad_msg_qkv: float32 [768, 2304], P('frames', 'rows')
- grad_msg_out: float32 [768, 768], P('frames', 'rows')
- grad_attn_gain: float32 [768], P('frames')
- grad_attn_qkv: float32 [768, 2304], P('frames', 'rows')
- grad_attn_out: float32 [768, 768], P('frames', 'rows')
- grad_mlp_gain: float32 [768], P('frames')
- grad_up_weight: float32 [768, 3072], P('frames', 'rows')
- grad_down_weight: float32 [3072, 768], P('frames', 'rows')
The draws below stay inside these ranges and needn't reach their ends.
Inputs may be any that keep to these rules, and one draw needn't show every extreme that they name: `frame_device`: all frames of one video lie on devices with the same index along rows and name the same device. Of the 14 frames of one device at most 2 name the same device, and some device receives 2 from every device of its index along rows. `video_ids`: frames with one id form one video of at most 16 frames.
All inputs are finite; a program needn't handle non-finite values.
Results may differ from the reference program's by a relative error of at most 0.025.
Values may be sent and summed in bfloat16 or wider, within the bound.
No kernel may reach another device: no remote copies, remote signals or barrier semaphores. Data moves between devices by JAX's collectives and lax.ppermute only.
A program may use at most 256 MiB of HBM per device.

```python
import jax
import jax.numpy as jnp
from jax import lax

D = 768
H = 12
HD = 64
FF = 3072
P_SIZE = 197
FR_DEV = 14
CAP = 2
FRAMES = 448
N_FRAMES = 8
N_ROWS = 4


def routing(key):
    base = jax.random.fold_in(key, 4242)
    key_hot, key_score, key_length, key_table = jax.random.split(base, 4)
    slot_total = N_FRAMES * CAP
    block_count = N_FRAMES * N_ROWS
    hot_count = max(1, N_FRAMES // 16)
    ranking = jax.random.permutation(key_hot, N_FRAMES)
    favour = jnp.where(ranking < hot_count, 1 << 16, 0).astype(jnp.int32)
    candidate = jnp.arange(slot_total, dtype=jnp.int32)
    receiver = candidate // CAP
    noise = jax.random.randint(key_score, (block_count, slot_total), 0, 1 << 16, dtype=jnp.int32)
    score = (noise + favour[receiver][None, :]) * slot_total + candidate[None, :]
    top_scores, picked = lax.top_k(score, FR_DEV)
    device_map = (picked // CAP).reshape(FRAMES).astype(jnp.int32)
    block_of = jnp.arange(FRAMES, dtype=jnp.int32) // FR_DEV
    group_of = block_of % N_ROWS
    owner_key = group_of * N_FRAMES + device_map
    onehot = (owner_key[:, None] == jnp.arange(block_count, dtype=jnp.int32)[None, :]).astype(jnp.int32)
    before = jnp.cumsum(onehot, axis=0) - onehot
    rank = jnp.sum(before * onehot, axis=1)
    long_pick = jax.random.randint(key_length, (block_count,), 0, 4, dtype=jnp.int32)
    video_length = jnp.where(long_pick[owner_key] == 0, 16, 8)
    raw_ids = owner_key * slot_total + rank // video_length
    table = jax.random.permutation(key_table, block_count * slot_total).astype(jnp.int32)
    return (device_map, table[raw_ids])


def draw_video_ids(key, part):
    return routing(key)[1]


def draw_frame_device(key, part):
    return routing(key)[0]


def shard_levels(key, extent, cuts, smallest, largest):
    loudness, own = 1.0, jax.random.fold_in(key, 6)
    for axis_at, blocks in cuts:
        steps = jnp.exp(jax.random.uniform(jax.random.fold_in(own, axis_at), (blocks,), jnp.float32, smallest / len(cuts), largest / len(cuts)))
        loudness = loudness * jnp.repeat(steps, extent[axis_at] // blocks).reshape([-1 if axis == axis_at else 1 for axis in range(len(extent))])
    return loudness


def gaussian(stream_key, shape, deviation, reach, pieces=(), kind=jnp.bfloat16):
    entries = jax.random.normal(stream_key, shape, jnp.float32) * deviation
    if len(pieces) > 0:
        entries = shard_levels(stream_key, shape, pieces, -0.22, 0.18) * entries
    return jnp.clip(entries, min=-reach, max=reach).astype(kind)


def setup_inputs(seed: int = 0) -> dict:
    arg_keys = jax.random.split(jax.random.key(seed), 15)
    frames_in = gaussian(arg_keys[0], (FRAMES, P_SIZE, D), 1.0, 6.0, ((0, 32),))
    cotangent = gaussian(arg_keys[1], (FRAMES, P_SIZE, D), 1.0, 6.0, ((0, 32),))
    video_ids = draw_video_ids(jax.random.fold_in(arg_keys[14], 71), 0)
    frame_device = draw_frame_device(jax.random.fold_in(arg_keys[14], 71), 0)
    msg_weight = gaussian(arg_keys[4], (D, D), D ** -0.5, 0.21875)
    msg_gain = jnp.clip(1.0 + 0.1 * jax.random.normal(arg_keys[5], (D,), jnp.float32), 0.5, 1.5)
    msg_qkv = gaussian(arg_keys[6], (D, 3 * D), D ** -0.5, 0.21875)
    msg_out = gaussian(arg_keys[7], (D, D), (D // 8) ** -0.5, 0.625)
    attn_gain = jnp.clip(1.0 + 0.1 * jax.random.normal(arg_keys[8], (D,), jnp.float32), 0.5, 1.5)
    attn_qkv = gaussian(arg_keys[9], (D, 3 * D), D ** -0.5, 0.21875)
    attn_out = gaussian(arg_keys[10], (D, D), (D // 64) ** -0.5, 1.75)
    mlp_gain = jnp.clip(1.0 + 0.1 * jax.random.normal(arg_keys[11], (D,), jnp.float32), 0.5, 1.5)
    up_weight = gaussian(arg_keys[12], (D, FF), D ** -0.5, 0.21875)
    down_weight = gaussian(arg_keys[13], (FF, D), FF ** -0.5, 0.109375)
    return dict(frames_in=frames_in, cotangent=cotangent, video_ids=video_ids, frame_device=frame_device, msg_weight=msg_weight, msg_gain=msg_gain, msg_qkv=msg_qkv, msg_out=msg_out, attn_gain=attn_gain, attn_qkv=attn_qkv, attn_out=attn_out, mlp_gain=mlp_gain, up_weight=up_weight, down_weight=down_weight)


EPS = 1e-05
HIGH = lax.Precision.HIGHEST

@jax.custom_vjp
def low(v):
    return lax.optimization_barrier(v.astype(jnp.bfloat16)).astype(jnp.float32)

@jax.custom_vjp
def low_back(v):
    return v

def low_keep(v):
    return (low(v), None)

def low_pass(kept, grad):
    return (grad,)

def back_keep(v):
    return (v, None)

def back_low(kept, grad):
    return (low(grad),)
low.defvjp(low_keep, low_pass)
low_back.defvjp(back_keep, back_low)

def matmul_high(operand, matrix):
    return jnp.einsum('...i,ij->...j', operand, matrix, precision=HIGH)

def normalize(values):
    center = values - lax.optimization_barrier(jnp.mean(values, axis=-1, keepdims=True))
    spread = lax.optimization_barrier(jnp.mean(center * center, axis=-1, keepdims=True))
    return center * lax.rsqrt(spread + EPS)

def quick_gelu(values):
    return values * jax.nn.sigmoid(1.702 * values)

def frame_group(params, frames, message_kv):
    attn_gain, attn_qkv, attn_out, mlp_gain, up_weight, down_weight = params
    group_size = frames.shape[0]
    hidden = low(normalize(frames) * attn_gain)
    project = low(low_back(matmul_high(hidden, attn_qkv)))
    queries = project[..., :D].reshape(group_size, P_SIZE, H, HD)
    key_rows = jnp.concatenate([project[..., D:2 * D], message_kv[:, None, :D]], axis=1).reshape(group_size, P_SIZE + 1, H, HD)
    value_rows = jnp.concatenate([project[..., 2 * D:], message_kv[:, None, D:]], axis=1).reshape(group_size, P_SIZE + 1, H, HD)
    scores = low_back(jnp.einsum('gqhd,gkhd->ghqk', queries, key_rows, precision=HIGH) * 0.125)
    probs = low(jax.nn.softmax(scores, axis=-1))
    mixed_heads = low(low_back(jnp.einsum('ghqk,gkhd->gqhd', probs, value_rows, precision=HIGH))).reshape(group_size, P_SIZE, D)
    residual = frames + low_back(matmul_high(mixed_heads, attn_out))
    mlp_input = low(normalize(residual) * mlp_gain)
    up_part = low_back(matmul_high(mlp_input, up_weight))
    activated = low(quick_gelu(up_part))
    return residual + low_back(matmul_high(activated, down_weight))

def layer(frames, weights, video_ids, frame_device):
    msg_weight, msg_gain, msg_qkv, msg_out, attn_gain, attn_qkv, attn_out, mlp_gain, up_weight, down_weight = weights
    frame_count = frames.shape[0]
    message_start = low(low_back(matmul_high(frames[:, 0, :], msg_weight)))
    normed = low(normalize(message_start) * msg_gain)
    project = low(low_back(matmul_high(normed, msg_qkv)))
    queries = project[:, :D].reshape(frame_count, H, HD)
    key_rows = project[:, D:2 * D].reshape(frame_count, H, HD)
    value_rows = project[:, 2 * D:].reshape(frame_count, H, HD)
    scores = low_back(jnp.einsum('ihd,jhd->hij', queries, key_rows, precision=HIGH) * 0.125)
    allowed = (video_ids[:, None] == video_ids[None, :]) & (frame_device[:, None] == frame_device[None, :])
    scores = jnp.where(allowed[None], scores, -1e+30)
    probs = low(jax.nn.softmax(scores, axis=-1))
    mixed_heads = low(low_back(jnp.einsum('hij,jhd->ihd', probs, value_rows, precision=HIGH))).reshape(frame_count, D)
    message = low(low_back(message_start + low_back(matmul_high(mixed_heads, msg_out))))
    token_hidden = low(normalize(message) * attn_gain)
    message_kv = low(low_back(matmul_high(token_hidden, attn_qkv[:, D:])))
    groups = frame_count // FR_DEV
    params = (attn_gain, attn_qkv, attn_out, mlp_gain, up_weight, down_weight)

    def one_group(group_pair):
        return frame_group(params, group_pair[0], group_pair[1])
    result = lax.map(jax.checkpoint(one_group), (frames.reshape(groups, FR_DEV, P_SIZE, D), message_kv.reshape(groups, FR_DEV, 2 * D)))
    return result.reshape(frame_count, P_SIZE, D)

def reference(frames_in, cotangent, video_ids, frame_device, msg_weight, msg_gain, msg_qkv, msg_out, attn_gain, attn_qkv, attn_out, mlp_gain, up_weight, down_weight):
    weights = (msg_weight.astype(jnp.float32), msg_gain.astype(jnp.float32), msg_qkv.astype(jnp.float32), msg_out.astype(jnp.float32), attn_gain.astype(jnp.float32), attn_qkv.astype(jnp.float32), attn_out.astype(jnp.float32), mlp_gain.astype(jnp.float32), up_weight.astype(jnp.float32), down_weight.astype(jnp.float32))

    def forward(frames, weight_set):
        return layer(frames, weight_set, video_ids, frame_device)
    output, pullback = jax.vjp(forward, frames_in.astype(jnp.float32), weights)
    grad_frames, grads = pullback(cotangent.astype(jnp.float32))
    return (output.astype(jnp.bfloat16), grad_frames.astype(jnp.bfloat16), grads[0], grads[1], grads[2], grads[3], grads[4], grads[5], grads[6], grads[7], grads[8], grads[9])
```

```python
import functools

import jax
import jax.numpy as jnp
from jax import lax
from jax.experimental import pallas as pl
from jax.experimental.pallas import tpu as pltpu
from jax.sharding import PartitionSpec as P

H = 12
HD = 64
PAIR = 2 * HD
GROUP = 2
EPS = 1e-05
NEG = -1e30
FLOAT = jnp.float32
BFLOAT = jnp.bfloat16
VMEM_BYTES = 60 * 1024 * 1024


def params(**kw):
    return pltpu.CompilerParams(vmem_limit_bytes=VMEM_BYTES, **kw)


def padded_len(frame_len):
    return -(-(frame_len + 1) // 8) * 8


def whole(shape):
    return pl.BlockSpec(shape, lambda *_: (0,) * len(shape), pipeline_mode=pl.Buffered(1))


def rows_of(height, width):
    return pl.BlockSpec((height, width), lambda i: (i, 0))


def frames_of(pad, width):
    return pl.BlockSpec((GROUP, pad, width), lambda i: (i, 0, 0))


def normalize(values):
    center = values - jnp.mean(values, axis=-1, keepdims=True)
    spread = jnp.mean(center * center, axis=-1, keepdims=True)
    scale_inv = lax.rsqrt(spread + EPS)
    return (center * scale_inv, scale_inv)


def norm_back(grad_normed, normed, scale_inv):
    return scale_inv * (
        grad_normed
        - jnp.mean(grad_normed, axis=-1, keepdims=True)
        - normed * jnp.mean(grad_normed * normed, axis=-1, keepdims=True)
    )


def dot(a, b):
    return jnp.dot(a, b, preferred_element_type=FLOAT)


def dot_nt(a, b):
    return lax.dot_general(a, b, (((1,), (1,)), ((), ())), preferred_element_type=FLOAT)


def dot_tn(a, b):
    return lax.dot_general(a, b, (((0,), (0,)), ((), ())), preferred_element_type=FLOAT)


def load_rows(ref, frame_len):
    values = ref[...].astype(FLOAT)
    count, pad, width = values.shape
    row = lax.broadcasted_iota(jnp.int32, values.shape, 1)
    return jnp.where(row < frame_len, values, 0.0).reshape(count * pad, width)


def project_kernel(frame_len, x_ref, gain_ref, w_ref, hidden_ref, proj_ref):
    normed, _ = normalize(load_rows(x_ref, frame_len))
    hidden = (normed * gain_ref[...]).astype(BFLOAT)
    hidden_ref[...] = hidden
    width = hidden.shape[1]
    for part in range(3):
        cols = slice(part * width, (part + 1) * width)
        proj_ref[:, cols] = dot(hidden, w_ref[:, cols]).astype(BFLOAT)


def project(frames_in, gain, qkv):
    count, frame_len, width = frames_in.shape
    pad = padded_len(frame_len)
    block = GROUP * pad
    return pl.pallas_call(
        functools.partial(project_kernel, frame_len),
        grid=(count // GROUP,),
        in_specs=[frames_of(pad, width), whole((1, width)), whole(qkv.shape)],
        out_specs=[rows_of(block, width), rows_of(block, 3 * width)],
        out_shape=[
            jax.ShapeDtypeStruct((count * pad, width), BFLOAT),
            jax.ShapeDtypeStruct((count * pad, 3 * width), BFLOAT),
        ],
        compiler_params=params(),
        name="project",
    )(frames_in, gain, qkv)


def token_in(rows, token, frame_len):
    row = lax.broadcasted_iota(jnp.int32, rows.shape, 0)
    return jnp.where(row == frame_len, token, rows)


def attend_kernel(frame_len, x_ref, proj_ref, token_ref, out_w_ref, prob_ref, mixed_ref, res_ref):
    width = x_ref.shape[2]
    pad = x_ref.shape[1]
    pairs = width // PAIR

    def one_pair(j, carry):
        for f in range(GROUP):
            rows = pl.ds(f * pad, pad)
            at = [pl.ds(pl.multiple_of(part * width + j * PAIR, PAIR), PAIR) for part in range(3)]
            query = proj_ref[rows, at[0]]
            key = token_in(proj_ref[rows, at[1]], token_ref[f, :, at[0]], frame_len)
            value = token_in(proj_ref[rows, at[2]], token_ref[f, :, at[1]], frame_len)
            lane = lax.broadcasted_iota(jnp.int32, query.shape, 1)
            value_t = value.astype(FLOAT).T.astype(BFLOAT)
            outs = []
            for h in range(2):
                query_h = jnp.where((lane >= HD) == (h == 1), query, jnp.zeros_like(query))
                scores = dot_nt(key, query_h) * 0.125
                row = lax.broadcasted_iota(jnp.int32, scores.shape, 0)
                scores = jnp.where(row <= frame_len, scores, NEG)
                expo = jnp.exp(scores - jnp.max(scores, axis=0, keepdims=True))
                prob = (expo * (1.0 / jnp.sum(expo, axis=0, keepdims=True))).astype(BFLOAT)
                prob_ref[f, 2 * j + h] = prob
                outs.append(dot(value_t[h * HD : (h + 1) * HD], prob))
            mixed_ref[rows, at[0]] = jnp.concatenate(outs, axis=0).T.astype(BFLOAT)
        return carry

    lax.fori_loop(0, pairs, one_pair, 0)
    res_ref[...] = load_rows(x_ref, frame_len) + dot(mixed_ref[...], out_w_ref[...])


def attend(frames_in, proj, token_kv, out_w):
    count, frame_len, width = frames_in.shape
    pad = padded_len(frame_len)
    block = GROUP * pad
    heads = width // HD
    return pl.pallas_call(
        functools.partial(attend_kernel, frame_len),
        grid=(count // GROUP,),
        in_specs=[
            frames_of(pad, width),
            rows_of(block, 3 * width),
            frames_of(1, 2 * width),
            whole(out_w.shape),
        ],
        out_specs=[
            pl.BlockSpec((GROUP, heads, pad, pad), lambda i: (i, 0, 0, 0)),
            rows_of(block, width),
            rows_of(block, width),
        ],
        out_shape=[
            jax.ShapeDtypeStruct((count, heads, pad, pad), BFLOAT),
            jax.ShapeDtypeStruct((count * pad, width), BFLOAT),
            jax.ShapeDtypeStruct((count * pad, width), FLOAT),
        ],
        compiler_params=params(),
        name="attend",
    )(frames_in, proj, token_kv, out_w)


def mlp_kernel(
    frame_len,
    parts,
    res_ref,
    cot_ref,
    gain_ref,
    up_ref,
    down_ref,
    out_w_ref,
    output_ref,
    cot_rows_ref,
    second_ref,
    act_ref,
    grad_up_ref,
    branch_ref,
    grad_mixed_ref,
    gain_grad_ref,
):
    residual = res_ref[...]
    width = residual.shape[1]
    normed, scale_inv = normalize(residual)
    gain = gain_ref[...]
    second = (normed * gain).astype(BFLOAT)
    second_ref[...] = second
    cot = load_rows(cot_ref, frame_len)
    cot_bf = cot.astype(BFLOAT)
    cot_rows_ref[...] = cot_bf
    out = residual
    grad_second = jnp.zeros_like(residual)
    size = up_ref.shape[1] // parts
    for part in range(parts):
        cols = slice(part * size, (part + 1) * size)
        up_part = dot(second, up_ref[:, cols])
        sigma = 0.5 * jnp.tanh(0.851 * up_part) + 0.5
        gated = up_part * sigma
        act = gated.astype(BFLOAT)
        act_ref[:, cols] = act
        out = out + dot(act, down_ref[cols, :])
        grad_act = dot_nt(cot_bf, down_ref[cols, :])
        grad_up = (grad_act * (sigma + 1.702 * gated * (1.0 - sigma))).astype(BFLOAT)
        grad_up_ref[:, cols] = grad_up
        grad_second = grad_second + dot_nt(grad_up, up_ref[:, cols])
    output_ref[...] = out.astype(BFLOAT).reshape(output_ref.shape)
    gain_grad = jnp.sum(grad_second * normed, axis=0, keepdims=True)
    step = pl.program_id(0)
    gain_grad_ref[...] = jnp.where(step == 0, 0.0, gain_grad_ref[...]) + gain_grad
    branch = (cot + norm_back(grad_second * gain, normed, scale_inv)).astype(BFLOAT)
    branch_ref[...] = branch
    grad_mixed_ref[...] = dot_nt(branch, out_w_ref[...]).astype(BFLOAT)


def mlp(residual, cotangent, gain, up, down, out_w):
    count, frame_len, width = cotangent.shape
    pad = padded_len(frame_len)
    block = GROUP * pad
    rows = count * pad
    hidden = up.shape[1]
    shape = jax.ShapeDtypeStruct
    return pl.pallas_call(
        functools.partial(mlp_kernel, frame_len, 4),
        grid=(count // GROUP,),
        in_specs=[
            rows_of(block, width),
            frames_of(pad, width),
            whole((1, width)),
            whole(up.shape),
            whole(down.shape),
            whole(out_w.shape),
        ],
        out_specs=[
            frames_of(pad, width),
            rows_of(block, width),
            rows_of(block, width),
            rows_of(block, hidden),
            rows_of(block, hidden),
            rows_of(block, width),
            rows_of(block, width),
            pl.BlockSpec((1, width), lambda i: (0, 0)),
        ],
        out_shape=[
            shape((count, frame_len, width), BFLOAT),
            shape((rows, width), BFLOAT),
            shape((rows, width), BFLOAT),
            shape((rows, hidden), BFLOAT),
            shape((rows, hidden), BFLOAT),
            shape((rows, width), BFLOAT),
            shape((rows, width), BFLOAT),
            shape((1, width), FLOAT),
        ],
        compiler_params=params(),
        name="mlp",
    )(residual, cotangent, gain, up, down, out_w)


def weight_grad_kernel(left_ref, right_ref, out_ref):
    out_ref[...] = dot_tn(left_ref[...], right_ref[...]).astype(BFLOAT).reshape(out_ref.shape)


def weight_grad(left, right, tile, out_shape, out_block, out_index, name):
    rows = left.shape[0]
    return pl.pallas_call(
        weight_grad_kernel,
        grid=(right.shape[1] // tile,),
        in_specs=[whole(left.shape), pl.BlockSpec((rows, tile), lambda i: (0, i))],
        out_specs=pl.BlockSpec(out_block, out_index),
        out_shape=jax.ShapeDtypeStruct(out_shape, BFLOAT),
        compiler_params=params(),
        name=name,
    )(left, right)


def split_grad_kernel(left_ref, right_ref, out_ref, all_ref):
    step = pl.program_id(0)
    tile = right_ref.shape[1]
    all_ref[:, pl.ds(pl.multiple_of(step * tile, tile), tile)] = dot_tn(
        left_ref[...], right_ref[...]
    ).astype(BFLOAT)
    size = out_ref.shape[2]

    @pl.when(step == pl.num_programs(0) - 1)
    def _():
        for part in range(out_ref.shape[0]):
            out_ref[part] = all_ref[:, part * size : (part + 1) * size]


def split_grad(left, right, tile, parts, name):
    rows, width = left.shape
    columns = right.shape[1]
    shape = (parts, width, columns // parts)
    return pl.pallas_call(
        split_grad_kernel,
        grid=(columns // tile,),
        in_specs=[whole(left.shape), pl.BlockSpec((rows, tile), lambda i: (0, i))],
        out_specs=pl.BlockSpec(shape, lambda i: (0, 0, 0)),
        out_shape=jax.ShapeDtypeStruct(shape, BFLOAT),
        scratch_shapes=[pltpu.VMEM((width, columns), BFLOAT)],
        compiler_params=params(),
        name=name,
    )(left, right)


def attend_back_kernel(
    frame_len,
    proj_ref,
    token_ref,
    prob_ref,
    grad_mixed_ref,
    hidden_ref,
    token_hidden_ref,
    grad_proj_ref,
    full_hidden_ref,
    token_grad_ref,
):
    pad = prob_ref.shape[2]
    width = grad_mixed_ref.shape[1]
    for f in range(GROUP):
        rows = pl.ds(f * pad, pad)
        full_hidden_ref[rows, :] = token_in(hidden_ref[rows, :], token_hidden_ref[f], frame_len)

    def one_pair(j, carry):
        for f in range(GROUP):
            rows = pl.ds(f * pad, pad)
            at = [pl.ds(pl.multiple_of(part * width + j * PAIR, PAIR), PAIR) for part in range(3)]
            query = proj_ref[rows, at[0]]
            key = token_in(proj_ref[rows, at[1]], token_ref[f, :, at[0]], frame_len)
            value = token_in(proj_ref[rows, at[2]], token_ref[f, :, at[1]], frame_len)
            grad = grad_mixed_ref[rows, at[0]]
            lane = lax.broadcasted_iota(jnp.int32, query.shape, 1)
            key_t = key.astype(FLOAT).T.astype(BFLOAT)
            grad_query, grad_key, grad_value = [], [], []
            for h in range(2):
                prob = prob_ref[f, 2 * j + h]
                grad_h = jnp.where((lane >= HD) == (h == 1), grad, jnp.zeros_like(grad))
                grad_prob = dot_nt(value, grad_h)
                prob_f = prob.astype(FLOAT)
                part = prob_f * grad_prob
                scores = part - prob_f * jnp.sum(part, axis=0, keepdims=True)
                scores = scores.astype(BFLOAT)
                grad_value.append(dot(prob, grad))
                grad_key.append(dot(scores, query))
                grad_query.append(dot(key_t[h * HD : (h + 1) * HD], scores))
            grad_query = jnp.concatenate(grad_query, axis=0).T * 0.125
            grad_proj_ref[rows, at[0]] = grad_query.astype(BFLOAT)
            grad_key = jnp.where(lane >= HD, grad_key[1], grad_key[0]) * 0.125
            grad_proj_ref[rows, at[1]] = grad_key.astype(BFLOAT)
            grad_value = jnp.where(lane >= HD, grad_value[1], grad_value[0])
            grad_proj_ref[rows, at[2]] = grad_value.astype(BFLOAT)
        return carry

    lax.fori_loop(0, width // PAIR, one_pair, 0)
    for f in range(GROUP):
        row = f * pad + frame_len
        token_grad_ref[f] = grad_proj_ref[row : row + 1, width:]


def attend_back(proj, token_kv, prob, grad_mixed, hidden, token_hidden, frame_len):
    count, heads, pad, _ = prob.shape
    width = heads * HD
    block = GROUP * pad
    return pl.pallas_call(
        functools.partial(attend_back_kernel, frame_len),
        grid=(count // GROUP,),
        in_specs=[
            rows_of(block, 3 * width),
            frames_of(1, 2 * width),
            pl.BlockSpec((GROUP, heads, pad, pad), lambda i: (i, 0, 0, 0)),
            rows_of(block, width),
            rows_of(block, width),
            frames_of(1, width),
        ],
        out_specs=[rows_of(block, 3 * width), rows_of(block, width), frames_of(1, 2 * width)],
        out_shape=[
            jax.ShapeDtypeStruct((count * pad, 3 * width), BFLOAT),
            jax.ShapeDtypeStruct((count * pad, width), BFLOAT),
            jax.ShapeDtypeStruct((count, 1, 2 * width), BFLOAT),
        ],
        compiler_params=params(),
        name="attend_back",
    )(proj, token_kv, prob, grad_mixed, hidden, token_hidden)


def first_back_kernel(
    frame_len, x_ref, grad_proj_ref, branch_ref, class_ref, gain_ref, w_ref, grad_in_ref, gain_grad_ref
):
    normed, scale_inv = normalize(load_rows(x_ref, frame_len))
    grad = dot_nt(grad_proj_ref[...], w_ref[...])
    shape = (GROUP, grad.shape[0] // GROUP, grad.shape[1])
    step = pl.program_id(0)
    gain_grad = jnp.sum(grad * normed, axis=0, keepdims=True)
    gain_grad_ref[...] = jnp.where(step == 0, 0.0, gain_grad_ref[...]) + gain_grad
    total = branch_ref[...].astype(FLOAT) + norm_back(grad * gain_ref[...], normed, scale_inv)
    total = total.reshape(shape)
    row = lax.broadcasted_iota(jnp.int32, shape, 1)
    total = jnp.where(row == 0, total + class_ref[...], total)
    grad_in_ref[...] = total.astype(BFLOAT)


def first_back(frames_in, grad_proj, branch, class_grad, gain, qkv):
    count, frame_len, width = frames_in.shape
    pad = padded_len(frame_len)
    block = GROUP * pad
    return pl.pallas_call(
        functools.partial(first_back_kernel, frame_len),
        grid=(count // GROUP,),
        in_specs=[
            frames_of(pad, width),
            rows_of(block, 3 * width),
            rows_of(block, width),
            frames_of(1, width),
            whole((1, width)),
            whole(qkv.shape),
        ],
        out_specs=[frames_of(pad, width), pl.BlockSpec((1, width), lambda i: (0, 0))],
        out_shape=[
            jax.ShapeDtypeStruct((count, frame_len, width), BFLOAT),
            jax.ShapeDtypeStruct((1, width), FLOAT),
        ],
        compiler_params=params(),
        name="first_back",
    )(frames_in, grad_proj, branch, class_grad, gain, qkv)


def message_kernel(
    own,
    class_ref,
    id_row_ref,
    id_col_ref,
    weight_ref,
    gain_ref,
    qkv_ref,
    out_w_ref,
    attn_gain_ref,
    key_w_ref,
    value_w_ref,
    start_ref,
    hidden_ref,
    proj_ref,
    prob_ref,
    mixed_ref,
    message_ref,
    token_hidden_ref,
    token_kv_ref,
):
    width = weight_ref.shape[0]
    start = dot(class_ref[...], weight_ref[...]).astype(BFLOAT)
    start_ref[...] = start
    normed, _ = normalize(start.astype(FLOAT))
    hidden = (normed * gain_ref[...]).astype(BFLOAT)
    hidden_ref[...] = hidden
    proj_ref[...] = dot(hidden, qkv_ref[...]).astype(BFLOAT)
    visible = id_col_ref[...] == id_row_ref[...]

    def one_pair(j, carry):
        at = [pl.ds(pl.multiple_of(part * width + j * PAIR, PAIR), PAIR) for part in range(3)]
        query, key, value = (proj_ref[:, at[part]] for part in range(3))
        lane = lax.broadcasted_iota(jnp.int32, query.shape, 1)
        value_t = value.astype(FLOAT).T.astype(BFLOAT)
        outs = []
        for h in range(2):
            query_h = jnp.where((lane >= HD) == (h == 1), query, jnp.zeros_like(query))
            scores = jnp.where(visible, dot_nt(key, query_h) * 0.125, NEG)
            expo = jnp.exp(scores - jnp.max(scores, axis=0, keepdims=True))
            prob = (expo * (1.0 / jnp.sum(expo, axis=0, keepdims=True))).astype(BFLOAT)
            prob_ref[2 * j + h] = prob
            outs.append(dot(value_t[h * HD : (h + 1) * HD], prob))
        mixed_ref[:, at[0]] = jnp.concatenate(outs, axis=0).T.astype(BFLOAT)
        return carry

    lax.fori_loop(0, width // PAIR, one_pair, 0)
    message = start[:own].astype(FLOAT) + dot(mixed_ref[:own, :], out_w_ref[...])
    message = message.astype(BFLOAT)
    message_ref[...] = message
    normed, _ = normalize(message.astype(FLOAT))
    token_hidden = (normed * attn_gain_ref[...]).astype(BFLOAT)
    token_hidden_ref[...] = token_hidden
    token_kv_ref[:, :width] = dot(token_hidden, key_w_ref[...]).astype(BFLOAT)
    token_kv_ref[:, width:] = dot(token_hidden, value_w_ref[...]).astype(BFLOAT)


def message_forward(class_all, ids, own, weight, gain, qkv, out_w, attn_gain, attn_qkv):
    slots, width = class_all.shape
    heads = width // HD
    shape = jax.ShapeDtypeStruct
    part = lambda index: pl.BlockSpec((width, width), lambda i, index=index: (0, index))
    return pl.pallas_call(
        functools.partial(message_kernel, own),
        grid=(1,),
        in_specs=[
            whole((slots, width)),
            whole((1, slots)),
            whole((slots, 1)),
            whole(weight.shape),
            whole((1, width)),
            whole(qkv.shape),
            whole(out_w.shape),
            whole((1, width)),
            part(1),
            part(2),
        ],
        out_specs=[
            whole((slots, width)),
            whole((slots, width)),
            whole((slots, 3 * width)),
            whole((heads, slots, slots)),
            whole((slots, width)),
            whole((own, width)),
            whole((own, width)),
            whole((own, 2 * width)),
        ],
        out_shape=[
            shape((slots, width), BFLOAT),
            shape((slots, width), BFLOAT),
            shape((slots, 3 * width), BFLOAT),
            shape((heads, slots, slots), BFLOAT),
            shape((slots, width), BFLOAT),
            shape((own, width), BFLOAT),
            shape((own, width), BFLOAT),
            shape((own, 2 * width), BFLOAT),
        ],
        compiler_params=params(),
        name="message_forward",
    )(
        class_all,
        ids.reshape(1, slots),
        ids.reshape(slots, 1),
        weight,
        gain,
        qkv,
        out_w,
        attn_gain,
        attn_qkv,
        attn_qkv,
    )


def token_back_kernel(token_grad_ref, message_ref, gain_ref, key_w_ref, value_w_ref, grad_ref, gain_grad_ref):
    width = message_ref.shape[1]
    normed, scale_inv = normalize(message_ref[...].astype(FLOAT))
    grad = dot_nt(token_grad_ref[:, :width], key_w_ref[...])
    grad = grad + dot_nt(token_grad_ref[:, width:], value_w_ref[...])
    gain_grad_ref[...] = jnp.sum(grad * normed, axis=0, keepdims=True)
    grad_ref[...] = norm_back(grad * gain_ref[...], normed, scale_inv).astype(BFLOAT)


def token_back(token_grad, message, gain, attn_qkv):
    own, width = message.shape
    part = lambda index: pl.BlockSpec((width, width), lambda i, index=index: (0, index))
    return pl.pallas_call(
        token_back_kernel,
        grid=(1,),
        in_specs=[whole(token_grad.shape), whole(message.shape), whole((1, width)), part(1), part(2)],
        out_specs=[whole((own, width)), whole((1, width))],
        out_shape=[
            jax.ShapeDtypeStruct((own, width), BFLOAT),
            jax.ShapeDtypeStruct((1, width), FLOAT),
        ],
        compiler_params=params(),
        name="token_back",
    )(token_grad, message, gain, attn_qkv, attn_qkv)


def message_back_kernel(
    own,
    parts,
    block_ref,
    grad_ref,
    class_ref,
    start_ref,
    hidden_ref,
    proj_ref,
    prob_ref,
    mixed_ref,
    weight_ref,
    gain_ref,
    qkv_ref,
    out_w_ref,
    class_grad_ref,
    gain_grad_ref,
    sums_ref,
    grad_mixed_ref,
    grad_proj_ref,
):
    width = weight_ref.shape[0]
    grad = grad_ref[...]
    j = pl.program_id(0)

    @pl.when(j == 0)
    def _():
        grad_mixed_ref[...] = dot_nt(grad, out_w_ref[...]).astype(BFLOAT)

    def finish():
        grad_proj = grad_proj_ref[...]
        grad_hidden = dot_nt(grad_proj, qkv_ref[...])
        normed, scale_inv = normalize(start_ref[...].astype(FLOAT))
        gain_grad_ref[...] = jnp.sum(grad_hidden[:own] * normed[:own], axis=0, keepdims=True)
        back = norm_back(grad_hidden * gain_ref[...], normed, scale_inv)
        start_grad = (grad.astype(FLOAT) + back).astype(BFLOAT)
        class_grad_ref[...] = dot_nt(start_grad[:own], weight_ref[...])
        size = sums_ref.shape[1]
        row = lax.broadcasted_iota(jnp.int32, (size, width), 0)
        column = lax.broadcasted_iota(jnp.int32, (size, width), 1)
        pick = (column == row + block_ref[0] * size).astype(BFLOAT)
        offset = 0
        for left, right in (
            (hidden_ref[...], grad_proj),
            (class_ref[...], start_grad),
            (mixed_ref[...], grad),
        ):
            total = dot(dot_nt(pick, left).astype(BFLOAT), right).astype(BFLOAT)
            columns = total.shape[1] // parts
            for part in range(parts):
                sums_ref[part, :, offset : offset + columns] = total[
                    :, part * columns : (part + 1) * columns
                ]
            offset += columns

    at = [pl.ds(pl.multiple_of(part * width + j * PAIR, PAIR), PAIR) for part in range(3)]
    query, key, value = (proj_ref[:, at[part]] for part in range(3))
    grad_m = grad_mixed_ref[:, at[0]]
    lane = lax.broadcasted_iota(jnp.int32, query.shape, 1)
    key_t = key.astype(FLOAT).T.astype(BFLOAT)
    grad_query, grad_key, grad_value = [], [], []
    for h in range(2):
        prob = prob_ref[h]
        grad_h = jnp.where((lane >= HD) == (h == 1), grad_m, jnp.zeros_like(grad_m))
        grad_prob = dot_nt(value, grad_h)
        prob_f = prob.astype(FLOAT)
        part = prob_f * grad_prob
        scores = (part - prob_f * jnp.sum(part, axis=0, keepdims=True)).astype(BFLOAT)
        grad_value.append(dot(prob, grad_m))
        grad_key.append(dot(scores, query))
        grad_query.append(dot(key_t[h * HD : (h + 1) * HD], scores))
    grad_query = jnp.concatenate(grad_query, axis=0).T * 0.125
    grad_proj_ref[:, at[0]] = grad_query.astype(BFLOAT)
    grad_key = jnp.where(lane >= HD, grad_key[1], grad_key[0]) * 0.125
    grad_proj_ref[:, at[1]] = grad_key.astype(BFLOAT)
    grad_value = jnp.where(lane >= HD, grad_value[1], grad_value[0])
    grad_proj_ref[:, at[2]] = grad_value.astype(BFLOAT)

    @pl.when(j == pl.num_programs(0) - 1)
    def _():
        finish()


def message_back(block, parts, size, own, grad_all, class_all, saved, weight, gain, qkv, out_w):
    slots, width = class_all.shape
    start, hidden, proj, prob, mixed = saved
    shape = jax.ShapeDtypeStruct
    sums = (parts, size, 5 * width // parts)
    args = (grad_all, class_all, start, hidden, proj, prob, mixed, weight, gain, qkv, out_w)
    return pl.pallas_call(
        functools.partial(message_back_kernel, own, parts),
        grid=(width // PAIR,),
        in_specs=[pl.BlockSpec(memory_space=pltpu.SMEM)]
        + [pl.BlockSpec((2, slots, slots), lambda j: (j, 0, 0)) if a is prob else whole(a.shape) for a in args],
        out_specs=[whole((own, width)), whole((1, width)), whole(sums)],
        out_shape=[shape((own, width), FLOAT), shape((1, width), FLOAT), shape(sums, BFLOAT)],
        scratch_shapes=[pltpu.VMEM((slots, width), BFLOAT), pltpu.VMEM((slots, 3 * width), BFLOAT)],
        compiler_params=params(),
        name="message_back",
    )(block, *args)


def swap(values, axis, distance):
    return lax.ppermute(values, axis, [(i, i ^ distance) for i in range(lax.axis_size(axis))])


def gather_frames(values):
    owners = lax.axis_size("frames")
    if owners > 8:
        order = lax.axis_index("frames") ^ jnp.arange(owners)
        stacked = jnp.take(lax.all_gather(values, "frames"), order, axis=0)
    else:
        stacked = jnp.stack([values] + [swap(values, "frames", d) for d in range(1, owners)])
    return stacked.reshape(owners * values.shape[0], *values.shape[1:])


def pick(values, index, axis=0):
    return lax.dynamic_index_in_dim(values, index, axis, keepdims=False)


def add(*terms):
    total = terms[0].astype(FLOAT)
    for term in terms[1:]:
        total = total + term.astype(FLOAT)
    return total


def halve(values, axis, distance):
    bit = (lax.axis_index(axis) // distance) % 2
    got = swap(pick(values, 1 - bit, 1), axis, distance)
    return add(got, pick(values, bit, 1)).astype(BFLOAT)


def sum_over(values, axis, limit):
    size, distance = lax.axis_size(axis), 1
    block = values.shape[1:]
    while size > limit:
        values = halve(values.reshape(size // 2, 2, *block), axis, distance)
        size, distance = size // 2, 2 * distance
    index = lax.axis_index(axis) // distance
    terms = [pick(values, index)]
    for d in range(1, size):
        terms.append(swap(pick(values, index ^ d), axis, d * distance))
    return add(*terms)


def per_device(
    frames_in,
    cotangent,
    video_ids,
    frame_device,
    msg_weight,
    msg_gain,
    msg_qkv,
    msg_out,
    attn_gain,
    attn_qkv,
    attn_out,
    mlp_gain,
    up_weight,
    down_weight,
):
    count, frame_len, width = frames_in.shape
    owners, parts = lax.axis_size("frames"), lax.axis_size("rows")
    hidden_width = up_weight.shape[1]
    own = -(-count // 16) * 16
    msg_gain, attn_gain, mlp_gain = (g.reshape(1, width) for g in (msg_gain, attn_gain, mlp_gain))
    block_index = lax.axis_index("frames").astype(jnp.int32).reshape(1)

    extra = ((0, own - count), (0, 0))
    class_all = gather_frames(jnp.pad(frames_in[:, 0, :], extra))
    ids = video_ids * owners + frame_device
    ids = gather_frames(jnp.pad(ids, (0, own - count), constant_values=-1))

    hidden, proj = project(frames_in, attn_gain, attn_qkv)
    *saved, message, token_hidden, token_kv = message_forward(
        class_all, ids, own, msg_weight, msg_gain, msg_qkv, msg_out, attn_gain, attn_qkv
    )
    token_kv = token_kv[:count, None]
    token_hidden = token_hidden[:count, None]
    prob, mixed, residual = attend(frames_in, proj, token_kv, attn_out)
    output, cot, second, act, grad_up, branch, grad_mixed, mlp_gain_grad = mlp(
        residual, cotangent, mlp_gain, up_weight, down_weight, attn_out
    )
    tile = 384
    tiles = hidden_width // tile
    half = hidden_width // parts // tile
    down_sum = weight_grad(
        cot,
        act,
        tile,
        (parts, tiles, width // parts, tile),
        (parts, 1, width // parts, tile),
        lambda i: (0, i, 0, 0),
        "grad_down",
    )
    up_sum = weight_grad(
        second,
        grad_up,
        tile,
        (parts, width, hidden_width // parts),
        (1, width, tile),
        lambda i: (i // half, 0, i % half),
        "grad_up",
    )
    out_sum = split_grad(mixed, branch, 256, parts, "grad_attn_out")
    grad_proj, hidden, token_grad = attend_back(
        proj, token_kv, prob, grad_mixed, hidden, token_hidden, frame_len
    )
    message_grad, token_gain_grad = token_back(
        jnp.pad(token_grad.reshape(count, 2 * width), extra), message, attn_gain, attn_qkv
    )
    grad_all = gather_frames(message_grad)
    qkv_sum = split_grad(hidden, grad_proj, 768, parts, "grad_attn_qkv")
    class_grad, msg_gain_grad, msg_sums = message_back(
        block_index,
        parts,
        width // owners,
        own,
        grad_all,
        class_all,
        saved,
        msg_weight,
        msg_gain,
        msg_qkv,
        msg_out,
    )
    grad_in, attn_gain_grad = first_back(
        frames_in, grad_proj, branch, class_grad[:count, None], attn_gain, attn_qkv
    )

    def summed(values):
        values = sum_over(values, "rows", 2)
        values = values.astype(BFLOAT).reshape(owners, -1, *values.shape[1:])
        return sum_over(values, "frames", 4)

    down_sum = sum_over(down_sum, "rows", 2).astype(BFLOAT)
    if tiles != owners:
        down_sum = jnp.swapaxes(down_sum, 1, 2).reshape(width // parts, owners, -1)
        down_sum = jnp.swapaxes(down_sum, 0, 1)
    grad_down = sum_over(down_sum, "frames", 4).T
    grad_up = summed(up_sum)
    grad_out = summed(out_sum)
    grad_qkv = summed(qkv_sum)
    msg_sums = sum_over(msg_sums, "rows", 2)
    cuts = (3 * width // parts, 4 * width // parts)
    grad_msg_qkv, grad_msg_weight, grad_msg_out = jnp.split(msg_sums, cuts, axis=1)
    gains = jnp.concatenate([msg_gain_grad, attn_gain_grad + token_gain_grad, mlp_gain_grad])
    gains = add(gains, *(swap(gains, "rows", d) for d in range(1, parts)))
    gains = jnp.swapaxes(gains.reshape(3, owners, -1), 0, 1)
    gains = sum_over(gains, "frames", 8)
    return (
        output,
        grad_in,
        grad_msg_weight,
        gains[0],
        grad_msg_qkv,
        grad_msg_out,
        gains[1],
        grad_qkv,
        grad_out,
        gains[2],
        grad_up,
        grad_down,
    )


def solution(mesh):
    split = P(("frames", "rows"))
    matrix = P("frames", "rows")
    gain = P("frames")
    return jax.shard_map(
        per_device,
        mesh=mesh,
        in_specs=(split, split, split, split) + (P(),) * 10,
        out_specs=(
            split,
            split,
            matrix,
            gain,
            matrix,
            matrix,
            gain,
            matrix,
            matrix,
            gain,
            matrix,
            matrix,
        ),
        check_vma=False,
    )
```

```python
import functools

import jax
import jax.numpy as jnp
from jax import lax
from jax.experimental import pallas as pl
from jax.experimental.pallas import tpu as pltpu
from jax.sharding import PartitionSpec as P

H = 12
HD = 64
PAIR = 2 * HD
GROUP = 2
EPS = 1e-05
NEG = -1e30
BASE = 128.0
DIGITS = 3
LANES = 128
FLOAT = jnp.float32
BFLOAT = jnp.bfloat16
VMEM_BYTES = 60 * 1024 * 1024


def params(**kw):
    return pltpu.CompilerParams(vmem_limit_bytes=VMEM_BYTES, **kw)


def cost(flops, moved):
    return pl.CostEstimate(flops=int(flops / 100), transcendentals=0, bytes_accessed=int(moved / 100))


def padded_len(frame_len):
    return -(-(frame_len + 1) // 8) * 8


def whole(shape):
    return pl.BlockSpec(shape, lambda *_: (0,) * len(shape), pipeline_mode=pl.Buffered(1))


def rows_of(height, width, first=0):
    return pl.BlockSpec((height, width), lambda i: (i + first, 0))


def frames_of(pad, width, first=0):
    return pl.BlockSpec((GROUP, pad, width), lambda i: (i + first, 0, 0))


def normalize(values):
    center = values - jnp.mean(values, axis=-1, keepdims=True)
    spread = jnp.mean(center * center, axis=-1, keepdims=True)
    scale_inv = lax.rsqrt(spread + EPS)
    return (center * scale_inv, scale_inv)


def norm_back(grad_normed, normed, scale_inv):
    return scale_inv * (
        grad_normed
        - jnp.mean(grad_normed, axis=-1, keepdims=True)
        - normed * jnp.mean(grad_normed * normed, axis=-1, keepdims=True)
    )


def dot(a, b):
    return jnp.dot(a, b, preferred_element_type=FLOAT)


def dot_nt(a, b):
    return lax.dot_general(a, b, (((1,), (1,)), ((), ())), preferred_element_type=FLOAT)


def dot_tn(a, b):
    return lax.dot_general(a, b, (((0,), (0,)), ((), ())), preferred_element_type=FLOAT)


def load_rows(ref, frame_len):
    values = ref[...].astype(FLOAT)
    count, pad, width = values.shape
    row = lax.broadcasted_iota(jnp.int32, values.shape, 1)
    return jnp.where(row < frame_len, values, 0.0).reshape(count * pad, width)


def project_kernel(frame_len, x_ref, gain_ref, w_ref, proj_ref):
    normed, _ = normalize(load_rows(x_ref, frame_len))
    hidden = (normed * gain_ref[...]).astype(BFLOAT)
    width = hidden.shape[1]
    for part in range(3):
        cols = slice(part * width, (part + 1) * width)
        proj_ref[:, cols] = dot(hidden, w_ref[:, cols]).astype(BFLOAT)


def alias_call(
    kernel, grid, in_specs, args, prior, out_specs, out_shape, name, flops, moved, scratch=()
):
    extra = [] if prior is None else list(prior)

    def body(*refs):
        kernel(*refs[: len(args)], *refs[len(args) + len(extra) :])

    return pl.pallas_call(
        body,
        grid=grid,
        in_specs=in_specs + [pl.BlockSpec(memory_space=pl.ANY)] * len(extra),
        out_specs=out_specs,
        out_shape=out_shape,
        input_output_aliases={len(args) + i: i for i in range(len(extra))},
        scratch_shapes=list(scratch),
        compiler_params=params(),
        cost_estimate=cost(flops, moved),
        name=name,
    )(*args, *extra)


def project(frames_in, gain, qkv, first, steps, prior):
    count, frame_len, width = frames_in.shape
    pad = padded_len(frame_len)
    block = GROUP * pad
    return alias_call(
        functools.partial(project_kernel, frame_len),
        (steps,),
        [frames_of(pad, width, first), whole((width,)), whole(qkv.shape)],
        (frames_in, gain, qkv),
        prior,
        [rows_of(block, 3 * width, first)],
        [jax.ShapeDtypeStruct((count * pad, 3 * width), BFLOAT)],
        "project",
        6 * steps * block * width * width,
        8 * steps * block * width,
    )


def last_rows(rows, change):
    cut = rows.shape[0] - 8
    return jnp.concatenate([rows[:cut], change(rows[cut:], cut)], axis=0)


def token_in(rows, token, frame_len):
    def change(tail, cut):
        row = lax.broadcasted_iota(jnp.int32, tail.shape, 0)
        return jnp.where(row == frame_len - cut, token, tail)

    return last_rows(rows, change)


def one_head(pair, h):
    lane = lax.broadcasted_iota(jnp.int32, pair.shape, 1)
    return jnp.where((lane >= HD) == (h == 1), pair, jnp.zeros_like(pair))


def attend_kernel(
    frame_len, x_ref, proj_ref, token_ref, out_w_ref, expo_ref, mixed_ref, scale_ref, res_ref
):
    width = x_ref.shape[2]
    pad = x_ref.shape[1]
    pairs = width // PAIR

    def hide(tail, cut):
        row = lax.broadcasted_iota(jnp.int32, tail.shape, 0)
        return jnp.where(row <= frame_len - cut, tail, NEG)

    def at(part, j):
        return pl.ds(part * width + j * PAIR, PAIR)

    def weigh(f, j):
        rows = pl.ds(f * pad, pad)
        query = proj_ref[rows, at(0, j)] * 0.125
        key = token_in(proj_ref[rows, at(1, j)], token_ref[f, :, at(0, j)], frame_len)
        for h in range(2):
            scores = last_rows(dot_nt(key, one_head(query, h)), hide)
            expo = jnp.exp(scores - jnp.max(scores, axis=0, keepdims=True)).astype(BFLOAT)
            expo_ref[f, 2 * j + h] = expo

    def mix(f, j):
        rows = pl.ds(f * pad, pad)
        value = token_in(proj_ref[rows, at(2, j)], token_ref[f, :, at(1, j)], frame_len)
        value_t = value.astype(FLOAT).T.astype(BFLOAT)
        outs, scales = [], []
        for h in range(2):
            ones = jnp.ones((8, pad), BFLOAT)
            out = dot(jnp.concatenate([value_t[h * HD : (h + 1) * HD], ones]), expo_ref[f, 2 * j + h])
            scale = 1.0 / out[HD : HD + 1]
            outs.append(out[:HD] * scale)
            scales.append(jnp.broadcast_to(scale, (HD, pad)))
        mixed_ref[rows, at(0, j)] = jnp.concatenate(outs, axis=0).T.astype(BFLOAT)
        scale_ref[rows, at(0, j)] = jnp.concatenate(scales, axis=0).T.astype(BFLOAT)

    units = [(f, j) for j in range(pairs) for f in range(GROUP)]
    for i in range(len(units) + 2):
        if i < len(units):
            weigh(*units[i])
        if i >= 2:
            mix(*units[i - 2])
    res_ref[...] = load_rows(x_ref, frame_len) + dot(mixed_ref[...], out_w_ref[...])


def attend(frames_in, proj, token_kv, out_w):
    count, frame_len, width = frames_in.shape
    pad = padded_len(frame_len)
    block = GROUP * pad
    heads = width // HD
    return pl.pallas_call(
        functools.partial(attend_kernel, frame_len),
        grid=(count // GROUP,),
        in_specs=[
            frames_of(pad, width),
            rows_of(block, 3 * width),
            frames_of(1, 2 * width),
            whole(out_w.shape),
        ],
        out_specs=[
            pl.BlockSpec((GROUP, heads, pad, pad), lambda i: (i, 0, 0, 0)),
            rows_of(block, width),
            rows_of(block, width),
            rows_of(block, width),
        ],
        out_shape=[
            jax.ShapeDtypeStruct((count, heads, pad, pad), BFLOAT),
            jax.ShapeDtypeStruct((count * pad, width), BFLOAT),
            jax.ShapeDtypeStruct((count * pad, width), BFLOAT),
            jax.ShapeDtypeStruct((count * pad, width), FLOAT),
        ],
        compiler_params=params(),
        cost_estimate=cost(25e9, 50e6),
        name="attend",
    )(frames_in, proj, token_kv, out_w)


def mlp_kernel(
    frame_len,
    parts,
    res_ref,
    cot_ref,
    gain_ref,
    up_ref,
    down_ref,
    out_w_ref,
    mixed_ref,
    scale_ref,
    cot_rows_ref,
    second_ref,
    act_ref,
    grad_up_ref,
    branch_ref,
    grad_mixed_ref,
    delta_ref,
    gain_grad_ref,
):
    residual = res_ref[...]
    width = residual.shape[1]
    normed, scale_inv = normalize(residual)
    gain = gain_ref[...]
    second = (normed * gain).astype(BFLOAT)
    second_ref[...] = second
    cot = load_rows(cot_ref, frame_len)
    cot_bf = cot.astype(BFLOAT)
    cot_rows_ref[...] = cot_bf
    grad_second = jnp.zeros_like(residual)
    size = up_ref.shape[1] // parts
    for part in range(parts):
        cols = slice(part * size, (part + 1) * size)
        up_part = dot(second, up_ref[:, cols])
        sigma = 0.5 * jnp.tanh(0.851 * up_part) + 0.5
        gated = up_part * sigma
        act = gated.astype(BFLOAT)
        act_ref[:, cols] = act
        grad_act = dot_nt(cot_bf, down_ref[cols, :])
        grad_up = (grad_act * (sigma + 1.702 * gated * (1.0 - sigma))).astype(BFLOAT)
        grad_up_ref[:, cols] = grad_up
        grad_second = grad_second + dot_nt(grad_up, up_ref[:, cols])
    gain_grad = jnp.sum(grad_second * normed, axis=0, keepdims=True)
    step = pl.program_id(0)
    gain_grad_ref[...] = jnp.where(step == 0, 0.0, gain_grad_ref[...]) + gain_grad
    branch = (cot + norm_back(grad_second * gain, normed, scale_inv)).astype(BFLOAT)
    branch_ref[...] = branch
    grad_mixed = dot_nt(branch, out_w_ref[...]) * scale_ref[...].astype(FLOAT)
    grad_mixed = grad_mixed.astype(BFLOAT)
    grad_mixed_ref[...] = grad_mixed
    heads = delta_ref.shape[1]
    head = lax.broadcasted_iota(jnp.int32, (heads, width), 0)
    lane = lax.broadcasted_iota(jnp.int32, (heads, width), 1)
    of_head = (lane // HD == head).astype(BFLOAT)
    product = grad_mixed * mixed_ref[...]
    pad = delta_ref.shape[2]
    for f in range(GROUP):
        delta_ref[f] = dot_nt(of_head, product[f * pad : (f + 1) * pad])


def mlp(residual, cotangent, gain, up, down, out_w, mixed, scale):
    count, frame_len, width = cotangent.shape
    pad = padded_len(frame_len)
    block = GROUP * pad
    rows = count * pad
    heads = width // HD
    hidden = up.shape[1]
    shape = jax.ShapeDtypeStruct
    return pl.pallas_call(
        functools.partial(mlp_kernel, frame_len, 4),
        grid=(count // GROUP,),
        in_specs=[
            rows_of(block, width),
            frames_of(pad, width),
            whole((width,)),
            whole(up.shape),
            whole(down.shape),
            whole(out_w.shape),
            rows_of(block, width),
            rows_of(block, width),
        ],
        out_specs=[
            rows_of(block, width),
            rows_of(block, width),
            rows_of(block, hidden),
            rows_of(block, hidden),
            rows_of(block, width),
            rows_of(block, width),
            pl.BlockSpec((GROUP, heads, pad), lambda i: (i, 0, 0)),
            pl.BlockSpec((1, width), lambda i: (0, 0)),
        ],
        out_shape=[
            shape((rows, width), BFLOAT),
            shape((rows, width), BFLOAT),
            shape((rows, hidden), BFLOAT),
            shape((rows, hidden), BFLOAT),
            shape((rows, width), BFLOAT),
            shape((rows, width), BFLOAT),
            shape((count, heads, pad), FLOAT),
            shape((1, width), FLOAT),
        ],
        compiler_params=params(),
        cost_estimate=cost(6 * rows * width * hidden, 60e6),
        name="mlp",
    )(residual, cotangent, gain, up, down, out_w, mixed, scale)


def output_kernel(res_ref, act_ref, down_ref, output_ref):
    out = res_ref[...] + dot(act_ref[...], down_ref[...])
    output_ref[...] = out.astype(BFLOAT).reshape(output_ref.shape)


def mlp_output(residual, act, down, shape, first, steps, prior):
    count, frame_len, width = shape
    pad = padded_len(frame_len)
    block = GROUP * pad
    hidden = down.shape[0]
    return alias_call(
        output_kernel,
        (steps,),
        [rows_of(block, width, first), rows_of(block, hidden, first), whole(down.shape)],
        (residual, act, down),
        prior,
        [frames_of(pad, width, first)],
        [jax.ShapeDtypeStruct(shape, BFLOAT)],
        "mlp_output",
        2 * steps * block * width * hidden,
        8 * steps * block * width,
    )


def weight_grad_kernel(core_ref, left_ref, right_ref, *refs):
    send_ref, keep_ref = refs[-2:]
    total = dot_tn(left_ref[...], right_ref[...]).astype(BFLOAT)
    step = pl.program_id(0)

    @pl.when(step < 2)
    def _():
        send_ref[0] = total

    @pl.when(step >= 2)
    def _():
        keep_ref[0] = total


def up_grad(core, left, right, parts, prior):
    rows, width = left.shape
    lanes = right.shape[1] // parts

    def block(i, core_ref):
        return 2 * (i % 2) + jnp.where(i < 2, 1 - core_ref[0], core_ref[0])

    return pl.pallas_call(
        weight_grad_kernel,
        grid_spec=pltpu.PrefetchScalarGridSpec(
            num_scalar_prefetch=1,
            grid=(parts,),
            in_specs=[
                pl.BlockSpec(left.shape, lambda i, c: (0, 0), pipeline_mode=pl.Buffered(1)),
                pl.BlockSpec((rows, lanes), lambda i, c: (0, block(i, c))),
                pl.BlockSpec(memory_space=pl.ANY),
                pl.BlockSpec(memory_space=pl.ANY),
            ],
            out_specs=[
                pl.BlockSpec((1, width, lanes), lambda i, c: (jnp.minimum(i, 1), 0, 0)),
                pl.BlockSpec((1, width, lanes), lambda i, c: (jnp.maximum(i - 2, 0), 0, 0)),
            ],
        ),
        out_shape=[jax.ShapeDtypeStruct(p.shape, BFLOAT) for p in prior],
        input_output_aliases={3: 0, 4: 1},
        compiler_params=params(),
        cost_estimate=cost(2 * left.size * right.shape[1], 2 * (left.size + right.size)),
        name="grad_up",
    )(core, left, right, *prior)


def by_core(core, blocks):
    pairs = [(blocks[2 * y], blocks[2 * y + 1]) for y in range(len(blocks) // 2)]
    first = core == 0
    send = [jnp.where(first, odd, even) for even, odd in pairs]
    return send, [jnp.where(first, even, odd) for even, odd in pairs]


def down_grad_kernel(core_ref, left_ref, right_ref, send_ref, keep_ref):
    total = dot_tn(left_ref[...], right_ref[...]).astype(BFLOAT)
    parts, pieces, height, columns = 2 * send_ref.shape[0], *send_ref.shape[1:]
    for piece in range(pieces):
        cols = slice(piece * columns, (piece + 1) * columns)
        blocks = [total[part * height : (part + 1) * height, cols] for part in range(parts)]
        for ref, values in zip((send_ref, keep_ref), by_core(core_ref[0], blocks)):
            for y, value in enumerate(values):
                ref[y, piece] = value


def down_grad(core, left, right, parts, tile):
    rows, width = left.shape
    tiles = right.shape[1] // tile
    shape = (parts // 2, tiles, width // parts, tile)
    spec = pl.BlockSpec((parts // 2, 2, width // parts, tile), lambda i: (0, i, 0, 0))
    return pl.pallas_call(
        down_grad_kernel,
        grid=(tiles // 2,),
        in_specs=[
            pl.BlockSpec(memory_space=pltpu.SMEM),
            whole(left.shape),
            pl.BlockSpec((rows, 2 * tile), lambda i: (0, i)),
        ],
        out_specs=[spec, spec],
        out_shape=[jax.ShapeDtypeStruct(shape, BFLOAT)] * 2,
        compiler_params=params(),
        cost_estimate=cost(2 * left.size * right.shape[1], 2 * (left.size + right.size)),
        name="grad_down",
    )(core, left, right)


def with_gain(block, gain, lanes):
    column = jnp.broadcast_to(gain, (8, gain.shape[1])).T.astype(BFLOAT)
    blank = jnp.zeros((block.shape[0], lanes - block.shape[1] - 8), BFLOAT)
    return jnp.concatenate([block, column, blank], axis=1)


def store_split(core, total_ref, gain, send_refs, keep_refs):
    halves = send_refs[0].shape[0]
    parts = 2 * halves
    size = total_ref.shape[1] // parts
    lanes = sum(ref.shape[2] for ref in send_refs)
    for y in range(halves):
        blocks = [
            with_gain(total_ref[:, part * size : (part + 1) * size].astype(BFLOAT), gain, lanes)
            for part in (2 * y, 2 * y + 1)
        ]
        for refs, (value,) in zip((send_refs, keep_refs), by_core(core, blocks)):
            offset = 0
            for ref in refs:
                ref[y] = value[:, offset : offset + ref.shape[2]]
                offset += ref.shape[2]


def split_grad_kernel(core_ref, left_ref, right_ref, gain_ref, send_ref, keep_ref, all_ref):
    step = pl.program_id(0)
    tile = right_ref.shape[1]
    all_ref[:, pl.ds(pl.multiple_of(step * tile, tile), tile)] = dot_tn(
        left_ref[...], right_ref[...]
    ).astype(BFLOAT)

    @pl.when(step == pl.num_programs(0) - 1)
    def _():
        store_split(core_ref[0], all_ref, gain_ref[...], [send_ref], [keep_ref])


def split_grad(core, left, right, gain, tile, parts, shape, index, name):
    rows, width = left.shape
    columns = right.shape[1]
    size = -(-columns // parts // LANES) * LANES
    spec = pl.BlockSpec((parts // 2, width, size), lambda i: (0, 0, index))
    return pl.pallas_call(
        split_grad_kernel,
        grid=(columns // tile,),
        in_specs=[
            pl.BlockSpec(memory_space=pltpu.SMEM),
            whole(left.shape),
            pl.BlockSpec((rows, tile), lambda i: (0, i)),
            whole(gain.shape),
        ],
        out_specs=[spec, spec],
        out_shape=[jax.ShapeDtypeStruct(shape, BFLOAT)] * 2,
        scratch_shapes=[pltpu.VMEM((width, columns), BFLOAT)],
        compiler_params=params(),
        cost_estimate=cost(2 * left.size * columns, 2 * (left.size + right.size)),
        name=name,
    )(core, left, right, gain)


def attend_back_kernel(
    frame_len,
    core_ref,
    proj_ref,
    token_ref,
    expo_ref,
    grad_mixed_ref,
    delta_ref,
    x_ref,
    branch_ref,
    message_ref,
    gain_ref,
    w_ref,
    grad_in_ref,
    class_ref,
    message_grad_ref,
    send_0_ref,
    send_1_ref,
    keep_0_ref,
    keep_1_ref,
    scores_ref,
    grad_proj_ref,
    total_ref,
    gain_grad_ref,
):
    pad = expo_ref.shape[2]
    width = grad_mixed_ref.shape[1]
    pairs = width // PAIR
    step = pl.program_id(0)

    @pl.when(step == 0)
    def _():
        total_ref[...] = jnp.zeros_like(total_ref)
        gain_grad_ref[...] = jnp.zeros_like(gain_grad_ref)

    def at(part, j):
        return pl.ds(part * width + j * PAIR, PAIR)

    def weigh(f, j):
        rows = pl.ds(f * pad, pad)
        value = token_in(proj_ref[rows, at(2, j)], token_ref[f, :, at(1, j)], frame_len)
        grad = grad_mixed_ref[rows, at(0, j)]
        for h in range(2):
            head = 2 * j + h
            grad_prob = dot_nt(value, one_head(grad, h)) - delta_ref[f, head : head + 1, :]
            scores_ref[f, head] = expo_ref[f, head] * grad_prob.astype(BFLOAT)

    def mix(f, j):
        rows = pl.ds(f * pad, pad)
        query = proj_ref[rows, at(0, j)]
        key = token_in(proj_ref[rows, at(1, j)], token_ref[f, :, at(0, j)], frame_len)
        grad = grad_mixed_ref[rows, at(0, j)]
        key_t = key.astype(FLOAT).T.astype(BFLOAT)
        grad_query, grad_key, grad_value = [], [], []
        for h in range(2):
            scores = scores_ref[f, 2 * j + h]
            grad_value.append(dot(expo_ref[f, 2 * j + h], one_head(grad, h)))
            grad_key.append(dot(scores, one_head(query, h)))
            grad_query.append(dot(key_t[h * HD : (h + 1) * HD], scores))
        grad_query = jnp.concatenate(grad_query, axis=0).T * 0.125
        grad_proj_ref[rows, at(0, j)] = grad_query.astype(BFLOAT)
        grad_key = (grad_key[0] + grad_key[1]) * 0.125
        grad_proj_ref[rows, at(1, j)] = grad_key.astype(BFLOAT)
        grad_value = grad_value[0] + grad_value[1]
        grad_proj_ref[rows, at(2, j)] = grad_value.astype(BFLOAT)

    units = [(f, j) for j in range(pairs) for f in range(GROUP)]
    for i in range(len(units) + 2):
        if i < len(units):
            weigh(*units[i])
        if i >= 2:
            mix(*units[i - 2])

    values = load_rows(x_ref, frame_len)
    values = jnp.concatenate(
        [
            token_in(values[f * pad : (f + 1) * pad], message_ref[f].astype(FLOAT), frame_len)
            for f in range(GROUP)
        ]
    )
    normed, scale_inv = normalize(values)
    hidden = (normed * gain_ref[...]).astype(BFLOAT)
    for part in range(3):
        cols = slice(part * width, (part + 1) * width)
        total_ref[:, cols] += dot_tn(hidden, grad_proj_ref[:, cols])
    grad = dot_nt(grad_proj_ref[...], w_ref[...])
    gain_grad_ref[...] += jnp.sum(grad * normed, axis=0, keepdims=True)
    total = branch_ref[...].astype(FLOAT) + norm_back(grad * gain_ref[...], normed, scale_inv)
    total = total.reshape(GROUP, pad, width)
    grad_in_ref[...] = total.astype(BFLOAT)
    for f in range(GROUP):
        class_ref[f] = total[f, :1]
        message_grad_ref[f] = total[f, frame_len : frame_len + 1].astype(BFLOAT)

    @pl.when(step == pl.num_programs(0) - 1)
    def _():
        store_split(
            core_ref[0],
            total_ref,
            gain_grad_ref[...],
            [send_0_ref, send_1_ref],
            [keep_0_ref, keep_1_ref],
        )


def attend_back(
    core, proj, token_kv, expo, grad_mixed, delta, frames_in, branch, message, gain, qkv, parts
):
    count, heads, pad, _ = expo.shape
    frame_len, width = frames_in.shape[1:]
    block = GROUP * pad
    lanes = -(-3 * width // parts // LANES) * LANES
    first = lanes // (2 * LANES) * LANES + LANES
    sums = [(parts // 2, width, n) for n in (first, lanes - first)] * 2
    shape = jax.ShapeDtypeStruct
    return pl.pallas_call(
        functools.partial(attend_back_kernel, frame_len),
        grid=(count // GROUP,),
        in_specs=[
            pl.BlockSpec(memory_space=pltpu.SMEM),
            rows_of(block, 3 * width),
            frames_of(1, 2 * width),
            pl.BlockSpec((GROUP, heads, pad, pad), lambda i: (i, 0, 0, 0)),
            rows_of(block, width),
            pl.BlockSpec((GROUP, heads, pad), lambda i: (i, 0, 0)),
            frames_of(pad, width),
            rows_of(block, width),
            frames_of(1, width),
            whole((width,)),
            whole(qkv.shape),
        ],
        out_specs=[frames_of(pad, width), frames_of(1, width), frames_of(1, width)]
        + [whole(s) for s in sums],
        out_shape=[
            shape((count, frame_len, width), BFLOAT),
            shape((count, 1, width), FLOAT),
            shape((count, 1, width), BFLOAT),
        ]
        + [shape(s, BFLOAT) for s in sums],
        scratch_shapes=[
            pltpu.VMEM((GROUP, heads, pad, pad), BFLOAT),
            pltpu.VMEM((block, 3 * width), BFLOAT),
            pltpu.VMEM((width, 3 * width), FLOAT),
            pltpu.VMEM((1, width), FLOAT),
        ],
        compiler_params=params(),
        cost_estimate=cost(45e9, 50e6),
        name="attend_back",
    )(core, proj, token_kv, expo, grad_mixed, delta, frames_in, branch, message, gain, qkv)


def in_turn(count, slots, first, second):
    if slots > 256:

        def both(j, carry):
            first(j)
            second(j)
            return carry

        lax.fori_loop(0, count, both, 0)
        return
    for j in range(count + 2):
        if j < count:
            first(j)
        if j >= 2:
            second(j - 2)


def message_kernel(
    own,
    class_ref,
    weight_ref,
    gain_ref,
    qkv_ref,
    out_w_ref,
    attn_gain_ref,
    key_w_ref,
    value_w_ref,
    start_ref,
    hidden_ref,
    proj_ref,
    prob_ref,
    mixed_ref,
    message_ref,
    token_kv_ref,
):
    width = weight_ref.shape[0]
    start = dot(class_ref[:, :width], weight_ref[...]).astype(BFLOAT)
    start_ref[...] = start
    normed, _ = normalize(start.astype(FLOAT))
    hidden = (normed * gain_ref[...]).astype(BFLOAT)
    hidden_ref[...] = hidden
    proj_ref[...] = dot(hidden, qkv_ref[...]).astype(BFLOAT)
    digits = class_ref[:, width:].astype(FLOAT)
    lane = lax.broadcasted_iota(jnp.int32, digits.shape, 1)
    weights = jnp.where(lane == 0, 1.0, jnp.where(lane == 1, BASE, BASE * BASE))
    digits = jnp.where(lane < DIGITS, digits * weights, 0.0)
    id_col = jnp.sum(digits, axis=1, keepdims=True)
    id_row = jnp.sum(digits.T, axis=0, keepdims=True)
    visible = id_col == id_row

    def at(part, j):
        start = part * width + j * PAIR
        return pl.ds(start if isinstance(j, int) else pl.multiple_of(start, PAIR), PAIR)

    def weigh(j):
        query = proj_ref[:, at(0, j)] * 0.125
        for h in range(2):
            scores = jnp.where(visible, dot_nt(proj_ref[:, at(1, j)], one_head(query, h)), NEG)
            expo = jnp.exp(scores - jnp.max(scores, axis=0, keepdims=True))
            prob = expo * (1.0 / jnp.sum(expo, axis=0, keepdims=True))
            prob_ref[2 * j + h] = prob.astype(BFLOAT)

    def mix(j):
        value_t = proj_ref[:, at(2, j)].astype(FLOAT).T.astype(BFLOAT)
        outs = [dot(value_t[h * HD : (h + 1) * HD], prob_ref[2 * j + h]) for h in range(2)]
        mixed_ref[:, at(0, j)] = jnp.concatenate(outs, axis=0).T.astype(BFLOAT)

    in_turn(width // PAIR, start.shape[0], weigh, mix)
    message = start[:own].astype(FLOAT) + dot(mixed_ref[:own, :], out_w_ref[...])
    message = message.astype(BFLOAT)
    message_ref[...] = message
    normed, _ = normalize(message.astype(FLOAT))
    token_hidden = (normed * attn_gain_ref[...]).astype(BFLOAT)
    token_kv_ref[:, :width] = dot(token_hidden, key_w_ref[...]).astype(BFLOAT)
    token_kv_ref[:, width:] = dot(token_hidden, value_w_ref[...]).astype(BFLOAT)


def message_forward(class_all, own, weight, gain, qkv, out_w, attn_gain, attn_qkv):
    slots = class_all.shape[0]
    width = weight.shape[0]
    heads = width // HD
    shape = jax.ShapeDtypeStruct
    part = lambda index: pl.BlockSpec((width, width), lambda i, index=index: (0, index))
    return pl.pallas_call(
        functools.partial(message_kernel, own),
        grid=(1,),
        in_specs=[
            whole(class_all.shape),
            whole(weight.shape),
            whole((width,)),
            whole(qkv.shape),
            whole(out_w.shape),
            whole((width,)),
            part(1),
            part(2),
        ],
        out_specs=[
            whole((slots, width)),
            whole((slots, width)),
            whole((slots, 3 * width)),
            whole((heads, slots, slots)),
            whole((slots, width)),
            whole((own, width)),
            whole((own, 2 * width)),
        ],
        out_shape=[
            shape((slots, width), BFLOAT),
            shape((slots, width), BFLOAT),
            shape((slots, 3 * width), BFLOAT),
            shape((heads, slots, slots), BFLOAT),
            shape((slots, width), BFLOAT),
            shape((own, width), BFLOAT),
            shape((own, 2 * width), BFLOAT),
        ],
        compiler_params=params(),
        cost_estimate=cost(7e9, 9e6),
        name="message_forward",
    )(
        class_all,
        weight,
        gain,
        qkv,
        out_w,
        attn_gain,
        attn_qkv,
        attn_qkv,
    )


def message_back_kernel(
    own,
    parts,
    together,
    block_ref,
    grad_ref,
    class_ref,
    start_ref,
    hidden_ref,
    proj_ref,
    prob_ref,
    mixed_ref,
    weight_ref,
    gain_ref,
    qkv_ref,
    out_w_ref,
    class_grad_ref,
    sums_ref,
    grad_mixed_ref,
    grad_proj_ref,
    scores_ref,
):
    width = weight_ref.shape[0]
    grad = grad_ref[...]
    j = pl.program_id(0)

    @pl.when(j == 0)
    def _():
        grad_mixed_ref[...] = dot_nt(grad, out_w_ref[...]).astype(BFLOAT)

    def finish():
        grad_proj = grad_proj_ref[...]
        grad_hidden = dot_nt(grad_proj, qkv_ref[...])
        normed, scale_inv = normalize(start_ref[...].astype(FLOAT))
        gain_grad = jnp.sum(grad_hidden * normed, axis=0, keepdims=True)
        back = norm_back(grad_hidden * gain_ref[...], normed, scale_inv)
        start_grad = (grad.astype(FLOAT) + back).astype(BFLOAT)
        class_grad_ref[...] = dot_nt(start_grad[:own], weight_ref[...])
        size = sums_ref.shape[1]
        row = lax.broadcasted_iota(jnp.int32, (size, width), 0)
        column = lax.broadcasted_iota(jnp.int32, (size, width), 1)
        mine = column == row + block_ref[0] * size
        pick = mine.astype(BFLOAT)
        gain_grad = jnp.sum(jnp.where(mine, gain_grad, 0.0), axis=1, keepdims=True)
        lanes = sums_ref.shape[2] - 5 * width // parts
        for part in range(parts):
            sums_ref[part, :, 5 * width // parts :] = jnp.broadcast_to(
                gain_grad, (size, lanes)
            ).astype(BFLOAT)
        offset = 0
        for left, right in (
            (hidden_ref[...], grad_proj),
            (class_ref[:, :width], start_grad),
            (mixed_ref[...], grad),
        ):
            total = dot(dot_nt(pick, left).astype(BFLOAT), right).astype(BFLOAT)
            columns = total.shape[1] // parts
            for part in range(parts):
                sums_ref[part, :, offset : offset + columns] = total[
                    :, part * columns : (part + 1) * columns
                ]
            offset += columns

    def at(part, k):
        if together == 1:
            return pl.ds(pl.multiple_of(part * width + j * PAIR, PAIR), PAIR)
        return pl.ds(part * width + k * PAIR, PAIR)

    def weigh(k):
        value = proj_ref[:, at(2, k)]
        for h in range(2):
            grad_prob = dot_nt(value, one_head(grad_mixed_ref[:, at(0, k)], h))
            prob = prob_ref[2 * k + h].astype(FLOAT)
            part = prob * grad_prob
            scores = part - prob * jnp.sum(part, axis=0, keepdims=True)
            scores_ref[2 * k + h] = scores.astype(BFLOAT)

    def mix(k):
        query, key, grad_m = proj_ref[:, at(0, k)], proj_ref[:, at(1, k)], grad_mixed_ref[:, at(0, k)]
        key_t = key.astype(FLOAT).T.astype(BFLOAT)
        grad_query, grad_key, grad_value = [], [], []
        for h in range(2):
            scores = scores_ref[2 * k + h]
            grad_value.append(dot(prob_ref[2 * k + h], one_head(grad_m, h)))
            grad_key.append(dot(scores, one_head(query, h)))
            grad_query.append(dot(key_t[h * HD : (h + 1) * HD], scores))
        grad_query = jnp.concatenate(grad_query, axis=0).T * 0.125
        grad_proj_ref[:, at(0, k)] = grad_query.astype(BFLOAT)
        grad_proj_ref[:, at(1, k)] = ((grad_key[0] + grad_key[1]) * 0.125).astype(BFLOAT)
        grad_proj_ref[:, at(2, k)] = (grad_value[0] + grad_value[1]).astype(BFLOAT)

    if together == 1:
        weigh(0)
        mix(0)
    else:
        in_turn(together, grad.shape[0], weigh, mix)

    @pl.when(j == pl.num_programs(0) - 1)
    def _():
        finish()


def message_back(block, parts, size, own, grad_all, class_all, saved, weight, gain, qkv, out_w):
    slots, width = grad_all.shape
    start, hidden, proj, prob, mixed = saved
    shape = jax.ShapeDtypeStruct
    sums = (parts, size, -(-(5 * width // parts + 1) // LANES) * LANES)
    together = width // PAIR if slots <= 256 else 1
    args = (grad_all, class_all, start, hidden, proj, prob, mixed, weight, gain, qkv, out_w)
    return pl.pallas_call(
        functools.partial(message_back_kernel, own, parts, together),
        grid=(width // PAIR // together,),
        in_specs=[pl.BlockSpec(memory_space=pltpu.SMEM)]
        + [pl.BlockSpec((2 * together, slots, slots), lambda j: (j, 0, 0)) if a is prob else whole(a.shape) for a in args],
        out_specs=[whole((own, width)), whole(sums)],
        out_shape=[shape((own, width), FLOAT), shape(sums, BFLOAT)],
        scratch_shapes=[
            pltpu.VMEM((slots, width), BFLOAT),
            pltpu.VMEM((slots, 3 * width), BFLOAT),
            pltpu.VMEM((2 * together, slots, slots), BFLOAT),
        ],
        compiler_params=params(),
        cost_estimate=cost(8e9, 9e6),
        name="message_back",
    )(block, *args)


def swap(values, axis, distance):
    return lax.ppermute(values, axis, [(i, i ^ distance) for i in range(lax.axis_size(axis))])


def tied(values, *others):
    return lax.optimization_barrier((values, others))[0]


def pick(values, index, axis=0):
    return lax.dynamic_index_in_dim(values, index, axis, keepdims=False)


def add(*terms):
    total = terms[0].astype(FLOAT)
    for term in terms[1:]:
        total = total + term.astype(FLOAT)
    return total


class Gather:
    def __init__(self, axis, values):
        self.axis, self.values = axis, values
        self.distance, self.left = 1, lax.axis_size(axis)

    def begin(self):
        while self.left > 8:
            self.finish(self.start(2))
        self.got = self.start(2 if self.left == 8 else self.left)

    def start(self, size):
        got = [swap(self.values, self.axis, d * self.distance) for d in range(1, size)]
        self.distance, self.left = self.distance * size, self.left // size
        return got

    def finish(self, got):
        self.values = jnp.concatenate([self.values, *got])

    def end(self, *after):
        self.finish(tied(self.got, *after))
        return self.values


class Sum:
    def __init__(self, values):
        self.values = values

    @classmethod
    def of_cores(cls, sent, kept):
        self = cls(None)
        self.keep, self.sent = kept, sent
        self.got = [swap(sent, "rows", 1)]
        return self

    def begin(self, axis, distance, dim):
        bit = (lax.axis_index(axis) // distance) % 2
        self.keep = pick(self.values, bit, dim)
        self.sent = pick(self.values, 1 - bit, dim)
        self.got = [swap(self.sent, axis, distance)]
        return self.sent

    def end(self, *after):
        self.values = add(*tied(self.got, *after), self.keep).astype(BFLOAT)
        return self.values

    def begin_frames(self, dim=0):
        self.left, self.distance, self.dim = lax.axis_size("frames"), 1, dim
        shape = self.values.shape
        if len(shape) == 2 + dim:
            self.values = self.values.reshape(*shape[:dim], self.left, -1, shape[-1])
        while self.left > 8:
            self.step_frames()
            self.end()
        return self.step_frames()

    def step_frames(self):
        shape, dim = self.values.shape, self.dim
        self.values = self.values.reshape(*shape[:dim], self.left // 2, 2, *shape[dim + 1 :])
        sent = self.begin("frames", self.distance, dim + 1)
        self.left, self.distance = self.left // 2, self.distance * 2
        return sent

    def begin_last(self):
        index = lax.axis_index("frames") // self.distance
        self.keep = pick(self.values, index)
        sent = [pick(self.values, index ^ d) for d in range(1, self.left)]
        self.got = [
            swap(block, "frames", (d + 1) * self.distance) for d, block in enumerate(sent)
        ]
        return sent

    def end_last(self, *after):
        return add(*tied(self.got, *after), self.keep)


def per_device(
    frames_in,
    cotangent,
    video_ids,
    frame_device,
    msg_weight,
    msg_gain,
    msg_qkv,
    msg_out,
    attn_gain,
    attn_qkv,
    attn_out,
    mlp_gain,
    up_weight,
    down_weight,
):
    count, frame_len, width = frames_in.shape
    owners, parts = lax.axis_size("frames"), lax.axis_size("rows")
    hidden_width = up_weight.shape[1]
    own = -(-count // 16) * 16
    steps = count // GROUP
    block_index = lax.axis_index("frames").astype(jnp.int32).reshape(1)
    extra = ((0, own - count), (0, 0))

    ids = (video_ids * owners + frame_device)[:, None]
    base = int(BASE)
    digits = jnp.concatenate([ids % base, ids // base % base, ids // (base * base)], axis=1)
    digits = jnp.pad(digits, ((0, own - count), (0, LANES - DIGITS)), constant_values=-1)
    payload = jnp.concatenate([jnp.pad(frames_in[:, 0, :], extra), digits.astype(BFLOAT)], axis=1)
    gather = Gather("frames", payload)
    gather.begin()
    frames = tied(frames_in, payload)
    early = steps // 2
    projected = project(frames, attn_gain, attn_qkv, 0, early, None)
    gather.end(projected[0])
    gather.begin()
    (proj,) = project(
        tied(frames, gather.values), attn_gain, attn_qkv, early, steps - early, projected
    )
    class_all = gather.end(proj)

    *saved, message, token_kv = message_forward(
        class_all, own, msg_weight, msg_gain, msg_qkv, msg_out, attn_gain, attn_qkv
    )
    token_kv = token_kv[:count, None]
    message = message[:count, None]
    expo, mixed, scale, residual = attend(frames_in, proj, token_kv, attn_out)
    cot, second, act, grad_up, branch, grad_mixed, delta, mlp_gain_grad = mlp(
        residual, cotangent, mlp_gain, up_weight, down_weight, attn_out, mixed, scale
    )

    core = (lax.axis_index("rows") % 2).astype(jnp.int32).reshape(1)
    tile = 3 * LANES
    tiles = hidden_width // tile
    down = Sum.of_cores(*down_grad(core, cot, act, parts, tile))
    lanes = hidden_width // parts
    out_lanes = -(-width // parts // LANES) * LANES
    shape = (parts // 2, width, lanes + out_lanes)
    out_sums = split_grad(
        core,
        tied(mixed, down.sent),
        branch,
        mlp_gain_grad,
        256,
        parts,
        shape,
        lanes // out_lanes,
        "grad_attn_out",
    )
    values = down.end(*out_sums)
    split = tiles * 5 // 8
    down_a, down_b = Sum(values[:, :split]), Sum(values[:, split:])
    sent = down_a.begin("rows", 2, 0)
    up = Sum.of_cores(*up_grad(core, tied(second, sent), grad_up, parts, out_sums))

    def finish_output(first, number, prior, *others):
        return mlp_output(
            tied(residual, *others), act, down_weight, frames_in.shape, first, number, prior
        )

    pieces = (2, 2, steps - 4)
    down_a.end(up.sent)
    output = finish_output(0, pieces[0], None, up.sent, down_b.begin("rows", 2, 0))
    down.values = jnp.concatenate([down_a.values, down_b.end(output)])
    if tiles != owners:
        moved = jnp.swapaxes(down.values, 0, 1).reshape(width // parts, owners, -1)
        down.values = jnp.swapaxes(moved, 0, 1)
    up.end(output)
    sent = [down.begin_frames(), up.begin("rows", 2, 0)]
    grad_in, class_rows, message_grad, *qkv_sums = attend_back(
        core,
        proj,
        token_kv,
        expo,
        tied(grad_mixed, sent),
        delta,
        frames_in,
        branch,
        message,
        attn_gain,
        attn_qkv,
        parts,
    )
    message_grad = jnp.pad(message_grad.reshape(count, width), extra)
    gather = Gather("frames", message_grad)
    gather.begin()
    qkv_a, qkv_b = (Sum.of_cores(qkv_sums[i], qkv_sums[2 + i]) for i in range(2))
    down.end(message_grad)
    values = up.end(message_grad)
    split = values.shape[-1] // 2
    up_a, up_b = Sum(values[..., :split]), Sum(values[..., split:])
    sent = [message_grad, down.begin_last(), up_a.begin_frames()]
    output = finish_output(pieces[0], pieces[1], output, sent)
    gather.end(output)
    gather.begin()
    qkv_a.end(output)
    qkv_b.end(output)
    up_a.end(output)
    sent = [gather.values, qkv_a.begin("rows", 2, 0), qkv_b.begin_frames(1), up_b.begin_frames()]
    grad_down = down.end_last(output).T
    output = finish_output(sum(pieces[:2]), pieces[2], output, sent)
    grad_all = gather.end(output)
    up.values = jnp.concatenate([up_a.values, up_b.end(output)], axis=2)
    up.left, up.distance = up_a.left, up_a.distance
    qkv_a.end(output)
    qkv_b.end(output)
    sent = [up.begin_last(), qkv_a.begin_frames(), qkv_b.begin("rows", 2, 0)]
    class_grad, msg_sums = message_back(
        block_index,
        parts,
        width // owners,
        own,
        tied(grad_all, sent),
        class_all,
        saved,
        msg_weight,
        msg_gain,
        msg_qkv,
        msg_out,
    )
    msg = Sum(msg_sums.reshape(2, 2, *msg_sums.shape[1:]))
    msg.begin("rows", 1, 1)
    qkv = Sum(jnp.concatenate([qkv_a.end(msg_sums), qkv_b.end(msg_sums)], axis=2))
    qkv.left, qkv.distance = qkv_a.left, qkv_a.distance
    qkv.begin_last()
    msg.end()
    msg.begin("rows", 2, 0)
    class_rows = (class_rows[:, 0] + class_grad[:count]).astype(BFLOAT)
    grad_in = lax.dynamic_update_slice(grad_in, class_rows[:, None], (0, 0, 0))
    grad_up = up.end_last(msg_sums)
    msg_total = add(msg.got[0], msg.keep)
    grad_qkv = qkv.end_last()
    third, fourth, fifth = (n * width // parts for n in (3, 4, 5))
    return (
        output[0],
        grad_in,
        msg_total[:, third:fourth],
        msg_total[:, fifth],
        msg_total[:, :third],
        msg_total[:, fourth:fifth],
        grad_qkv[:, third],
        grad_qkv[:, :third],
        grad_up[:, lanes : lanes + width // parts],
        grad_up[:, lanes + width // parts],
        grad_up[:, :lanes],
        grad_down,
    )


def solution(mesh):
    split = P(("frames", "rows"))
    matrix = P("frames", "rows")
    gain = P("frames")
    return jax.shard_map(
        per_device,
        mesh=mesh,
        in_specs=(split, split, split, split) + (P(),) * 10,
        out_specs=(
            split,
            split,
            matrix,
            gain,
            matrix,
            matrix,
            gain,
            matrix,
            matrix,
            gain,
            matrix,
            matrix,
        ),
        check_vma=False,
    )
```

```python
import functools

import jax
import jax.numpy as jnp
import numpy as np
from jax import lax
from jax.experimental import pallas as pl
from jax.experimental.pallas import tpu as pltpu
from jax.sharding import PartitionSpec as P

H = 12
HD = 64
PAIR = 2 * HD
GROUP = 2
EPS = 1e-05
NEG = -1e30
BASE = 128.0
DIGITS = 3
LANES = 128
FLOAT = jnp.float32
BFLOAT = jnp.bfloat16
VMEM_BYTES = 60 * 1024 * 1024


def params(**kw):
    return pltpu.CompilerParams(vmem_limit_bytes=VMEM_BYTES, **kw)


def cost(flops, moved):
    return pl.CostEstimate(flops=int(flops / 100), transcendentals=0, bytes_accessed=int(moved / 100))


def padded_len(frame_len):
    return -(-(frame_len + 1) // 8) * 8


def whole(shape):
    return pl.BlockSpec(shape, lambda *_: (0,) * len(shape), pipeline_mode=pl.Buffered(1))


def rows_of(height, width, first=0):
    return pl.BlockSpec((height, width), lambda i: (i + first, 0))


def frames_of(pad, width, first=0):
    return pl.BlockSpec((GROUP, pad, width), lambda i: (i + first, 0, 0))


def normalize(values):
    center = values - jnp.mean(values, axis=-1, keepdims=True)
    spread = jnp.mean(center * center, axis=-1, keepdims=True)
    scale_inv = lax.rsqrt(spread + EPS)
    return (center * scale_inv, scale_inv)


def norm_back(grad_normed, normed, scale_inv):
    return scale_inv * (
        grad_normed
        - jnp.mean(grad_normed, axis=-1, keepdims=True)
        - normed * jnp.mean(grad_normed * normed, axis=-1, keepdims=True)
    )


def dot(a, b):
    return jnp.dot(a, b, preferred_element_type=FLOAT)


def dot_nt(a, b):
    return lax.dot_general(a, b, (((1,), (1,)), ((), ())), preferred_element_type=FLOAT)


def dot_tn(a, b):
    return lax.dot_general(a, b, (((0,), (0,)), ((), ())), preferred_element_type=FLOAT)


def load_rows(ref, frame_len):
    values = ref[...].astype(FLOAT)
    count, pad, width = values.shape
    row = lax.broadcasted_iota(jnp.int32, values.shape, 1)
    return jnp.where(row < frame_len, values, 0.0).reshape(count * pad, width)


def project_kernel(frame_len, x_ref, gain_ref, w_ref, proj_ref):
    normed, _ = normalize(load_rows(x_ref, frame_len))
    hidden = (normed * gain_ref[...]).astype(BFLOAT)
    width = hidden.shape[1]
    for part in range(3):
        cols = slice(part * width, (part + 1) * width)
        proj_ref[:, cols] = dot(hidden, w_ref[:, cols]).astype(BFLOAT)


def alias_call(
    kernel, grid, in_specs, args, prior, out_specs, out_shape, name, flops, moved, scratch=()
):
    extra = [] if prior is None else list(prior)

    def body(*refs):
        kernel(*refs[: len(args)], *refs[len(args) + len(extra) :])

    return pl.pallas_call(
        body,
        grid=grid,
        in_specs=in_specs + [pl.BlockSpec(memory_space=pl.ANY)] * len(extra),
        out_specs=out_specs,
        out_shape=out_shape,
        input_output_aliases={len(args) + i: i for i in range(len(extra))},
        scratch_shapes=list(scratch),
        compiler_params=params(),
        cost_estimate=cost(flops, moved),
        name=name,
    )(*args, *extra)


def project(frames_in, gain, qkv, first, steps, prior):
    count, frame_len, width = frames_in.shape
    pad = padded_len(frame_len)
    block = GROUP * pad
    return alias_call(
        functools.partial(project_kernel, frame_len),
        (steps,),
        [frames_of(pad, width, first), whole((width,)), whole(qkv.shape)],
        (frames_in, gain, qkv),
        prior,
        [rows_of(block, 3 * width, first)],
        [jax.ShapeDtypeStruct((count * pad, 3 * width), BFLOAT)],
        "project",
        6 * steps * block * width * width,
        8 * steps * block * width,
    )


def last_rows(rows, change):
    cut = rows.shape[0] - 8
    return jnp.concatenate([rows[:cut], change(rows[cut:], cut)], axis=0)


def token_in(rows, token, frame_len):
    def change(tail, cut):
        row = lax.broadcasted_iota(jnp.int32, tail.shape, 0)
        return jnp.where(row == frame_len - cut, token, tail)

    return last_rows(rows, change)


def one_head(pair, h):
    lane = lax.broadcasted_iota(jnp.int32, pair.shape, 1)
    return jnp.where((lane >= HD) == (h == 1), pair, jnp.zeros_like(pair))


def attend_kernel(
    frame_len, x_ref, proj_ref, token_ref, out_w_ref, expo_ref, mixed_ref, scale_ref, res_ref
):
    width = x_ref.shape[2]
    pad = x_ref.shape[1]
    pairs = width // PAIR

    def hide(tail, cut):
        row = lax.broadcasted_iota(jnp.int32, tail.shape, 0)
        return jnp.where(row <= frame_len - cut, tail, NEG)

    def at(part, j):
        return pl.ds(part * width + j * PAIR, PAIR)

    def weigh(f, j):
        rows = pl.ds(f * pad, pad)
        query = proj_ref[rows, at(0, j)] * 0.125
        key = token_in(proj_ref[rows, at(1, j)], token_ref[f, :, at(0, j)], frame_len)
        for h in range(2):
            scores = last_rows(dot_nt(key, one_head(query, h)), hide)
            expo = jnp.exp(scores - jnp.max(scores, axis=0, keepdims=True)).astype(BFLOAT)
            expo_ref[f, 2 * j + h] = expo

    def mix(f, j):
        rows = pl.ds(f * pad, pad)
        value = token_in(proj_ref[rows, at(2, j)], token_ref[f, :, at(1, j)], frame_len)
        value_t = value.astype(FLOAT).T.astype(BFLOAT)
        outs = []
        for h in range(2):
            ones = jnp.ones((8, pad), BFLOAT)
            out = dot(jnp.concatenate([value_t[h * HD : (h + 1) * HD], ones]), expo_ref[f, 2 * j + h])
            scale = 1.0 / out[HD : HD + 1]
            outs.append(out[:HD] * scale)
            scale_ref[f, 2 * j + h : 2 * j + h + 1, :] = scale
        mixed_ref[rows, at(0, j)] = jnp.concatenate(outs, axis=0).T.astype(BFLOAT)

    units = [(f, j) for j in range(pairs) for f in range(GROUP)]
    for i in range(len(units) + 2):
        if i < len(units):
            weigh(*units[i])
        if i >= 2:
            mix(*units[i - 2])
    residual = load_rows(x_ref, frame_len) + dot(mixed_ref[...], out_w_ref[...])
    res_ref[...] = residual.astype(BFLOAT)


def attend(frames_in, proj, token_kv, out_w):
    count, frame_len, width = frames_in.shape
    pad = padded_len(frame_len)
    block = GROUP * pad
    heads = width // HD
    return pl.pallas_call(
        functools.partial(attend_kernel, frame_len),
        grid=(count // GROUP,),
        in_specs=[
            frames_of(pad, width),
            rows_of(block, 3 * width),
            frames_of(1, 2 * width),
            whole(out_w.shape),
        ],
        out_specs=[
            pl.BlockSpec((GROUP, heads, pad, pad), lambda i: (i, 0, 0, 0)),
            rows_of(block, width),
            frames_of(heads, pad),
            rows_of(block, width),
        ],
        out_shape=[
            jax.ShapeDtypeStruct((count, heads, pad, pad), BFLOAT),
            jax.ShapeDtypeStruct((count * pad, width), BFLOAT),
            jax.ShapeDtypeStruct((count, heads, pad), FLOAT),
            jax.ShapeDtypeStruct((count * pad, width), BFLOAT),
        ],
        compiler_params=params(),
        cost_estimate=cost(25e9, 50e6),
        name="attend",
    )(frames_in, proj, token_kv, out_w)


def mlp_kernel(
    frame_len,
    parts,
    res_ref,
    cot_ref,
    gain_ref,
    up_ref,
    down_ref,
    out_w_ref,
    mixed_ref,
    scale_ref,
    cot_rows_ref,
    second_ref,
    act_ref,
    grad_up_ref,
    branch_ref,
    grad_mixed_ref,
    delta_ref,
    gain_grad_ref,
):
    residual = res_ref[...].astype(FLOAT)
    width = residual.shape[1]
    normed, scale_inv = normalize(residual)
    gain = gain_ref[...]
    second = (normed * gain).astype(BFLOAT)
    second_ref[...] = second
    cot = load_rows(cot_ref, frame_len)
    cot_bf = cot.astype(BFLOAT)
    cot_rows_ref[...] = cot_bf
    grad_second = jnp.zeros_like(residual)
    size = up_ref.shape[1] // parts
    for part in range(parts):
        cols = slice(part * size, (part + 1) * size)
        up_part = dot(second, up_ref[:, cols])
        sigma = 0.5 * jnp.tanh(0.851 * up_part) + 0.5
        gated = up_part * sigma
        act = gated.astype(BFLOAT)
        act_ref[:, cols] = act
        grad_act = dot_nt(cot_bf, down_ref[cols, :])
        grad_up = (grad_act * (sigma + 1.702 * gated * (1.0 - sigma))).astype(BFLOAT)
        grad_up_ref[:, cols] = grad_up
        grad_second = grad_second + dot_nt(grad_up, up_ref[:, cols])
    gain_grad = jnp.sum(grad_second * normed, axis=0, keepdims=True)
    step = pl.program_id(0)
    gain_grad_ref[...] = jnp.where(step == 0, 0.0, gain_grad_ref[...]) + gain_grad
    branch = (cot + norm_back(grad_second * gain, normed, scale_inv)).astype(BFLOAT)
    branch_ref[...] = branch
    heads, pad = delta_ref.shape[1:]
    head = lax.broadcasted_iota(jnp.int32, (heads, width), 0)
    lane = lax.broadcasted_iota(jnp.int32, (heads, width), 1)
    of_head = (lane // HD == head).astype(FLOAT)
    scales = []
    for f in range(GROUP):
        high = scale_ref[f].astype(BFLOAT).astype(FLOAT)
        rows = jnp.concatenate([high, scale_ref[f] - high]).astype(BFLOAT)
        scales.append(dot_tn(rows, jnp.concatenate([of_head, of_head]).astype(BFLOAT)))
    of_head = of_head.astype(BFLOAT)
    grad_mixed = dot_nt(branch, out_w_ref[...]) * jnp.concatenate(scales)
    grad_mixed = grad_mixed.astype(BFLOAT)
    grad_mixed_ref[...] = grad_mixed
    product = grad_mixed * mixed_ref[...]
    for f in range(GROUP):
        delta_ref[f] = dot_nt(of_head, product[f * pad : (f + 1) * pad])


def mlp(residual, cotangent, gain, up, down, out_w, mixed, scale):
    count, frame_len, width = cotangent.shape
    pad = padded_len(frame_len)
    block = GROUP * pad
    rows = count * pad
    heads = width // HD
    hidden = up.shape[1]
    shape = jax.ShapeDtypeStruct
    return pl.pallas_call(
        functools.partial(mlp_kernel, frame_len, 4),
        grid=(count // GROUP,),
        in_specs=[
            rows_of(block, width),
            frames_of(pad, width),
            whole((width,)),
            whole(up.shape),
            whole(down.shape),
            whole(out_w.shape),
            rows_of(block, width),
            frames_of(heads, pad),
        ],
        out_specs=[
            rows_of(block, width),
            rows_of(block, width),
            rows_of(block, hidden),
            rows_of(block, hidden),
            rows_of(block, width),
            rows_of(block, width),
            pl.BlockSpec((GROUP, heads, pad), lambda i: (i, 0, 0)),
            pl.BlockSpec((1, width), lambda i: (0, 0)),
        ],
        out_shape=[
            shape((rows, width), BFLOAT),
            shape((rows, width), BFLOAT),
            shape((rows, hidden), BFLOAT),
            shape((rows, hidden), BFLOAT),
            shape((rows, width), BFLOAT),
            shape((rows, width), BFLOAT),
            shape((count, heads, pad), FLOAT),
            shape((1, width), FLOAT),
        ],
        compiler_params=params(),
        cost_estimate=cost(6 * rows * width * hidden, 60e6),
        name="mlp",
    )(residual, cotangent, gain, up, down, out_w, mixed, scale)


def output_kernel(res_ref, act_ref, down_ref, output_ref):
    out = res_ref[...].astype(FLOAT) + dot(act_ref[...], down_ref[...])
    output_ref[...] = out.astype(BFLOAT).reshape(output_ref.shape)


def mlp_output(residual, act, down, shape, first, steps, prior):
    count, frame_len, width = shape
    pad = padded_len(frame_len)
    block = GROUP * pad
    hidden = down.shape[0]
    return alias_call(
        output_kernel,
        (steps,),
        [rows_of(block, width, first), rows_of(block, hidden, first), whole(down.shape)],
        (residual, act, down),
        prior,
        [frames_of(pad, width, first)],
        [jax.ShapeDtypeStruct(shape, BFLOAT)],
        "mlp_output",
        2 * steps * block * width * hidden,
        8 * steps * block * width,
    )


def weight_grad_kernel(core_ref, left_ref, right_ref, *refs):
    send_ref, keep_ref = refs[-2:]
    total = dot_tn(left_ref[...], right_ref[...]).astype(BFLOAT)
    step = pl.program_id(0)

    @pl.when(step < 2)
    def _():
        send_ref[0] = total

    @pl.when(step >= 2)
    def _():
        keep_ref[0] = total


def up_grad(core, left, right, parts, prior):
    rows, width = left.shape
    lanes = right.shape[1] // parts

    def block(i, core_ref):
        return 2 * (i % 2) + jnp.where(i < 2, 1 - core_ref[0], core_ref[0])

    return pl.pallas_call(
        weight_grad_kernel,
        grid_spec=pltpu.PrefetchScalarGridSpec(
            num_scalar_prefetch=1,
            grid=(parts,),
            in_specs=[
                pl.BlockSpec(left.shape, lambda i, c: (0, 0), pipeline_mode=pl.Buffered(1)),
                pl.BlockSpec((rows, lanes), lambda i, c: (0, block(i, c))),
                pl.BlockSpec(memory_space=pl.ANY),
                pl.BlockSpec(memory_space=pl.ANY),
            ],
            out_specs=[
                pl.BlockSpec((1, width, lanes), lambda i, c: (jnp.minimum(i, 1), 0, 0)),
                pl.BlockSpec((1, width, lanes), lambda i, c: (jnp.maximum(i - 2, 0), 0, 0)),
            ],
        ),
        out_shape=[jax.ShapeDtypeStruct(p.shape, BFLOAT) for p in prior],
        input_output_aliases={3: 0, 4: 1},
        compiler_params=params(),
        cost_estimate=cost(2 * left.size * right.shape[1], 2 * (left.size + right.size)),
        name="grad_up",
    )(core, left, right, *prior)


def by_core(core, blocks):
    pairs = [(blocks[2 * y], blocks[2 * y + 1]) for y in range(len(blocks) // 2)]
    first = core == 0
    send = [jnp.where(first, odd, even) for even, odd in pairs]
    return send, [jnp.where(first, even, odd) for even, odd in pairs]


def down_grad_kernel(core_ref, left_ref, right_ref, send_ref, keep_ref):
    total = dot_tn(left_ref[...], right_ref[...]).astype(BFLOAT)
    parts, pieces, height, columns = 2 * send_ref.shape[0], *send_ref.shape[1:]
    for piece in range(pieces):
        cols = slice(piece * columns, (piece + 1) * columns)
        blocks = [total[part * height : (part + 1) * height, cols] for part in range(parts)]
        for ref, values in zip((send_ref, keep_ref), by_core(core_ref[0], blocks)):
            for y, value in enumerate(values):
                ref[y, piece] = value


def down_grad(core, left, right, parts, tile):
    rows, width = left.shape
    tiles = right.shape[1] // tile
    shape = (parts // 2, tiles, width // parts, tile)
    spec = pl.BlockSpec((parts // 2, 2, width // parts, tile), lambda i: (0, i, 0, 0))
    return pl.pallas_call(
        down_grad_kernel,
        grid=(tiles // 2,),
        in_specs=[
            pl.BlockSpec(memory_space=pltpu.SMEM),
            whole(left.shape),
            pl.BlockSpec((rows, 2 * tile), lambda i: (0, i)),
        ],
        out_specs=[spec, spec],
        out_shape=[jax.ShapeDtypeStruct(shape, BFLOAT)] * 2,
        compiler_params=params(),
        cost_estimate=cost(2 * left.size * right.shape[1], 2 * (left.size + right.size)),
        name="grad_down",
    )(core, left, right)


def with_gain(block, gain, lanes):
    column = jnp.broadcast_to(gain, (8, gain.shape[1])).T.astype(BFLOAT)
    blank = jnp.zeros((block.shape[0], lanes - block.shape[1] - 8), BFLOAT)
    return jnp.concatenate([block, column, blank], axis=1)


def store_split(core, total_ref, gain, send_refs, keep_refs):
    halves = send_refs[0].shape[0]
    parts = 2 * halves
    size = total_ref.shape[1] // parts
    lanes = sum(ref.shape[2] for ref in send_refs)
    for y in range(halves):
        blocks = [
            with_gain(total_ref[:, part * size : (part + 1) * size].astype(BFLOAT), gain, lanes)
            for part in (2 * y, 2 * y + 1)
        ]
        for refs, (value,) in zip((send_refs, keep_refs), by_core(core, blocks)):
            offset = 0
            for ref in refs:
                ref[y] = value[:, offset : offset + ref.shape[2]]
                offset += ref.shape[2]


def split_grad_kernel(core_ref, left_ref, right_ref, gain_ref, send_ref, keep_ref, all_ref):
    step = pl.program_id(0)
    tile = right_ref.shape[1]
    all_ref[:, pl.ds(pl.multiple_of(step * tile, tile), tile)] = dot_tn(
        left_ref[...], right_ref[...]
    ).astype(BFLOAT)

    @pl.when(step == pl.num_programs(0) - 1)
    def _():
        store_split(core_ref[0], all_ref, gain_ref[...], [send_ref], [keep_ref])


def split_grad(core, left, right, gain, tile, parts, shape, index, name):
    rows, width = left.shape
    columns = right.shape[1]
    size = -(-columns // parts // LANES) * LANES
    spec = pl.BlockSpec((parts // 2, width, size), lambda i: (0, 0, index))
    return pl.pallas_call(
        split_grad_kernel,
        grid=(columns // tile,),
        in_specs=[
            pl.BlockSpec(memory_space=pltpu.SMEM),
            whole(left.shape),
            pl.BlockSpec((rows, tile), lambda i: (0, i)),
            whole(gain.shape),
        ],
        out_specs=[spec, spec],
        out_shape=[jax.ShapeDtypeStruct(shape, BFLOAT)] * 2,
        scratch_shapes=[pltpu.VMEM((width, columns), BFLOAT)],
        compiler_params=params(),
        cost_estimate=cost(2 * left.size * columns, 2 * (left.size + right.size)),
        name=name,
    )(core, left, right, gain)


def attend_back_kernel(
    frame_len,
    core_ref,
    proj_ref,
    token_ref,
    expo_ref,
    grad_mixed_ref,
    delta_ref,
    x_ref,
    branch_ref,
    message_ref,
    gain_ref,
    w_ref,
    grad_in_ref,
    class_ref,
    message_grad_ref,
    send_0_ref,
    send_1_ref,
    keep_0_ref,
    keep_1_ref,
    scores_ref,
    grad_proj_ref,
    total_ref,
    gain_grad_ref,
):
    pad = expo_ref.shape[2]
    width = grad_mixed_ref.shape[1]
    pairs = width // PAIR
    step = pl.program_id(0)

    @pl.when(step == 0)
    def _():
        total_ref[...] = jnp.zeros_like(total_ref)
        gain_grad_ref[...] = jnp.zeros_like(gain_grad_ref)

    def at(part, j):
        return pl.ds(part * width + j * PAIR, PAIR)

    def weigh(f, j):
        rows = pl.ds(f * pad, pad)
        value = token_in(proj_ref[rows, at(2, j)], token_ref[f, :, at(1, j)], frame_len)
        grad = grad_mixed_ref[rows, at(0, j)]
        for h in range(2):
            head = 2 * j + h
            grad_prob = dot_nt(value, one_head(grad, h)) - delta_ref[f, head : head + 1, :]
            scores_ref[f, head] = expo_ref[f, head] * grad_prob.astype(BFLOAT)

    def mix(f, j):
        rows = pl.ds(f * pad, pad)
        query = proj_ref[rows, at(0, j)]
        key = token_in(proj_ref[rows, at(1, j)], token_ref[f, :, at(0, j)], frame_len)
        grad = grad_mixed_ref[rows, at(0, j)]
        key_t = key.astype(FLOAT).T.astype(BFLOAT)
        grad_query, grad_key, grad_value = [], [], []
        for h in range(2):
            scores = scores_ref[f, 2 * j + h]
            grad_value.append(dot(expo_ref[f, 2 * j + h], one_head(grad, h)))
            grad_key.append(dot(scores, one_head(query, h)))
            grad_query.append(dot(key_t[h * HD : (h + 1) * HD], scores))
        grad_query = jnp.concatenate(grad_query, axis=0).T * 0.125
        grad_proj_ref[rows, at(0, j)] = grad_query.astype(BFLOAT)
        grad_key = (grad_key[0] + grad_key[1]) * 0.125
        grad_proj_ref[rows, at(1, j)] = grad_key.astype(BFLOAT)
        grad_value = grad_value[0] + grad_value[1]
        grad_proj_ref[rows, at(2, j)] = grad_value.astype(BFLOAT)

    units = [(f, j) for j in range(pairs) for f in range(GROUP)]
    for i in range(len(units) + 2):
        if i < len(units):
            weigh(*units[i])
        if i >= 2:
            mix(*units[i - 2])

    values = load_rows(x_ref, frame_len)
    values = jnp.concatenate(
        [
            token_in(values[f * pad : (f + 1) * pad], message_ref[f].astype(FLOAT), frame_len)
            for f in range(GROUP)
        ]
    )
    normed, scale_inv = normalize(values)
    hidden = (normed * gain_ref[...]).astype(BFLOAT)
    for part in range(3):
        cols = slice(part * width, (part + 1) * width)
        total_ref[:, cols] += dot_tn(hidden, grad_proj_ref[:, cols])
    grad = dot_nt(grad_proj_ref[...], w_ref[...])
    gain_grad_ref[...] += jnp.sum(grad * normed, axis=0, keepdims=True)
    total = branch_ref[...].astype(FLOAT) + norm_back(grad * gain_ref[...], normed, scale_inv)
    total = total.reshape(GROUP, pad, width)
    grad_in_ref[...] = total.astype(BFLOAT)
    for f in range(GROUP):
        class_ref[f] = total[f, :1]
        message_grad_ref[f] = total[f, frame_len : frame_len + 1].astype(BFLOAT)

    @pl.when(step == pl.num_programs(0) - 1)
    def _():
        store_split(
            core_ref[0],
            total_ref,
            gain_grad_ref[...],
            [send_0_ref, send_1_ref],
            [keep_0_ref, keep_1_ref],
        )


def attend_back(
    core, proj, token_kv, expo, grad_mixed, delta, frames_in, branch, message, gain, qkv, parts
):
    count, heads, pad, _ = expo.shape
    frame_len, width = frames_in.shape[1:]
    block = GROUP * pad
    lanes = -(-3 * width // parts // LANES) * LANES
    first = lanes // (2 * LANES) * LANES + LANES
    sums = [(parts // 2, width, n) for n in (first, lanes - first)] * 2
    shape = jax.ShapeDtypeStruct
    return pl.pallas_call(
        functools.partial(attend_back_kernel, frame_len),
        grid=(count // GROUP,),
        in_specs=[
            pl.BlockSpec(memory_space=pltpu.SMEM),
            rows_of(block, 3 * width),
            frames_of(1, 2 * width),
            pl.BlockSpec((GROUP, heads, pad, pad), lambda i: (i, 0, 0, 0)),
            rows_of(block, width),
            pl.BlockSpec((GROUP, heads, pad), lambda i: (i, 0, 0)),
            frames_of(pad, width),
            rows_of(block, width),
            frames_of(1, width),
            whole((width,)),
            whole(qkv.shape),
        ],
        out_specs=[frames_of(pad, width), frames_of(1, width), frames_of(1, width)]
        + [whole(s) for s in sums],
        out_shape=[
            shape((count, frame_len, width), BFLOAT),
            shape((count, 1, width), FLOAT),
            shape((count, 1, width), BFLOAT),
        ]
        + [shape(s, BFLOAT) for s in sums],
        scratch_shapes=[
            pltpu.VMEM((GROUP, heads, pad, pad), BFLOAT),
            pltpu.VMEM((block, 3 * width), BFLOAT),
            pltpu.VMEM((width, 3 * width), FLOAT),
            pltpu.VMEM((1, width), FLOAT),
        ],
        compiler_params=params(),
        cost_estimate=cost(45e9, 50e6),
        name="attend_back",
    )(core, proj, token_kv, expo, grad_mixed, delta, frames_in, branch, message, gain, qkv)


def in_turn(count, slots, first, second):
    if slots > 256:

        def both(j, carry):
            first(j)
            second(j)
            return carry

        lax.fori_loop(0, count, both, 0)
        return
    for j in range(count + 2):
        if j < count:
            first(j)
        if j >= 2:
            second(j - 2)


def message_kernel(
    own,
    class_ref,
    weight_ref,
    gain_ref,
    qkv_ref,
    out_w_ref,
    attn_gain_ref,
    key_w_ref,
    value_w_ref,
    start_ref,
    hidden_ref,
    proj_ref,
    prob_ref,
    mixed_ref,
    message_ref,
    token_kv_ref,
):
    width = weight_ref.shape[0]
    start = dot(class_ref[:, :width], weight_ref[...]).astype(BFLOAT)
    start_ref[...] = start
    normed, _ = normalize(start.astype(FLOAT))
    hidden = (normed * gain_ref[...]).astype(BFLOAT)
    hidden_ref[...] = hidden
    proj_ref[...] = dot(hidden, qkv_ref[...]).astype(BFLOAT)
    digits = class_ref[:, width:].astype(FLOAT)
    lane = lax.broadcasted_iota(jnp.int32, digits.shape, 1)
    weights = jnp.where(lane == 0, 1.0, jnp.where(lane == 1, BASE, BASE * BASE))
    digits = jnp.where(lane < DIGITS, digits * weights, 0.0)
    id_col = jnp.sum(digits, axis=1, keepdims=True)
    id_row = jnp.sum(digits.T, axis=0, keepdims=True)
    visible = id_col == id_row

    def at(part, j):
        start = part * width + j * PAIR
        return pl.ds(start if isinstance(j, int) else pl.multiple_of(start, PAIR), PAIR)

    def weigh(j):
        query = proj_ref[:, at(0, j)] * 0.125
        for h in range(2):
            scores = jnp.where(visible, dot_nt(proj_ref[:, at(1, j)], one_head(query, h)), NEG)
            expo = jnp.exp(scores - jnp.max(scores, axis=0, keepdims=True))
            prob = expo * (1.0 / jnp.sum(expo, axis=0, keepdims=True))
            prob_ref[2 * j + h] = prob.astype(BFLOAT)

    def mix(j):
        value_t = proj_ref[:, at(2, j)].astype(FLOAT).T.astype(BFLOAT)
        outs = [dot(value_t[h * HD : (h + 1) * HD], prob_ref[2 * j + h]) for h in range(2)]
        mixed_ref[:, at(0, j)] = jnp.concatenate(outs, axis=0).T.astype(BFLOAT)

    in_turn(width // PAIR, start.shape[0], weigh, mix)
    message = start[:own].astype(FLOAT) + dot(mixed_ref[:own, :], out_w_ref[...])
    message = message.astype(BFLOAT)
    message_ref[...] = message
    normed, _ = normalize(message.astype(FLOAT))
    token_hidden = (normed * attn_gain_ref[...]).astype(BFLOAT)
    token_kv_ref[:, :width] = dot(token_hidden, key_w_ref[...]).astype(BFLOAT)
    token_kv_ref[:, width:] = dot(token_hidden, value_w_ref[...]).astype(BFLOAT)


def message_forward(class_all, own, weight, gain, qkv, out_w, attn_gain, attn_qkv):
    slots = class_all.shape[0]
    width = weight.shape[0]
    heads = width // HD
    shape = jax.ShapeDtypeStruct
    part = lambda index: pl.BlockSpec((width, width), lambda i, index=index: (0, index))
    return pl.pallas_call(
        functools.partial(message_kernel, own),
        grid=(1,),
        in_specs=[
            whole(class_all.shape),
            whole(weight.shape),
            whole((width,)),
            whole(qkv.shape),
            whole(out_w.shape),
            whole((width,)),
            part(1),
            part(2),
        ],
        out_specs=[
            whole((slots, width)),
            whole((slots, width)),
            whole((slots, 3 * width)),
            whole((heads, slots, slots)),
            whole((slots, width)),
            whole((own, width)),
            whole((own, 2 * width)),
        ],
        out_shape=[
            shape((slots, width), BFLOAT),
            shape((slots, width), BFLOAT),
            shape((slots, 3 * width), BFLOAT),
            shape((heads, slots, slots), BFLOAT),
            shape((slots, width), BFLOAT),
            shape((own, width), BFLOAT),
            shape((own, 2 * width), BFLOAT),
        ],
        compiler_params=params(),
        cost_estimate=cost(7e9, 9e6),
        name="message_forward",
    )(
        class_all,
        weight,
        gain,
        qkv,
        out_w,
        attn_gain,
        attn_qkv,
        attn_qkv,
    )


def message_back_kernel(
    own,
    parts,
    together,
    block_ref,
    grad_ref,
    class_ref,
    start_ref,
    hidden_ref,
    proj_ref,
    prob_ref,
    mixed_ref,
    weight_ref,
    gain_ref,
    qkv_ref,
    out_w_ref,
    class_grad_ref,
    sums_ref,
    grad_mixed_ref,
    grad_proj_ref,
    scores_ref,
):
    width = weight_ref.shape[0]
    grad = grad_ref[...]
    j = pl.program_id(0)

    @pl.when(j == 0)
    def _():
        grad_mixed_ref[...] = dot_nt(grad, out_w_ref[...]).astype(BFLOAT)

    def finish():
        grad_proj = grad_proj_ref[...]
        grad_hidden = dot_nt(grad_proj, qkv_ref[...])
        normed, scale_inv = normalize(start_ref[...].astype(FLOAT))
        gain_grad = jnp.sum(grad_hidden * normed, axis=0, keepdims=True)
        back = norm_back(grad_hidden * gain_ref[...], normed, scale_inv)
        start_grad = (grad.astype(FLOAT) + back).astype(BFLOAT)
        class_grad_ref[...] = dot_nt(start_grad[:own], weight_ref[...])
        size = sums_ref.shape[1]
        row = lax.broadcasted_iota(jnp.int32, (size, width), 0)
        column = lax.broadcasted_iota(jnp.int32, (size, width), 1)
        mine = column == row + block_ref[0] * size
        pick = mine.astype(BFLOAT)
        gain_grad = jnp.sum(jnp.where(mine, gain_grad, 0.0), axis=1, keepdims=True)
        lanes = sums_ref.shape[2] - 5 * width // parts
        for part in range(parts):
            sums_ref[part, :, 5 * width // parts :] = jnp.broadcast_to(
                gain_grad, (size, lanes)
            ).astype(BFLOAT)
        offset = 0
        for left, right in (
            (hidden_ref[...], grad_proj),
            (class_ref[:, :width], start_grad),
            (mixed_ref[...], grad),
        ):
            total = dot(dot_nt(pick, left).astype(BFLOAT), right).astype(BFLOAT)
            columns = total.shape[1] // parts
            for part in range(parts):
                sums_ref[part, :, offset : offset + columns] = total[
                    :, part * columns : (part + 1) * columns
                ]
            offset += columns

    def at(part, k):
        if together == 1:
            return pl.ds(pl.multiple_of(part * width + j * PAIR, PAIR), PAIR)
        return pl.ds(part * width + k * PAIR, PAIR)

    def weigh(k):
        value = proj_ref[:, at(2, k)]
        for h in range(2):
            grad_prob = dot_nt(value, one_head(grad_mixed_ref[:, at(0, k)], h))
            prob = prob_ref[2 * k + h].astype(FLOAT)
            part = prob * grad_prob
            scores = part - prob * jnp.sum(part, axis=0, keepdims=True)
            scores_ref[2 * k + h] = scores.astype(BFLOAT)

    def mix(k):
        query, key, grad_m = proj_ref[:, at(0, k)], proj_ref[:, at(1, k)], grad_mixed_ref[:, at(0, k)]
        key_t = key.astype(FLOAT).T.astype(BFLOAT)
        grad_query, grad_key, grad_value = [], [], []
        for h in range(2):
            scores = scores_ref[2 * k + h]
            grad_value.append(dot(prob_ref[2 * k + h], one_head(grad_m, h)))
            grad_key.append(dot(scores, one_head(query, h)))
            grad_query.append(dot(key_t[h * HD : (h + 1) * HD], scores))
        grad_query = jnp.concatenate(grad_query, axis=0).T * 0.125
        grad_proj_ref[:, at(0, k)] = grad_query.astype(BFLOAT)
        grad_proj_ref[:, at(1, k)] = ((grad_key[0] + grad_key[1]) * 0.125).astype(BFLOAT)
        grad_proj_ref[:, at(2, k)] = (grad_value[0] + grad_value[1]).astype(BFLOAT)

    if together == 1:
        weigh(0)
        mix(0)
    else:
        in_turn(together, grad.shape[0], weigh, mix)

    @pl.when(j == pl.num_programs(0) - 1)
    def _():
        finish()


def message_back(block, parts, size, own, grad_all, class_all, saved, weight, gain, qkv, out_w):
    slots, width = grad_all.shape
    start, hidden, proj, prob, mixed = saved
    shape = jax.ShapeDtypeStruct
    sums = (parts, size, -(-(5 * width // parts + 1) // LANES) * LANES)
    together = width // PAIR if slots <= 256 else 1
    args = (grad_all, class_all, start, hidden, proj, prob, mixed, weight, gain, qkv, out_w)
    return pl.pallas_call(
        functools.partial(message_back_kernel, own, parts, together),
        grid=(width // PAIR // together,),
        in_specs=[pl.BlockSpec(memory_space=pltpu.SMEM)]
        + [pl.BlockSpec((2 * together, slots, slots), lambda j: (j, 0, 0)) if a is prob else whole(a.shape) for a in args],
        out_specs=[whole((own, width)), whole(sums)],
        out_shape=[shape((own, width), FLOAT), shape(sums, BFLOAT)],
        scratch_shapes=[
            pltpu.VMEM((slots, width), BFLOAT),
            pltpu.VMEM((slots, 3 * width), BFLOAT),
            pltpu.VMEM((2 * together, slots, slots), BFLOAT),
        ],
        compiler_params=params(),
        cost_estimate=cost(8e9, 9e6),
        name="message_back",
    )(block, *args)


def swap(values, axis, distance):
    return lax.ppermute(values, axis, [(i, i ^ distance) for i in range(lax.axis_size(axis))])


def tied(values, *others):
    return lax.optimization_barrier((values, others))[0]


def meet(outputs, *transfers):
    outputs, got = lax.optimization_barrier((outputs, [transfer.got for transfer in transfers]))
    for transfer, values in zip(transfers, got):
        transfer.got = values
    return outputs


def pick(values, index, axis=0):
    return lax.dynamic_index_in_dim(values, index, axis, keepdims=False)


def add(*terms):
    total = terms[0].astype(FLOAT)
    for term in terms[1:]:
        total = total + term.astype(FLOAT)
    return total


class Gather:
    def __init__(self, axis, values):
        self.axis, self.values = axis, values
        self.distance, self.left = 1, lax.axis_size(axis)

    def begin(self, direct=True):
        while self.left > 8:
            self.finish(self.start(2))
        self.got = self.start(self.left if direct and self.left < 8 else 2)

    def start(self, size):
        got = [swap(self.values, self.axis, d * self.distance) for d in range(1, size)]
        self.distance, self.left = self.distance * size, self.left // size
        return got

    def finish(self, got):
        self.values = jnp.concatenate([self.values, *got])

    def end(self):
        self.finish(self.got)
        return self.values


class Sum:
    def __init__(self, terms):
        self.terms = terms

    @classmethod
    def of_cores(cls, sent, kept):
        self = cls([kept])
        self.sent = sent
        self.got = [swap(sent, "rows", 1)]
        return self

    def part(self, index):
        return Sum([term[index] for term in self.terms])

    def total(self):
        return add(*self.terms)

    def begin(self, axis, distance, dim):
        bit = (lax.axis_index(axis) // distance) % 2
        sent = add(*(pick(term, 1 - bit, dim) for term in self.terms)).astype(BFLOAT)
        self.terms = [pick(term, bit, dim) for term in self.terms]
        self.got = [swap(sent, axis, distance)]
        return sent

    def end(self, apart=False):
        self.terms = self.got + self.terms
        if not apart:
            self.terms = [self.total().astype(BFLOAT)]

    def begin_frames(self, dim=0):
        self.left, self.distance, self.dim = lax.axis_size("frames"), 1, dim
        shape = self.terms[0].shape
        if len(shape) == 2 + dim:
            shape = (*shape[:dim], self.left, -1, shape[-1])
            self.terms = [term.reshape(shape) for term in self.terms]
        while self.left > 8:
            self.step_frames()
            self.end()
        return self.step_frames()

    def step_frames(self):
        shape, dim = self.terms[0].shape, self.dim
        shape = (*shape[:dim], self.left // 2, 2, *shape[dim + 1 :])
        self.terms = [term.reshape(shape) for term in self.terms]
        sent = self.begin("frames", self.distance, dim + 1)
        self.left, self.distance = self.left // 2, self.distance * 2
        return sent

    def begin_last(self):
        index = lax.axis_index("frames") // self.distance
        sent = [
            add(*(pick(term, index ^ d) for term in self.terms)).astype(BFLOAT)
            for d in range(1, self.left)
        ]
        self.terms = [pick(term, index) for term in self.terms]
        self.got = [
            swap(block, "frames", (d + 1) * self.distance) for d, block in enumerate(sent)
        ]
        return sent


def joined(first, second, axis):
    self = Sum([jnp.concatenate([first.total(), second.total()], axis=axis).astype(BFLOAT)])
    if hasattr(first, "left"):
        self.left, self.distance, self.dim = first.left, first.distance, first.dim
    return self


def per_device(
    frames_in,
    cotangent,
    video_ids,
    frame_device,
    msg_weight,
    msg_gain,
    msg_qkv,
    msg_out,
    attn_gain,
    attn_qkv,
    attn_out,
    mlp_gain,
    up_weight,
    down_weight,
):
    count, frame_len, width = frames_in.shape
    owners, parts = lax.axis_size("frames"), lax.axis_size("rows")
    hidden_width = up_weight.shape[1]
    own = -(-count // 16) * 16
    steps = count // GROUP
    block_index = lax.axis_index("frames").astype(jnp.int32).reshape(1)
    extra = ((0, own - count), (0, 0))

    ids = (video_ids * owners + frame_device)[:, None]
    base = int(BASE)
    digits = jnp.concatenate([ids % base, ids // base % base, ids // (base * base)], axis=1)
    digits = jnp.pad(digits, ((0, own - count), (0, LANES - DIGITS)), constant_values=-1)
    payload = jnp.concatenate([jnp.pad(frames_in[:, 0, :], extra), digits.astype(BFLOAT)], axis=1)
    gather = Gather("frames", payload)
    gather.begin()
    frames = tied(frames_in, payload)
    early = steps // 2
    projected = meet(project(frames, attn_gain, attn_qkv, 0, early, None), gather)
    gather.end()
    gather.begin()
    (proj,) = project(
        tied(frames, gather.values), attn_gain, attn_qkv, early, steps - early, projected
    )
    proj = meet(proj, gather)
    class_all = gather.end()

    *saved, message, token_kv = message_forward(
        class_all, own, msg_weight, msg_gain, msg_qkv, msg_out, attn_gain, attn_qkv
    )
    token_kv = token_kv[:count, None]
    message = message[:count, None]
    expo, mixed, scale, residual = attend(frames_in, proj, token_kv, attn_out)
    cot, second, act, grad_up, branch, grad_mixed, delta, mlp_gain_grad = mlp(
        residual, cotangent, mlp_gain, up_weight, down_weight, attn_out, mixed, scale
    )

    core = (lax.axis_index("rows") % 2).astype(jnp.int32).reshape(1)
    tile = 3 * LANES
    tiles = hidden_width // tile
    down = Sum.of_cores(*down_grad(core, cot, act, parts, tile))
    lanes = hidden_width // parts
    out_lanes = -(-width // parts // LANES) * LANES
    shape = (parts // 2, width, lanes + out_lanes)
    out_sums = split_grad(
        core,
        tied(mixed, down.sent),
        branch,
        mlp_gain_grad,
        256,
        parts,
        shape,
        lanes // out_lanes,
        "grad_attn_out",
    )
    out_sums = meet(out_sums, down)
    down.end(apart=True)
    split = tiles * 5 // 8
    down_a, down_b = down.part(np.s_[:, :split]), down.part(np.s_[:, split:])
    sent = down_a.begin("rows", 2, 0)
    up_sums = up_grad(core, tied(second, sent), grad_up, parts, out_sums)
    up = Sum.of_cores(*meet(up_sums, down_a))

    def finish_output(first, number, prior, *others):
        return mlp_output(
            tied(residual, *others), act, down_weight, frames_in.shape, first, number, prior
        )

    pieces = (2, 2, steps - 4)
    down_a.end(apart=True)
    sent = [up.sent, down_b.begin("rows", 2, 0)]
    output = meet(finish_output(0, pieces[0], None, sent), down_b, up)
    down_b.end(apart=True)
    down = joined(down_a, down_b, 0)
    if tiles != owners:
        moved = jnp.swapaxes(down.terms[0], 0, 1).reshape(width // parts, owners, -1)
        down.terms = [jnp.swapaxes(moved, 0, 1)]
    up.end(apart=True)
    split = shape[-1] // 2
    up_a, up_b = up.part(np.s_[..., :split]), up.part(np.s_[..., split:])
    sent = [down.begin_frames(), up_a.begin("rows", 2, 0), up_b.begin_frames(1)]
    grads = attend_back(
        core,
        proj,
        token_kv,
        expo,
        tied(grad_mixed, sent),
        delta,
        frames_in,
        branch,
        message,
        attn_gain,
        attn_qkv,
        parts,
    )
    grad_in, class_rows, message_grad, *qkv_sums = meet(grads, down, up_a, up_b)
    message_grad = jnp.pad(message_grad.reshape(count, width), extra)
    gather = Gather("frames", message_grad)
    gather.begin()
    qkv_a, qkv_b = (Sum.of_cores(qkv_sums[i], qkv_sums[2 + i]) for i in range(2))
    for one in (down, up_a, up_b):
        one.end()
    gather.got = tied(gather.got, up_a.terms, up_b.terms, down.terms)
    gather.end()
    gather.begin(direct=False)
    sent = [gather.values, down.step_frames(), up_a.begin_frames(), up_b.begin("rows", 2, 0)]
    sent = meet(sent, qkv_a, qkv_b)
    qkv_a.end()
    qkv_b.end()
    sent = [sent, qkv_a.begin("rows", 2, 0), qkv_b.begin_frames(1)]
    output = finish_output(pieces[0], pieces[1], output, sent)
    output = meet(output, gather, down, up_a, up_b, qkv_a, qkv_b)
    gather.end()
    gather.begin(direct=False)
    down.end(apart=True)
    up_a.end(apart=True)
    up_b.end(apart=True)
    up = joined(up_a, up_b, 2)
    qkv_a.end()
    qkv_b.end()
    sent = [
        gather.values,
        down.begin_last(),
        up.step_frames(),
        qkv_a.begin_frames(),
        qkv_b.begin("rows", 2, 0),
    ]
    output = finish_output(sum(pieces[:2]), pieces[2], output, sent)
    output = meet(output, gather, down, up, qkv_a, qkv_b)
    gather.end()
    grad_all = gather.values
    up.end(apart=True)
    qkv_a.end(apart=True)
    qkv_b.end(apart=True)
    qkv = joined(qkv_a, qkv_b, 2)
    down.end(apart=True)
    grad_down = down.total().T
    sent = [up.begin_last(), qkv.begin_last(), grad_down]
    grads = message_back(
        block_index,
        parts,
        width // owners,
        own,
        tied(grad_all, sent),
        class_all,
        saved,
        msg_weight,
        msg_gain,
        msg_qkv,
        msg_out,
    )
    class_grad, msg_sums = meet(grads, up, qkv)
    msg = Sum([msg_sums.reshape(2, 2, *msg_sums.shape[1:])])
    msg.begin("rows", 1, 1)
    up.end(apart=True)
    qkv.end(apart=True)
    grad_up, grad_qkv = up.total(), qkv.total()
    class_rows = (class_rows[:, 0] + class_grad[:count]).astype(BFLOAT)
    grad_in = lax.dynamic_update_slice(grad_in, class_rows[:, None], (0, 0, 0))
    msg.end()
    msg.begin("rows", 2, 0)
    msg.end(apart=True)
    msg_total = msg.total()
    third, fourth, fifth = (n * width // parts for n in (3, 4, 5))
    return (
        output[0],
        grad_in,
        msg_total[:, third:fourth],
        msg_total[:, fifth],
        msg_total[:, :third],
        msg_total[:, fourth:fifth],
        grad_qkv[:, third],
        grad_qkv[:, :third],
        grad_up[:, lanes : lanes + width // parts],
        grad_up[:, lanes + width // parts],
        grad_up[:, :lanes],
        grad_down,
    )


def solution(mesh):
    split = P(("frames", "rows"))
    matrix = P("frames", "rows")
    gain = P("frames")
    return jax.shard_map(
        per_device,
        mesh=mesh,
        in_specs=(split, split, split, split) + (P(),) * 10,
        out_specs=(
            split,
            split,
            matrix,
            gain,
            matrix,
            matrix,
            gain,
            matrix,
            matrix,
            gain,
            matrix,
            matrix,
        ),
        check_vma=False,
    )
```

```python
import functools

import jax
import jax.numpy as jnp
import numpy as np
from jax import lax
from jax.experimental import pallas as pl
from jax.experimental.pallas import tpu as pltpu
from jax.sharding import PartitionSpec as P

H = 12
HD = 64
PAIR = 2 * HD
GROUP = 2
EPS = 1e-05
NEG = -1e30
BASE = 128.0
DIGITS = 3
LANES = 128
FLOAT = jnp.float32
BFLOAT = jnp.bfloat16
VMEM_BYTES = 60 * 1024 * 1024


def params(**kw):
    return pltpu.CompilerParams(vmem_limit_bytes=VMEM_BYTES, **kw)


def cost(flops, moved):
    return pl.CostEstimate(flops=int(flops / 100), transcendentals=0, bytes_accessed=int(moved / 100))


def padded_len(frame_len):
    return -(-(frame_len + 1) // 8) * 8


def whole(shape):
    return pl.BlockSpec(shape, lambda *_: (0,) * len(shape), pipeline_mode=pl.Buffered(1))


def rows_of(height, width, first=0):
    return pl.BlockSpec((height, width), lambda i: (i + first, 0))


def frames_of(pad, width, first=0):
    return pl.BlockSpec((GROUP, pad, width), lambda i: (i + first, 0, 0))


def normalize(values):
    center = values - jnp.mean(values, axis=-1, keepdims=True)
    spread = jnp.mean(center * center, axis=-1, keepdims=True)
    scale_inv = lax.rsqrt(spread + EPS)
    return (center * scale_inv, scale_inv)


def norm_back(grad_normed, normed, scale_inv):
    return scale_inv * (
        grad_normed
        - jnp.mean(grad_normed, axis=-1, keepdims=True)
        - normed * jnp.mean(grad_normed * normed, axis=-1, keepdims=True)
    )


def dot(a, b):
    return jnp.dot(a, b, preferred_element_type=FLOAT)


def dot_nt(a, b):
    return lax.dot_general(a, b, (((1,), (1,)), ((), ())), preferred_element_type=FLOAT)


def dot_tn(a, b):
    return lax.dot_general(a, b, (((0,), (0,)), ((), ())), preferred_element_type=FLOAT)


def load_rows(ref, frame_len):
    values = ref[...].astype(FLOAT)
    count, pad, width = values.shape
    row = lax.broadcasted_iota(jnp.int32, values.shape, 1)
    return jnp.where(row < frame_len, values, 0.0).reshape(count * pad, width)


def project_kernel(frame_len, x_ref, gain_ref, w_ref, proj_ref):
    normed, _ = normalize(load_rows(x_ref, frame_len))
    hidden = (normed * gain_ref[...]).astype(BFLOAT)
    width = hidden.shape[1]
    for part in range(3):
        cols = slice(part * width, (part + 1) * width)
        proj_ref[:, cols] = dot(hidden, w_ref[:, cols]).astype(BFLOAT)


def alias_call(
    kernel, grid, in_specs, args, prior, out_specs, out_shape, name, flops, moved, scratch=()
):
    extra = [] if prior is None else list(prior)

    def body(*refs):
        kernel(*refs[: len(args)], *refs[len(args) + len(extra) :])

    return pl.pallas_call(
        body,
        grid=grid,
        in_specs=in_specs + [pl.BlockSpec(memory_space=pl.ANY)] * len(extra),
        out_specs=out_specs,
        out_shape=out_shape,
        input_output_aliases={len(args) + i: i for i in range(len(extra))},
        scratch_shapes=list(scratch),
        compiler_params=params(),
        cost_estimate=cost(flops, moved),
        name=name,
    )(*args, *extra)


def project(frames_in, gain, qkv, first, steps, prior):
    count, frame_len, width = frames_in.shape
    pad = padded_len(frame_len)
    block = GROUP * pad
    return alias_call(
        functools.partial(project_kernel, frame_len),
        (steps,),
        [frames_of(pad, width, first), whole((width,)), whole(qkv.shape)],
        (frames_in, gain, qkv),
        prior,
        [rows_of(block, 3 * width, first)],
        [jax.ShapeDtypeStruct((count * pad, 3 * width), BFLOAT)],
        "project",
        6 * steps * block * width * width,
        8 * steps * block * width,
    )


def last_rows(rows, change):
    cut = rows.shape[0] - 8
    return jnp.concatenate([rows[:cut], change(rows[cut:], cut)], axis=0)


def token_in(rows, token, frame_len):
    def change(tail, cut):
        row = lax.broadcasted_iota(jnp.int32, tail.shape, 0)
        return jnp.where(row == frame_len - cut, token, tail)

    return last_rows(rows, change)


def one_head(pair, h):
    lane = lax.broadcasted_iota(jnp.int32, pair.shape, 1)
    return jnp.where((lane >= HD) == (h == 1), pair, jnp.zeros_like(pair))


def attend_kernel(
    frame_len, x_ref, proj_ref, token_ref, out_w_ref, expo_ref, mixed_ref, scale_ref, res_ref
):
    width = x_ref.shape[2]
    pad = x_ref.shape[1]
    pairs = width // PAIR

    def hide(tail, cut):
        row = lax.broadcasted_iota(jnp.int32, tail.shape, 0)
        return jnp.where(row <= frame_len - cut, tail, NEG)

    def at(part, j):
        return pl.ds(part * width + j * PAIR, PAIR)

    def weigh(f, j):
        rows = pl.ds(f * pad, pad)
        query = proj_ref[rows, at(0, j)] * 0.125
        key = token_in(proj_ref[rows, at(1, j)], token_ref[f, :, at(0, j)], frame_len)
        for h in range(2):
            scores = last_rows(dot_nt(one_head(key, h), query), hide)
            expo = jnp.exp(scores - jnp.max(scores, axis=0, keepdims=True)).astype(BFLOAT)
            expo_ref[f, 2 * j + h] = expo

    def mix(f, j):
        rows = pl.ds(f * pad, pad)
        value = token_in(proj_ref[rows, at(2, j)], token_ref[f, :, at(1, j)], frame_len)
        value_t = value.astype(FLOAT).T.astype(BFLOAT)
        outs = []
        for h in range(2):
            ones = jnp.ones((8, pad), BFLOAT)
            out = dot(jnp.concatenate([value_t[h * HD : (h + 1) * HD], ones]), expo_ref[f, 2 * j + h])
            scale = 1.0 / out[HD : HD + 1]
            outs.append(out[:HD] * scale)
            scale_ref[f, 2 * j + h : 2 * j + h + 1, :] = scale
        mixed_ref[rows, at(0, j)] = jnp.concatenate(outs, axis=0).T.astype(BFLOAT)

    units = [(f, j) for j in range(pairs) for f in range(GROUP)]
    for i in range(len(units) + 2):
        if i < len(units):
            weigh(*units[i])
        if i >= 2:
            mix(*units[i - 2])
    residual = load_rows(x_ref, frame_len) + dot(mixed_ref[...], out_w_ref[...])
    res_ref[...] = residual.astype(BFLOAT)


def attend(frames_in, proj, token_kv, out_w):
    count, frame_len, width = frames_in.shape
    pad = padded_len(frame_len)
    block = GROUP * pad
    heads = width // HD
    return pl.pallas_call(
        functools.partial(attend_kernel, frame_len),
        grid=(count // GROUP,),
        in_specs=[
            frames_of(pad, width),
            rows_of(block, 3 * width),
            frames_of(1, 2 * width),
            whole(out_w.shape),
        ],
        out_specs=[
            pl.BlockSpec((GROUP, heads, pad, pad), lambda i: (i, 0, 0, 0)),
            rows_of(block, width),
            frames_of(heads, pad),
            rows_of(block, width),
        ],
        out_shape=[
            jax.ShapeDtypeStruct((count, heads, pad, pad), BFLOAT),
            jax.ShapeDtypeStruct((count * pad, width), BFLOAT),
            jax.ShapeDtypeStruct((count, heads, pad), FLOAT),
            jax.ShapeDtypeStruct((count * pad, width), BFLOAT),
        ],
        compiler_params=params(),
        cost_estimate=cost(25e9, 50e6),
        name="attend",
    )(frames_in, proj, token_kv, out_w)


def mlp_kernel(
    frame_len,
    parts,
    res_ref,
    cot_ref,
    gain_ref,
    up_ref,
    down_ref,
    out_w_ref,
    mixed_ref,
    scale_ref,
    cot_rows_ref,
    second_ref,
    act_ref,
    grad_up_ref,
    branch_ref,
    grad_mixed_ref,
    delta_ref,
    gain_grad_ref,
):
    residual = res_ref[...].astype(FLOAT)
    width = residual.shape[1]
    normed, scale_inv = normalize(residual)
    gain = gain_ref[...]
    second = (normed * gain).astype(BFLOAT)
    second_ref[...] = second
    cot = load_rows(cot_ref, frame_len)
    cot_bf = cot.astype(BFLOAT)
    cot_rows_ref[...] = cot_bf
    grad_second = jnp.zeros_like(residual)
    size = up_ref.shape[1] // parts
    for part in range(parts):
        cols = slice(part * size, (part + 1) * size)
        up_part = dot(second, up_ref[:, cols])
        sigma = 0.5 * jnp.tanh(0.851 * up_part) + 0.5
        gated = up_part * sigma
        act = gated.astype(BFLOAT)
        act_ref[:, cols] = act
        grad_act = dot_nt(cot_bf, down_ref[cols, :])
        grad_up = (grad_act * (sigma + 1.702 * gated * (1.0 - sigma))).astype(BFLOAT)
        grad_up_ref[:, cols] = grad_up
        grad_second = grad_second + dot_nt(grad_up, up_ref[:, cols])
    gain_grad = jnp.sum(grad_second * normed, axis=0, keepdims=True)
    step = pl.program_id(0)
    gain_grad_ref[...] = jnp.where(step == 0, 0.0, gain_grad_ref[...]) + gain_grad
    branch = (cot + norm_back(grad_second * gain, normed, scale_inv)).astype(BFLOAT)
    branch_ref[...] = branch
    heads, pad = delta_ref.shape[1:]
    head = lax.broadcasted_iota(jnp.int32, (heads, width), 0)
    lane = lax.broadcasted_iota(jnp.int32, (heads, width), 1)
    of_head = (lane // HD == head).astype(FLOAT)
    scales = []
    for f in range(GROUP):
        high = scale_ref[f].astype(BFLOAT).astype(FLOAT)
        rows = jnp.concatenate([high, scale_ref[f] - high]).astype(BFLOAT)
        scales.append(dot_tn(rows, jnp.concatenate([of_head, of_head]).astype(BFLOAT)))
    of_head = of_head.astype(BFLOAT)
    grad_mixed = dot_nt(branch, out_w_ref[...]) * jnp.concatenate(scales)
    grad_mixed = grad_mixed.astype(BFLOAT)
    grad_mixed_ref[...] = grad_mixed
    product = grad_mixed * mixed_ref[...]
    for f in range(GROUP):
        delta_ref[f] = dot_nt(of_head, product[f * pad : (f + 1) * pad])


def mlp(residual, cotangent, gain, up, down, out_w, mixed, scale):
    count, frame_len, width = cotangent.shape
    pad = padded_len(frame_len)
    block = GROUP * pad
    rows = count * pad
    heads = width // HD
    hidden = up.shape[1]
    shape = jax.ShapeDtypeStruct
    return pl.pallas_call(
        functools.partial(mlp_kernel, frame_len, 4),
        grid=(count // GROUP,),
        in_specs=[
            rows_of(block, width),
            frames_of(pad, width),
            whole((width,)),
            whole(up.shape),
            whole(down.shape),
            whole(out_w.shape),
            rows_of(block, width),
            frames_of(heads, pad),
        ],
        out_specs=[
            rows_of(block, width),
            rows_of(block, width),
            rows_of(block, hidden),
            rows_of(block, hidden),
            rows_of(block, width),
            rows_of(block, width),
            pl.BlockSpec((GROUP, heads, pad), lambda i: (i, 0, 0)),
            pl.BlockSpec((1, width), lambda i: (0, 0)),
        ],
        out_shape=[
            shape((rows, width), BFLOAT),
            shape((rows, width), BFLOAT),
            shape((rows, hidden), BFLOAT),
            shape((rows, hidden), BFLOAT),
            shape((rows, width), BFLOAT),
            shape((rows, width), BFLOAT),
            shape((count, heads, pad), FLOAT),
            shape((1, width), FLOAT),
        ],
        compiler_params=params(),
        cost_estimate=cost(6 * rows * width * hidden, 60e6),
        name="mlp",
    )(residual, cotangent, gain, up, down, out_w, mixed, scale)


def output_kernel(res_ref, act_ref, down_ref, output_ref):
    out = res_ref[...].astype(FLOAT) + dot(act_ref[...], down_ref[...])
    output_ref[...] = out.astype(BFLOAT).reshape(output_ref.shape)


def mlp_output(residual, act, down, shape, first, steps, prior):
    count, frame_len, width = shape
    pad = padded_len(frame_len)
    block = GROUP * pad
    hidden = down.shape[0]
    return alias_call(
        output_kernel,
        (steps,),
        [rows_of(block, width, first), rows_of(block, hidden, first), whole(down.shape)],
        (residual, act, down),
        prior,
        [frames_of(pad, width, first)],
        [jax.ShapeDtypeStruct(shape, BFLOAT)],
        "mlp_output",
        2 * steps * block * width * hidden,
        8 * steps * block * width,
    )


def weight_grad_kernel(core_ref, left_ref, right_ref, *refs):
    send_ref, keep_ref = refs[-2:]
    total = dot_tn(left_ref[...], right_ref[...]).astype(BFLOAT)
    step = pl.program_id(0)

    @pl.when(step < 2)
    def _():
        send_ref[0] = total

    @pl.when(step >= 2)
    def _():
        keep_ref[0] = total


def up_grad(core, left, right, parts, prior):
    rows, width = left.shape
    lanes = right.shape[1] // parts

    def block(i, core_ref):
        return 2 * (i % 2) + jnp.where(i < 2, 1 - core_ref[0], core_ref[0])

    return pl.pallas_call(
        weight_grad_kernel,
        grid_spec=pltpu.PrefetchScalarGridSpec(
            num_scalar_prefetch=1,
            grid=(parts,),
            in_specs=[
                pl.BlockSpec(left.shape, lambda i, c: (0, 0), pipeline_mode=pl.Buffered(1)),
                pl.BlockSpec((rows, lanes), lambda i, c: (0, block(i, c))),
                pl.BlockSpec(memory_space=pl.ANY),
                pl.BlockSpec(memory_space=pl.ANY),
            ],
            out_specs=[
                pl.BlockSpec((1, width, lanes), lambda i, c: (jnp.minimum(i, 1), 0, 0)),
                pl.BlockSpec((1, width, lanes), lambda i, c: (jnp.maximum(i - 2, 0), 0, 0)),
            ],
        ),
        out_shape=[jax.ShapeDtypeStruct(p.shape, BFLOAT) for p in prior],
        input_output_aliases={3: 0, 4: 1},
        compiler_params=params(),
        cost_estimate=cost(2 * left.size * right.shape[1], 2 * (left.size + right.size)),
        name="grad_up",
    )(core, left, right, *prior)


def by_core(core, blocks):
    pairs = [(blocks[2 * y], blocks[2 * y + 1]) for y in range(len(blocks) // 2)]
    first = core == 0
    send = [jnp.where(first, odd, even) for even, odd in pairs]
    return send, [jnp.where(first, even, odd) for even, odd in pairs]


def down_grad_kernel(core_ref, left_ref, right_ref, send_ref, keep_ref):
    total = dot_tn(left_ref[...], right_ref[...]).astype(BFLOAT)
    parts, pieces, height, columns = 2 * send_ref.shape[0], *send_ref.shape[1:]
    for piece in range(pieces):
        cols = slice(piece * columns, (piece + 1) * columns)
        blocks = [total[part * height : (part + 1) * height, cols] for part in range(parts)]
        for ref, values in zip((send_ref, keep_ref), by_core(core_ref[0], blocks)):
            for y, value in enumerate(values):
                ref[y, piece] = value


def down_grad(core, left, right, parts, tile):
    rows, width = left.shape
    tiles = right.shape[1] // tile
    shape = (parts // 2, tiles, width // parts, tile)
    spec = pl.BlockSpec((parts // 2, 2, width // parts, tile), lambda i: (0, i, 0, 0))
    return pl.pallas_call(
        down_grad_kernel,
        grid=(tiles // 2,),
        in_specs=[
            pl.BlockSpec(memory_space=pltpu.SMEM),
            whole(left.shape),
            pl.BlockSpec((rows, 2 * tile), lambda i: (0, i)),
        ],
        out_specs=[spec, spec],
        out_shape=[jax.ShapeDtypeStruct(shape, BFLOAT)] * 2,
        compiler_params=params(),
        cost_estimate=cost(2 * left.size * right.shape[1], 2 * (left.size + right.size)),
        name="grad_down",
    )(core, left, right)


def with_gain(block, gain, lanes):
    column = jnp.broadcast_to(gain, (8, gain.shape[1])).T.astype(BFLOAT)
    blank = jnp.zeros((block.shape[0], lanes - block.shape[1] - 8), BFLOAT)
    return jnp.concatenate([block, column, blank], axis=1)


def store_split(core, total_ref, gain, send_refs, keep_refs):
    halves = send_refs[0].shape[0]
    parts = 2 * halves
    size = total_ref.shape[1] // parts
    lanes = sum(ref.shape[2] for ref in send_refs)
    for y in range(halves):
        blocks = [
            with_gain(total_ref[:, part * size : (part + 1) * size].astype(BFLOAT), gain, lanes)
            for part in (2 * y, 2 * y + 1)
        ]
        for refs, (value,) in zip((send_refs, keep_refs), by_core(core, blocks)):
            offset = 0
            for ref in refs:
                ref[y] = value[:, offset : offset + ref.shape[2]]
                offset += ref.shape[2]


def split_grad_kernel(core_ref, left_ref, right_ref, gain_ref, send_ref, keep_ref, all_ref):
    step = pl.program_id(0)
    tile = right_ref.shape[1]
    all_ref[:, pl.ds(pl.multiple_of(step * tile, tile), tile)] = dot_tn(
        left_ref[...], right_ref[...]
    ).astype(BFLOAT)

    @pl.when(step == pl.num_programs(0) - 1)
    def _():
        store_split(core_ref[0], all_ref, gain_ref[...], [send_ref], [keep_ref])


def split_grad(core, left, right, gain, tile, parts, shape, index, name):
    rows, width = left.shape
    columns = right.shape[1]
    size = -(-columns // parts // LANES) * LANES
    spec = pl.BlockSpec((parts // 2, width, size), lambda i: (0, 0, index))
    return pl.pallas_call(
        split_grad_kernel,
        grid=(columns // tile,),
        in_specs=[
            pl.BlockSpec(memory_space=pltpu.SMEM),
            whole(left.shape),
            pl.BlockSpec((rows, tile), lambda i: (0, i)),
            whole(gain.shape),
        ],
        out_specs=[spec, spec],
        out_shape=[jax.ShapeDtypeStruct(shape, BFLOAT)] * 2,
        scratch_shapes=[pltpu.VMEM((width, columns), BFLOAT)],
        compiler_params=params(),
        cost_estimate=cost(2 * left.size * columns, 2 * (left.size + right.size)),
        name=name,
    )(core, left, right, gain)


def attend_back_kernel(
    frame_len,
    core_ref,
    proj_ref,
    token_ref,
    expo_ref,
    grad_mixed_ref,
    delta_ref,
    x_ref,
    branch_ref,
    message_ref,
    gain_ref,
    w_ref,
    grad_in_ref,
    class_ref,
    message_grad_ref,
    send_0_ref,
    send_1_ref,
    keep_0_ref,
    keep_1_ref,
    scores_ref,
    grad_proj_ref,
    total_ref,
    gain_grad_ref,
):
    pad = expo_ref.shape[2]
    width = grad_mixed_ref.shape[1]
    pairs = width // PAIR
    step = pl.program_id(0)

    @pl.when(step == 0)
    def _():
        total_ref[...] = jnp.zeros_like(total_ref)
        gain_grad_ref[...] = jnp.zeros_like(gain_grad_ref)

    def at(part, j):
        return pl.ds(part * width + j * PAIR, PAIR)

    def weigh(f, j):
        rows = pl.ds(f * pad, pad)
        value = token_in(proj_ref[rows, at(2, j)], token_ref[f, :, at(1, j)], frame_len)
        grad = grad_mixed_ref[rows, at(0, j)]
        for h in range(2):
            head = 2 * j + h
            grad_prob = dot_nt(one_head(value, h), grad) - delta_ref[f, head : head + 1, :]
            scores_ref[f, head] = expo_ref[f, head] * grad_prob.astype(BFLOAT)

    def mix(f, j):
        rows = pl.ds(f * pad, pad)
        query = proj_ref[rows, at(0, j)]
        key = token_in(proj_ref[rows, at(1, j)], token_ref[f, :, at(0, j)], frame_len)
        grad = grad_mixed_ref[rows, at(0, j)]
        key_t = key.astype(FLOAT).T.astype(BFLOAT)
        grad_query, grad_key, grad_value = [], [], []
        for h in range(2):
            scores = scores_ref[f, 2 * j + h]
            grad_value.append(dot(expo_ref[f, 2 * j + h], one_head(grad, h)))
            grad_key.append(dot(scores, one_head(query, h)))
            grad_query.append(dot(key_t[h * HD : (h + 1) * HD], scores))
        grad_query = jnp.concatenate(grad_query, axis=0).T * 0.125
        grad_proj_ref[rows, at(0, j)] = grad_query.astype(BFLOAT)
        grad_key = (grad_key[0] + grad_key[1]) * 0.125
        grad_proj_ref[rows, at(1, j)] = grad_key.astype(BFLOAT)
        grad_value = grad_value[0] + grad_value[1]
        grad_proj_ref[rows, at(2, j)] = grad_value.astype(BFLOAT)

    units = [(f, j) for j in range(pairs) for f in range(GROUP)]
    for i in range(len(units) + 2):
        if i < len(units):
            weigh(*units[i])
        if i >= 2:
            mix(*units[i - 2])

    values = load_rows(x_ref, frame_len)
    values = jnp.concatenate(
        [
            token_in(values[f * pad : (f + 1) * pad], message_ref[f].astype(FLOAT), frame_len)
            for f in range(GROUP)
        ]
    )
    normed, scale_inv = normalize(values)
    hidden = (normed * gain_ref[...]).astype(BFLOAT)
    for part in range(3):
        cols = slice(part * width, (part + 1) * width)
        total_ref[:, cols] += dot_tn(hidden, grad_proj_ref[:, cols])
    grad = dot_nt(grad_proj_ref[...], w_ref[...])
    gain_grad_ref[...] += jnp.sum(grad * normed, axis=0, keepdims=True)
    total = branch_ref[...].astype(FLOAT) + norm_back(grad * gain_ref[...], normed, scale_inv)
    total = total.reshape(GROUP, pad, width)
    grad_in_ref[...] = total.astype(BFLOAT)
    for f in range(GROUP):
        class_ref[f] = total[f, :1]
        message_grad_ref[f] = total[f, frame_len : frame_len + 1].astype(BFLOAT)

    @pl.when(step == pl.num_programs(0) - 1)
    def _():
        store_split(
            core_ref[0],
            total_ref,
            gain_grad_ref[...],
            [send_0_ref, send_1_ref],
            [keep_0_ref, keep_1_ref],
        )


def attend_back(
    core, proj, token_kv, expo, grad_mixed, delta, frames_in, branch, message, gain, qkv, parts
):
    count, heads, pad, _ = expo.shape
    frame_len, width = frames_in.shape[1:]
    block = GROUP * pad
    lanes = -(-3 * width // parts // LANES) * LANES
    first = lanes // (2 * LANES) * LANES + LANES
    sums = [(parts // 2, width, n) for n in (first, lanes - first)] * 2
    shape = jax.ShapeDtypeStruct
    return pl.pallas_call(
        functools.partial(attend_back_kernel, frame_len),
        grid=(count // GROUP,),
        in_specs=[
            pl.BlockSpec(memory_space=pltpu.SMEM),
            rows_of(block, 3 * width),
            frames_of(1, 2 * width),
            pl.BlockSpec((GROUP, heads, pad, pad), lambda i: (i, 0, 0, 0)),
            rows_of(block, width),
            pl.BlockSpec((GROUP, heads, pad), lambda i: (i, 0, 0)),
            frames_of(pad, width),
            rows_of(block, width),
            frames_of(1, width),
            whole((width,)),
            whole(qkv.shape),
        ],
        out_specs=[frames_of(pad, width), frames_of(1, width), frames_of(1, width)]
        + [whole(s) for s in sums],
        out_shape=[
            shape((count, frame_len, width), BFLOAT),
            shape((count, 1, width), FLOAT),
            shape((count, 1, width), BFLOAT),
        ]
        + [shape(s, BFLOAT) for s in sums],
        scratch_shapes=[
            pltpu.VMEM((GROUP, heads, pad, pad), BFLOAT),
            pltpu.VMEM((block, 3 * width), BFLOAT),
            pltpu.VMEM((width, 3 * width), FLOAT),
            pltpu.VMEM((1, width), FLOAT),
        ],
        compiler_params=params(),
        cost_estimate=cost(45e9, 50e6),
        name="attend_back",
    )(core, proj, token_kv, expo, grad_mixed, delta, frames_in, branch, message, gain, qkv)


def in_turn(count, slots, first, second):
    if slots > 256:

        def both(j, carry):
            first(j)
            second(j)
            return carry

        lax.fori_loop(0, count, both, 0)
        return
    for j in range(count + 2):
        if j < count:
            first(j)
        if j >= 2:
            second(j - 2)


def message_kernel(
    own,
    pieces,
    *refs,
):
    gathered = jnp.concatenate([ref[...] for ref in refs[:pieces]])
    message_body(own, gathered, *refs[pieces:])


def message_body(
    own,
    gathered,
    weight_ref,
    gain_ref,
    qkv_ref,
    out_w_ref,
    attn_gain_ref,
    key_w_ref,
    value_w_ref,
    class_ref,
    start_ref,
    hidden_ref,
    proj_ref,
    prob_ref,
    mixed_ref,
    message_ref,
    token_kv_ref,
):
    width = weight_ref.shape[0]
    class_ref[...] = gathered[:, :width]
    start = dot(gathered[:, :width], weight_ref[...]).astype(BFLOAT)
    start_ref[...] = start
    normed, _ = normalize(start.astype(FLOAT))
    hidden = (normed * gain_ref[...]).astype(BFLOAT)
    hidden_ref[...] = hidden
    proj_ref[...] = dot(hidden, qkv_ref[...]).astype(BFLOAT)
    digits = gathered[:, width:].astype(FLOAT)
    lane = lax.broadcasted_iota(jnp.int32, digits.shape, 1)
    weights = jnp.where(lane == 0, 1.0, jnp.where(lane == 1, BASE, BASE * BASE))
    digits = jnp.where(lane < DIGITS, digits * weights, 0.0)
    id_col = jnp.sum(digits, axis=1, keepdims=True)
    id_row = jnp.sum(digits.T, axis=0, keepdims=True)
    visible = id_col == id_row

    def at(part, j):
        start = part * width + j * PAIR
        return pl.ds(start if isinstance(j, int) else pl.multiple_of(start, PAIR), PAIR)

    def weigh(j):
        query = proj_ref[:, at(0, j)] * 0.125
        for h in range(2):
            scores = jnp.where(visible, dot_nt(proj_ref[:, at(1, j)], one_head(query, h)), NEG)
            expo = jnp.exp(scores - jnp.max(scores, axis=0, keepdims=True))
            prob = expo * (1.0 / jnp.sum(expo, axis=0, keepdims=True))
            prob_ref[2 * j + h] = prob.astype(BFLOAT)

    def mix(j):
        value_t = proj_ref[:, at(2, j)].astype(FLOAT).T.astype(BFLOAT)
        outs = [dot(value_t[h * HD : (h + 1) * HD], prob_ref[2 * j + h]) for h in range(2)]
        mixed_ref[:, at(0, j)] = jnp.concatenate(outs, axis=0).T.astype(BFLOAT)

    in_turn(width // PAIR, start.shape[0], weigh, mix)
    message = start[:own].astype(FLOAT) + dot(mixed_ref[:own, :], out_w_ref[...])
    message = message.astype(BFLOAT)
    message_ref[...] = message
    normed, _ = normalize(message.astype(FLOAT))
    token_hidden = (normed * attn_gain_ref[...]).astype(BFLOAT)
    token_kv_ref[:, :width] = dot(token_hidden, key_w_ref[...]).astype(BFLOAT)
    token_kv_ref[:, width:] = dot(token_hidden, value_w_ref[...]).astype(BFLOAT)


def message_forward(class_parts, own, weight, gain, qkv, out_w, attn_gain, attn_qkv):
    slots = sum(part.shape[0] for part in class_parts)
    width = weight.shape[0]
    heads = width // HD
    shape = jax.ShapeDtypeStruct
    part = lambda index: pl.BlockSpec((width, width), lambda i, index=index: (0, index))
    return pl.pallas_call(
        functools.partial(message_kernel, own, len(class_parts)),
        grid=(1,),
        in_specs=[whole(p.shape) for p in class_parts]
        + [
            whole(weight.shape),
            whole((width,)),
            whole(qkv.shape),
            whole(out_w.shape),
            whole((width,)),
            part(1),
            part(2),
        ],
        out_specs=[
            whole((slots, width)),
            whole((slots, width)),
            whole((slots, width)),
            whole((slots, 3 * width)),
            whole((heads, slots, slots)),
            whole((slots, width)),
            whole((own, width)),
            whole((own, 2 * width)),
        ],
        out_shape=[
            shape((slots, width), BFLOAT),
            shape((slots, width), BFLOAT),
            shape((slots, width), BFLOAT),
            shape((slots, 3 * width), BFLOAT),
            shape((heads, slots, slots), BFLOAT),
            shape((slots, width), BFLOAT),
            shape((own, width), BFLOAT),
            shape((own, 2 * width), BFLOAT),
        ],
        compiler_params=params(),
        cost_estimate=cost(7e9, 9e6),
        name="message_forward",
    )(
        *class_parts,
        weight,
        gain,
        qkv,
        out_w,
        attn_gain,
        attn_qkv,
        attn_qkv,
    )


def message_back_kernel(
    own,
    parts,
    together,
    pieces,
    block_ref,
    *refs,
):
    grad = jnp.concatenate([ref[...] for ref in refs[:pieces]])
    message_back_body(own, parts, together, block_ref, grad, *refs[pieces:])


def message_back_body(
    own,
    parts,
    together,
    block_ref,
    grad,
    class_ref,
    start_ref,
    hidden_ref,
    proj_ref,
    prob_ref,
    mixed_ref,
    weight_ref,
    gain_ref,
    qkv_ref,
    out_w_ref,
    class_grad_ref,
    sums_ref,
    grad_mixed_ref,
    grad_proj_ref,
    scores_ref,
):
    width = weight_ref.shape[0]
    j = pl.program_id(0)

    @pl.when(j == 0)
    def _():
        grad_mixed_ref[...] = dot_nt(grad, out_w_ref[...]).astype(BFLOAT)

    def finish():
        grad_proj = grad_proj_ref[...]
        grad_hidden = dot_nt(grad_proj, qkv_ref[...])
        normed, scale_inv = normalize(start_ref[...].astype(FLOAT))
        gain_grad = jnp.sum(grad_hidden * normed, axis=0, keepdims=True)
        back = norm_back(grad_hidden * gain_ref[...], normed, scale_inv)
        start_grad = (grad.astype(FLOAT) + back).astype(BFLOAT)
        class_grad_ref[...] = dot_nt(start_grad[:own], weight_ref[...])
        size = sums_ref.shape[1]
        row = lax.broadcasted_iota(jnp.int32, (size, width), 0)
        column = lax.broadcasted_iota(jnp.int32, (size, width), 1)
        mine = column == row + block_ref[0] * size
        pick = mine.astype(BFLOAT)
        gain_grad = jnp.sum(jnp.where(mine, gain_grad, 0.0), axis=1, keepdims=True)
        lanes = sums_ref.shape[2] - 5 * width // parts
        for part in range(parts):
            sums_ref[part, :, 5 * width // parts :] = jnp.broadcast_to(
                gain_grad, (size, lanes)
            ).astype(BFLOAT)
        offset = 0
        for left, right in (
            (hidden_ref[...], grad_proj),
            (class_ref[:, :width], start_grad),
            (mixed_ref[...], grad),
        ):
            total = dot(dot_nt(pick, left).astype(BFLOAT), right).astype(BFLOAT)
            columns = total.shape[1] // parts
            for part in range(parts):
                sums_ref[part, :, offset : offset + columns] = total[
                    :, part * columns : (part + 1) * columns
                ]
            offset += columns

    def at(part, k):
        if together == 1:
            return pl.ds(pl.multiple_of(part * width + j * PAIR, PAIR), PAIR)
        return pl.ds(part * width + k * PAIR, PAIR)

    def weigh(k):
        value = proj_ref[:, at(2, k)]
        for h in range(2):
            grad_prob = dot_nt(value, one_head(grad_mixed_ref[:, at(0, k)], h))
            prob = prob_ref[2 * k + h].astype(FLOAT)
            part = prob * grad_prob
            scores = part - prob * jnp.sum(part, axis=0, keepdims=True)
            scores_ref[2 * k + h] = scores.astype(BFLOAT)

    def mix(k):
        query, key, grad_m = proj_ref[:, at(0, k)], proj_ref[:, at(1, k)], grad_mixed_ref[:, at(0, k)]
        key_t = key.astype(FLOAT).T.astype(BFLOAT)
        grad_query, grad_key, grad_value = [], [], []
        for h in range(2):
            scores = scores_ref[2 * k + h]
            grad_value.append(dot(prob_ref[2 * k + h], one_head(grad_m, h)))
            grad_key.append(dot(scores, one_head(query, h)))
            grad_query.append(dot(key_t[h * HD : (h + 1) * HD], scores))
        grad_query = jnp.concatenate(grad_query, axis=0).T * 0.125
        grad_proj_ref[:, at(0, k)] = grad_query.astype(BFLOAT)
        grad_proj_ref[:, at(1, k)] = ((grad_key[0] + grad_key[1]) * 0.125).astype(BFLOAT)
        grad_proj_ref[:, at(2, k)] = (grad_value[0] + grad_value[1]).astype(BFLOAT)

    if together == 1:
        weigh(0)
        mix(0)
    else:
        in_turn(together, grad.shape[0], weigh, mix)

    @pl.when(j == pl.num_programs(0) - 1)
    def _():
        finish()


def message_back(block, parts, size, own, grad_parts, saved, weight, gain, qkv, out_w):
    class_all, start, hidden, proj, prob, mixed = saved
    slots, width = class_all.shape
    shape = jax.ShapeDtypeStruct
    sums = (parts, size, -(-(5 * width // parts + 1) // LANES) * LANES)
    together = width // PAIR if slots <= 256 else 1
    args = (*grad_parts, class_all, start, hidden, proj, prob, mixed, weight, gain, qkv, out_w)
    return pl.pallas_call(
        functools.partial(message_back_kernel, own, parts, together, len(grad_parts)),
        grid=(width // PAIR // together,),
        in_specs=[pl.BlockSpec(memory_space=pltpu.SMEM)]
        + [pl.BlockSpec((2 * together, slots, slots), lambda j: (j, 0, 0)) if a is prob else whole(a.shape) for a in args],
        out_specs=[whole((own, width)), whole(sums)],
        out_shape=[shape((own, width), FLOAT), shape(sums, BFLOAT)],
        scratch_shapes=[
            pltpu.VMEM((slots, width), BFLOAT),
            pltpu.VMEM((slots, 3 * width), BFLOAT),
            pltpu.VMEM((2 * together, slots, slots), BFLOAT),
        ],
        compiler_params=params(),
        cost_estimate=cost(8e9, 9e6),
        name="message_back",
    )(block, *args)


def swap(values, axis, distance):
    return lax.ppermute(values, axis, [(i, i ^ distance) for i in range(lax.axis_size(axis))])


def tied(values, *others):
    return lax.optimization_barrier((values, others))[0]


def meet(outputs, *transfers):
    outputs, got = lax.optimization_barrier((outputs, [transfer.got for transfer in transfers]))
    for transfer, values in zip(transfers, got):
        transfer.got = values
    return outputs


def pick(values, index, axis=0, window=None):
    starts, sizes = [0] * values.ndim, list(values.shape)
    starts[axis], sizes[axis] = index, 1
    if window is not None:
        starts[window[0]], sizes[window[0]] = window[1:]
    return lax.squeeze(lax.dynamic_slice(values, starts, sizes), (axis,))


def add(*terms):
    total = terms[0].astype(FLOAT)
    for term in terms[1:]:
        total = total + term.astype(FLOAT)
    return total


class Gather:
    def __init__(self, axis, values):
        self.axis, self.values = axis, values
        self.distance, self.left = 1, lax.axis_size(axis)

    def begin(self, direct=True):
        while self.left > 8:
            self.finish(self.start(2))
        self.got = self.start(self.left if direct and self.left < 8 else 2)

    def start(self, size):
        got = [swap(self.values, self.axis, d * self.distance) for d in range(1, size)]
        self.distance, self.left = self.distance * size, self.left // size
        return got

    def finish(self, got):
        self.pieces = [self.values, *got]
        self.values = jnp.concatenate(self.pieces)

    def end(self):
        self.finish(self.got)
        return self.values


class Sum:
    def __init__(self, terms):
        self.terms = terms

    @classmethod
    def of_cores(cls, sent, kept):
        self = cls([kept])
        self.sent = sent
        self.got = [swap(sent, "rows", 1)]
        return self

    def part(self, index):
        return Sum([term[index] for term in self.terms])

    def total(self):
        return add(*self.terms)

    def begin(self, axis, distance, dim, window=None):
        bit = (lax.axis_index(axis) // distance) % 2
        sent = add(*(pick(term, 1 - bit, dim, window) for term in self.terms)).astype(BFLOAT)
        self.terms = [pick(term, bit, dim, window) for term in self.terms]
        self.got = [swap(sent, axis, distance)]
        return sent

    def end(self, apart=False):
        self.terms = self.got + self.terms
        if not apart:
            self.terms = [self.total().astype(BFLOAT)]

    def begin_frames(self, dim=0):
        self.left, self.distance, self.dim = lax.axis_size("frames"), 1, dim
        shape = self.terms[0].shape
        if len(shape) == 2 + dim:
            shape = (*shape[:dim], self.left, -1, shape[-1])
            self.terms = [term.reshape(shape) for term in self.terms]
        while self.left > 8:
            self.step_frames()
            self.end()
        return self.step_frames()

    def step_frames(self):
        shape, dim = self.terms[0].shape, self.dim
        shape = (*shape[:dim], self.left // 2, 2, *shape[dim + 1 :])
        self.terms = [term.reshape(shape) for term in self.terms]
        sent = self.begin("frames", self.distance, dim + 1)
        self.left, self.distance = self.left // 2, self.distance * 2
        return sent

    def begin_last(self):
        index = lax.axis_index("frames") // self.distance
        sent = [
            add(*(pick(term, index ^ d) for term in self.terms)).astype(BFLOAT)
            for d in range(1, self.left)
        ]
        self.terms = [pick(term, index) for term in self.terms]
        self.got = [
            swap(block, "frames", (d + 1) * self.distance) for d, block in enumerate(sent)
        ]
        return sent


def joined(first, second, axis):
    self = Sum([jnp.concatenate([first.total(), second.total()], axis=axis).astype(BFLOAT)])
    if hasattr(first, "left"):
        self.left, self.distance, self.dim = first.left, first.distance, first.dim
    return self


def per_device(
    frames_in,
    cotangent,
    video_ids,
    frame_device,
    msg_weight,
    msg_gain,
    msg_qkv,
    msg_out,
    attn_gain,
    attn_qkv,
    attn_out,
    mlp_gain,
    up_weight,
    down_weight,
):
    count, frame_len, width = frames_in.shape
    owners, parts = lax.axis_size("frames"), lax.axis_size("rows")
    hidden_width = up_weight.shape[1]
    own = -(-count // 16) * 16
    steps = count // GROUP
    block_index = lax.axis_index("frames").astype(jnp.int32).reshape(1)
    extra = ((0, own - count), (0, 0))

    ids = (video_ids * owners + frame_device)[:, None]
    base = int(BASE)
    digits = jnp.concatenate([ids % base, ids // base % base, ids // (base * base)], axis=1)
    digits = jnp.pad(digits, ((0, own - count), (0, LANES - DIGITS)), constant_values=-1)
    payload = jnp.concatenate([jnp.pad(frames_in[:, 0, :], extra), digits.astype(BFLOAT)], axis=1)
    gather = Gather("frames", payload)
    gather.begin()
    frames = tied(frames_in, payload)
    early = steps // 2
    projected = meet(project(frames, attn_gain, attn_qkv, 0, early, None), gather)
    gather.end()
    gather.begin()
    (proj,) = project(
        tied(frames, gather.values), attn_gain, attn_qkv, early, steps - early, projected
    )
    proj = meet(proj, gather)
    gather.end()

    *saved, message, token_kv = message_forward(
        gather.pieces, own, msg_weight, msg_gain, msg_qkv, msg_out, attn_gain, attn_qkv
    )
    token_kv = token_kv[:count, None]
    message = message[:count, None]
    expo, mixed, scale, residual = attend(frames_in, proj, token_kv, attn_out)
    cot, second, act, grad_up, branch, grad_mixed, delta, mlp_gain_grad = mlp(
        residual, cotangent, mlp_gain, up_weight, down_weight, attn_out, mixed, scale
    )

    core = (lax.axis_index("rows") % 2).astype(jnp.int32).reshape(1)
    tile = 3 * LANES
    tiles = hidden_width // tile
    down = Sum.of_cores(*down_grad(core, cot, act, parts, tile))
    lanes = hidden_width // parts
    out_lanes = -(-width // parts // LANES) * LANES
    shape = (parts // 2, width, lanes + out_lanes)
    out_sums = split_grad(
        core,
        tied(mixed, down.sent),
        branch,
        mlp_gain_grad,
        256,
        parts,
        shape,
        lanes // out_lanes,
        "grad_attn_out",
    )
    out_sums = meet(out_sums, down)
    down.end(apart=True)
    split = tiles * 5 // 8
    down_a, down_b = Sum(down.terms), Sum(down.terms)
    sent = down_a.begin("rows", 2, 0, (1, 0, split))
    up_sums = up_grad(core, tied(second, sent), grad_up, parts, out_sums)
    up = Sum.of_cores(*meet(up_sums, down_a))

    def finish_output(first, number, prior, *others):
        return mlp_output(
            tied(residual, *others), act, down_weight, frames_in.shape, first, number, prior
        )

    pieces = (2, 2, steps - 4)
    down_a.end(apart=True)
    sent = [up.sent, down_b.begin("rows", 2, 0, (1, split, tiles - split))]
    output = meet(finish_output(0, pieces[0], None, sent), down_b, up)
    down_b.end(apart=True)
    down = joined(down_a, down_b, 0)
    if tiles != owners:
        moved = jnp.swapaxes(down.terms[0], 0, 1).reshape(width // parts, owners, -1)
        down.terms = [jnp.swapaxes(moved, 0, 1)]
    up.end(apart=True)
    split = shape[-1] // 2
    up_a, up_b = up.part(np.s_[..., :split]), up.part(np.s_[..., split:])
    sent = [down.begin_frames(), up_a.begin("rows", 2, 0), up_b.begin_frames(1)]
    grads = attend_back(
        core,
        proj,
        token_kv,
        expo,
        tied(grad_mixed, sent),
        delta,
        frames_in,
        branch,
        message,
        attn_gain,
        attn_qkv,
        parts,
    )
    grad_in, class_rows, message_grad, *qkv_sums = meet(grads, down, up_a, up_b)
    message_grad = jnp.pad(message_grad.reshape(count, width), extra)
    gather = Gather("frames", message_grad)
    gather.begin()
    qkv_a, qkv_b = (Sum.of_cores(qkv_sums[i], qkv_sums[2 + i]) for i in range(2))
    for one in (down, up_a, up_b):
        one.end()
    gather.got = tied(gather.got, up_a.terms, up_b.terms, down.terms)
    gather.end()
    gather.begin(direct=False)
    sent = [gather.values, down.step_frames(), up_a.begin_frames(), up_b.begin("rows", 2, 0)]
    sent = meet(sent, qkv_a, qkv_b)
    qkv_a.end()
    qkv_b.end()
    sent = [sent, qkv_a.begin("rows", 2, 0), qkv_b.begin_frames(1)]
    output = finish_output(pieces[0], pieces[1], output, sent)
    output = meet(output, gather, down, up_a, up_b, qkv_a, qkv_b)
    gather.end()
    gather.begin(direct=False)
    down.end(apart=True)
    up_a.end(apart=True)
    up_b.end(apart=True)
    up = joined(up_a, up_b, 2)
    qkv_a.end()
    qkv_b.end()
    sent = [
        gather.values,
        down.begin_last(),
        up.step_frames(),
        qkv_a.begin_frames(),
        qkv_b.begin("rows", 2, 0),
    ]
    output = finish_output(sum(pieces[:2]), pieces[2], output, sent)
    output = meet(output, gather, down, up, qkv_a, qkv_b)
    gather.end()
    up.end(apart=True)
    qkv_a.end(apart=True)
    qkv_b.end(apart=True)
    qkv = joined(qkv_a, qkv_b, 2)
    down.end(apart=True)
    grad_down = down.total().T
    sent = [up.begin_last(), qkv.begin_last(), grad_down]
    grads = message_back(
        block_index,
        parts,
        width // owners,
        own,
        tied(gather.pieces, sent),
        saved,
        msg_weight,
        msg_gain,
        msg_qkv,
        msg_out,
    )
    class_grad, msg_sums = meet(grads, qkv)
    msg = Sum([msg_sums.reshape(2, 2, *msg_sums.shape[1:])])
    msg.begin("rows", 1, 1)
    msg.end()
    sent = msg.begin("rows", 2, 0)
    class_grad, qkv.got = tied((class_grad, qkv.got), sent)
    class_rows = (class_rows[:, 0] + class_grad[:count]).astype(BFLOAT)
    grad_in = lax.dynamic_update_slice(grad_in, class_rows[:, None], (0, 0, 0))
    for one in (up, qkv, msg):
        one.end(apart=True)
    grad_up, grad_qkv, msg_total = up.total(), qkv.total(), msg.total()
    third, fourth, fifth = (n * width // parts for n in (3, 4, 5))
    return (
        output[0],
        grad_in,
        msg_total[:, third:fourth],
        msg_total[:, fifth],
        msg_total[:, :third],
        msg_total[:, fourth:fifth],
        grad_qkv[:, third],
        grad_qkv[:, :third],
        grad_up[:, lanes : lanes + width // parts],
        grad_up[:, lanes + width // parts],
        grad_up[:, :lanes],
        grad_down,
    )


def solution(mesh):
    split = P(("frames", "rows"))
    matrix = P("frames", "rows")
    gain = P("frames")
    return jax.shard_map(
        per_device,
        mesh=mesh,
        in_specs=(split, split, split, split) + (P(),) * 10,
        out_specs=(
            split,
            split,
            matrix,
            gain,
            matrix,
            matrix,
            gain,
            matrix,
            matrix,
            gain,
            matrix,
            matrix,
        ),
        check_vma=False,
    )
```

```python
import functools

import jax
import jax.numpy as jnp
import numpy as np
from jax import lax
from jax.experimental import pallas as pl
from jax.experimental.pallas import tpu as pltpu
from jax.sharding import PartitionSpec as P

H = 12
HD = 64
PAIR = 2 * HD
GROUP = 2
EPS = 1e-05
NEG = -1e30
BASE = 128.0
DIGITS = 3
LANES = 128
FLOAT = jnp.float32
BFLOAT = jnp.bfloat16
VMEM_BYTES = 60 * 1024 * 1024


def params(**kw):
    return pltpu.CompilerParams(vmem_limit_bytes=VMEM_BYTES, **kw)


def cost(flops, moved):
    return pl.CostEstimate(flops=int(flops / 100), transcendentals=0, bytes_accessed=int(moved / 100))


def padded_len(frame_len):
    return -(-(frame_len + 1) // 8) * 8


def whole(shape):
    return pl.BlockSpec(shape, lambda *_: (0,) * len(shape), pipeline_mode=pl.Buffered(1))


def rows_of(height, width, first=0):
    return pl.BlockSpec((height, width), lambda i: (i + first, 0))


def frames_of(pad, width, first=0):
    return pl.BlockSpec((GROUP, pad, width), lambda i: (i + first, 0, 0))


def normalize(values):
    center = values - jnp.mean(values, axis=-1, keepdims=True)
    spread = jnp.mean(center * center, axis=-1, keepdims=True)
    scale_inv = lax.rsqrt(spread + EPS)
    return (center * scale_inv, scale_inv)


def norm_back(grad_normed, normed, scale_inv):
    return scale_inv * (
        grad_normed
        - jnp.mean(grad_normed, axis=-1, keepdims=True)
        - normed * jnp.mean(grad_normed * normed, axis=-1, keepdims=True)
    )


def dot(a, b):
    return jnp.dot(a, b, preferred_element_type=FLOAT)


def dot_nt(a, b):
    return lax.dot_general(a, b, (((1,), (1,)), ((), ())), preferred_element_type=FLOAT)


def dot_tn(a, b):
    return lax.dot_general(a, b, (((0,), (0,)), ((), ())), preferred_element_type=FLOAT)


def load_rows(ref, frame_len):
    values = ref[...].astype(FLOAT)
    count, pad, width = values.shape
    row = lax.broadcasted_iota(jnp.int32, values.shape, 1)
    return jnp.where(row < frame_len, values, 0.0).reshape(count * pad, width)


def project_kernel(frame_len, x_ref, gain_ref, w_ref, proj_ref):
    normed, _ = normalize(load_rows(x_ref, frame_len))
    hidden = (normed * gain_ref[...]).astype(BFLOAT)
    width = hidden.shape[1]
    for part in range(3):
        cols = slice(part * width, (part + 1) * width)
        proj_ref[:, cols] = dot(hidden, w_ref[:, cols]).astype(BFLOAT)


def alias_call(
    kernel, grid, in_specs, args, prior, out_specs, out_shape, name, flops, moved, scratch=()
):
    extra = [] if prior is None else list(prior)

    def body(*refs):
        kernel(*refs[: len(args)], *refs[len(args) + len(extra) :])

    return pl.pallas_call(
        body,
        grid=grid,
        in_specs=in_specs + [pl.BlockSpec(memory_space=pl.ANY)] * len(extra),
        out_specs=out_specs,
        out_shape=out_shape,
        input_output_aliases={len(args) + i: i for i in range(len(extra))},
        scratch_shapes=list(scratch),
        compiler_params=params(),
        cost_estimate=cost(flops, moved),
        name=name,
    )(*args, *extra)


def project(frames_in, gain, qkv, first, steps, prior):
    count, frame_len, width = frames_in.shape
    pad = padded_len(frame_len)
    block = GROUP * pad
    return alias_call(
        functools.partial(project_kernel, frame_len),
        (steps,),
        [frames_of(pad, width, first), whole((width,)), whole(qkv.shape)],
        (frames_in, gain, qkv),
        prior,
        [rows_of(block, 3 * width, first)],
        [jax.ShapeDtypeStruct((count * pad, 3 * width), BFLOAT)],
        "project",
        6 * steps * block * width * width,
        8 * steps * block * width,
    )


def last_rows(rows, change):
    cut = rows.shape[0] - 8
    return jnp.concatenate([rows[:cut], change(rows[cut:], cut)], axis=0)


def token_in(rows, token, frame_len):
    def change(tail, cut):
        row = lax.broadcasted_iota(jnp.int32, tail.shape, 0)
        return jnp.where(row == frame_len - cut, token, tail)

    return last_rows(rows, change)


def one_head(pair, h):
    lane = lax.broadcasted_iota(jnp.int32, pair.shape, 1)
    return jnp.where((lane >= HD) == (h == 1), pair, jnp.zeros_like(pair))


def attend_kernel(
    frame_len, x_ref, proj_ref, token_ref, out_w_ref, expo_ref, mixed_ref, scale_ref, res_ref
):
    width = x_ref.shape[2]
    pad = x_ref.shape[1]
    pairs = width // PAIR

    def hide(tail, cut):
        row = lax.broadcasted_iota(jnp.int32, tail.shape, 0)
        return jnp.where(row <= frame_len - cut, tail, NEG)

    def at(part, j):
        return pl.ds(part * width + j * PAIR, PAIR)

    def weigh(f, j):
        rows = pl.ds(f * pad, pad)
        query = proj_ref[rows, at(0, j)] * 0.125
        key = token_in(proj_ref[rows, at(1, j)], token_ref[f, :, at(0, j)], frame_len)
        for h in range(2):
            scores = last_rows(dot_nt(one_head(key, h), query), hide)
            expo = jnp.exp(scores - jnp.max(scores, axis=0, keepdims=True)).astype(BFLOAT)
            expo_ref[f, 2 * j + h] = expo

    def mix(f, j):
        rows = pl.ds(f * pad, pad)
        value = token_in(proj_ref[rows, at(2, j)], token_ref[f, :, at(1, j)], frame_len)
        value_t = value.astype(FLOAT).T.astype(BFLOAT)
        outs = []
        for h in range(2):
            ones = jnp.ones((8, pad), BFLOAT)
            out = dot(jnp.concatenate([value_t[h * HD : (h + 1) * HD], ones]), expo_ref[f, 2 * j + h])
            scale = 1.0 / out[HD : HD + 1]
            outs.append(out[:HD] * scale)
            scale_ref[f, 2 * j + h : 2 * j + h + 1, :] = scale
        mixed_ref[rows, at(0, j)] = jnp.concatenate(outs, axis=0).T.astype(BFLOAT)

    units = [(f, j) for j in range(pairs) for f in range(GROUP)]
    for i in range(len(units) + 2):
        if i < len(units):
            weigh(*units[i])
        if i >= 2:
            mix(*units[i - 2])
    residual = load_rows(x_ref, frame_len) + dot(mixed_ref[...], out_w_ref[...])
    res_ref[...] = residual.astype(BFLOAT)


def attend(frames_in, proj, token_kv, out_w):
    count, frame_len, width = frames_in.shape
    pad = padded_len(frame_len)
    block = GROUP * pad
    heads = width // HD
    return pl.pallas_call(
        functools.partial(attend_kernel, frame_len),
        grid=(count // GROUP,),
        in_specs=[
            frames_of(pad, width),
            rows_of(block, 3 * width),
            frames_of(1, 2 * width),
            whole(out_w.shape),
        ],
        out_specs=[
            pl.BlockSpec((GROUP, heads, pad, pad), lambda i: (i, 0, 0, 0)),
            rows_of(block, width),
            frames_of(heads, pad),
            rows_of(block, width),
        ],
        out_shape=[
            jax.ShapeDtypeStruct((count, heads, pad, pad), BFLOAT),
            jax.ShapeDtypeStruct((count * pad, width), BFLOAT),
            jax.ShapeDtypeStruct((count, heads, pad), FLOAT),
            jax.ShapeDtypeStruct((count * pad, width), BFLOAT),
        ],
        compiler_params=params(),
        cost_estimate=cost(25e9, 50e6),
        name="attend",
    )(frames_in, proj, token_kv, out_w)


def mlp_kernel(
    frame_len,
    parts,
    res_ref,
    cot_ref,
    gain_ref,
    up_ref,
    down_ref,
    out_w_ref,
    mixed_ref,
    scale_ref,
    cot_rows_ref,
    second_ref,
    act_ref,
    grad_up_ref,
    branch_ref,
    grad_mixed_ref,
    delta_ref,
    gain_grad_ref,
):
    residual = res_ref[...].astype(FLOAT)
    width = residual.shape[1]
    normed, scale_inv = normalize(residual)
    gain = gain_ref[...]
    second = (normed * gain).astype(BFLOAT)
    second_ref[...] = second
    cot = load_rows(cot_ref, frame_len)
    cot_bf = cot.astype(BFLOAT)
    cot_rows_ref[...] = cot_bf
    grad_second = jnp.zeros_like(residual)
    size = up_ref.shape[1] // parts
    for part in range(parts):
        cols = slice(part * size, (part + 1) * size)
        up_part = dot(second, up_ref[:, cols])
        sigma = 0.5 * jnp.tanh(0.851 * up_part) + 0.5
        gated = up_part * sigma
        act = gated.astype(BFLOAT)
        act_ref[:, cols] = act
        grad_act = dot_nt(cot_bf, down_ref[cols, :])
        grad_up = (grad_act * (sigma + 1.702 * gated * (1.0 - sigma))).astype(BFLOAT)
        grad_up_ref[:, cols] = grad_up
        grad_second = grad_second + dot_nt(grad_up, up_ref[:, cols])
    gain_grad = jnp.sum(grad_second * normed, axis=0, keepdims=True)
    step = pl.program_id(0)
    gain_grad_ref[...] = jnp.where(step == 0, 0.0, gain_grad_ref[...]) + gain_grad
    branch = (cot + norm_back(grad_second * gain, normed, scale_inv)).astype(BFLOAT)
    branch_ref[...] = branch
    heads, pad = delta_ref.shape[1:]
    head = lax.broadcasted_iota(jnp.int32, (heads, width), 0)
    lane = lax.broadcasted_iota(jnp.int32, (heads, width), 1)
    of_head = (lane // HD == head).astype(FLOAT)
    scales = []
    for f in range(GROUP):
        high = scale_ref[f].astype(BFLOAT).astype(FLOAT)
        rows = jnp.concatenate([high, scale_ref[f] - high]).astype(BFLOAT)
        scales.append(dot_tn(rows, jnp.concatenate([of_head, of_head]).astype(BFLOAT)))
    of_head = of_head.astype(BFLOAT)
    grad_mixed = dot_nt(branch, out_w_ref[...]) * jnp.concatenate(scales)
    grad_mixed = grad_mixed.astype(BFLOAT)
    grad_mixed_ref[...] = grad_mixed
    product = grad_mixed * mixed_ref[...]
    for f in range(GROUP):
        delta_ref[f] = dot_nt(of_head, product[f * pad : (f + 1) * pad])


def mlp(residual, cotangent, gain, up, down, out_w, mixed, scale):
    count, frame_len, width = cotangent.shape
    pad = padded_len(frame_len)
    block = GROUP * pad
    rows = count * pad
    heads = width // HD
    hidden = up.shape[1]
    shape = jax.ShapeDtypeStruct
    return pl.pallas_call(
        functools.partial(mlp_kernel, frame_len, 4),
        grid=(count // GROUP,),
        in_specs=[
            rows_of(block, width),
            frames_of(pad, width),
            whole((width,)),
            whole(up.shape),
            whole(down.shape),
            whole(out_w.shape),
            rows_of(block, width),
            frames_of(heads, pad),
        ],
        out_specs=[
            rows_of(block, width),
            rows_of(block, width),
            rows_of(block, hidden),
            rows_of(block, hidden),
            rows_of(block, width),
            rows_of(block, width),
            pl.BlockSpec((GROUP, heads, pad), lambda i: (i, 0, 0)),
            pl.BlockSpec((1, width), lambda i: (0, 0)),
        ],
        out_shape=[
            shape((rows, width), BFLOAT),
            shape((rows, width), BFLOAT),
            shape((rows, hidden), BFLOAT),
            shape((rows, hidden), BFLOAT),
            shape((rows, width), BFLOAT),
            shape((rows, width), BFLOAT),
            shape((count, heads, pad), FLOAT),
            shape((1, width), FLOAT),
        ],
        compiler_params=params(),
        cost_estimate=cost(6 * rows * width * hidden, 60e6),
        name="mlp",
    )(residual, cotangent, gain, up, down, out_w, mixed, scale)


def output_kernel(res_ref, act_ref, down_ref, output_ref):
    out = res_ref[...].astype(FLOAT) + dot(act_ref[...], down_ref[...])
    output_ref[...] = out.astype(BFLOAT).reshape(output_ref.shape)


def mlp_output(residual, act, down, shape, first, steps, prior):
    count, frame_len, width = shape
    pad = padded_len(frame_len)
    block = GROUP * pad
    hidden = down.shape[0]
    return alias_call(
        output_kernel,
        (steps,),
        [rows_of(block, width, first), rows_of(block, hidden, first), whole(down.shape)],
        (residual, act, down),
        prior,
        [frames_of(pad, width, first)],
        [jax.ShapeDtypeStruct(shape, BFLOAT)],
        "mlp_output",
        2 * steps * block * width * hidden,
        8 * steps * block * width,
    )


def weight_grad_kernel(core_ref, left_ref, right_ref, *refs):
    send_ref, keep_ref = refs[-2:]
    total = dot_tn(left_ref[...], right_ref[...]).astype(BFLOAT)
    step = pl.program_id(0)

    @pl.when(step < 2)
    def _():
        send_ref[0] = total

    @pl.when(step >= 2)
    def _():
        keep_ref[0] = total


def up_grad(core, left, right, parts, prior):
    rows, width = left.shape
    lanes = right.shape[1] // parts

    def block(i, core_ref):
        return 2 * (i % 2) + jnp.where(i < 2, 1 - core_ref[0], core_ref[0])

    return pl.pallas_call(
        weight_grad_kernel,
        grid_spec=pltpu.PrefetchScalarGridSpec(
            num_scalar_prefetch=1,
            grid=(parts,),
            in_specs=[
                pl.BlockSpec(left.shape, lambda i, c: (0, 0), pipeline_mode=pl.Buffered(1)),
                pl.BlockSpec((rows, lanes), lambda i, c: (0, block(i, c))),
                pl.BlockSpec(memory_space=pl.ANY),
                pl.BlockSpec(memory_space=pl.ANY),
            ],
            out_specs=[
                pl.BlockSpec((1, width, lanes), lambda i, c: (jnp.minimum(i, 1), 0, 0)),
                pl.BlockSpec((1, width, lanes), lambda i, c: (jnp.maximum(i - 2, 0), 0, 0)),
            ],
        ),
        out_shape=[jax.ShapeDtypeStruct(p.shape, BFLOAT) for p in prior],
        input_output_aliases={3: 0, 4: 1},
        compiler_params=params(),
        cost_estimate=cost(2 * left.size * right.shape[1], 2 * (left.size + right.size)),
        name="grad_up",
    )(core, left, right, *prior)


def by_core(core, blocks):
    pairs = [(blocks[2 * y], blocks[2 * y + 1]) for y in range(len(blocks) // 2)]
    first = core == 0
    send = [jnp.where(first, odd, even) for even, odd in pairs]
    return send, [jnp.where(first, even, odd) for even, odd in pairs]


def down_grad_kernel(core_ref, left_ref, right_ref, send_ref, keep_ref):
    total = dot_tn(left_ref[...], right_ref[...]).astype(BFLOAT)
    parts, pieces, height, columns = 2 * send_ref.shape[0], *send_ref.shape[1:]
    for piece in range(pieces):
        cols = slice(piece * columns, (piece + 1) * columns)
        blocks = [total[part * height : (part + 1) * height, cols] for part in range(parts)]
        for ref, values in zip((send_ref, keep_ref), by_core(core_ref[0], blocks)):
            for y, value in enumerate(values):
                ref[y, piece] = value


def down_grad(core, left, right, parts, tile):
    rows, width = left.shape
    tiles = right.shape[1] // tile
    shape = (parts // 2, tiles, width // parts, tile)
    spec = pl.BlockSpec((parts // 2, 2, width // parts, tile), lambda i: (0, i, 0, 0))
    return pl.pallas_call(
        down_grad_kernel,
        grid=(tiles // 2,),
        in_specs=[
            pl.BlockSpec(memory_space=pltpu.SMEM),
            whole(left.shape),
            pl.BlockSpec((rows, 2 * tile), lambda i: (0, i)),
        ],
        out_specs=[spec, spec],
        out_shape=[jax.ShapeDtypeStruct(shape, BFLOAT)] * 2,
        compiler_params=params(),
        cost_estimate=cost(2 * left.size * right.shape[1], 2 * (left.size + right.size)),
        name="grad_down",
    )(core, left, right)


def with_gain(block, gain, lanes):
    column = jnp.broadcast_to(gain, (8, gain.shape[1])).T.astype(BFLOAT)
    blank = jnp.zeros((block.shape[0], lanes - block.shape[1] - 8), BFLOAT)
    return jnp.concatenate([block, column, blank], axis=1)


def store_split(core, total_ref, gain, send_refs, keep_refs):
    halves = send_refs[0].shape[0]
    parts = 2 * halves
    size = total_ref.shape[1] // parts
    lanes = sum(ref.shape[2] for ref in send_refs)
    for y in range(halves):
        blocks = [
            with_gain(total_ref[:, part * size : (part + 1) * size].astype(BFLOAT), gain, lanes)
            for part in (2 * y, 2 * y + 1)
        ]
        for refs, (value,) in zip((send_refs, keep_refs), by_core(core, blocks)):
            offset = 0
            for ref in refs:
                ref[y] = value[:, offset : offset + ref.shape[2]]
                offset += ref.shape[2]


def split_grad_kernel(core_ref, left_ref, right_ref, gain_ref, send_ref, keep_ref, all_ref):
    step = pl.program_id(0)
    tile = right_ref.shape[1]
    all_ref[:, pl.ds(pl.multiple_of(step * tile, tile), tile)] = dot_tn(
        left_ref[...], right_ref[...]
    ).astype(BFLOAT)

    @pl.when(step == pl.num_programs(0) - 1)
    def _():
        store_split(core_ref[0], all_ref, gain_ref[...], [send_ref], [keep_ref])


def split_grad(core, left, right, gain, tile, parts, shape, index, name):
    rows, width = left.shape
    columns = right.shape[1]
    size = -(-columns // parts // LANES) * LANES
    spec = pl.BlockSpec((parts // 2, width, size), lambda i: (0, 0, index))
    return pl.pallas_call(
        split_grad_kernel,
        grid=(columns // tile,),
        in_specs=[
            pl.BlockSpec(memory_space=pltpu.SMEM),
            whole(left.shape),
            pl.BlockSpec((rows, tile), lambda i: (0, i)),
            whole(gain.shape),
        ],
        out_specs=[spec, spec],
        out_shape=[jax.ShapeDtypeStruct(shape, BFLOAT)] * 2,
        scratch_shapes=[pltpu.VMEM((width, columns), BFLOAT)],
        compiler_params=params(),
        cost_estimate=cost(2 * left.size * columns, 2 * (left.size + right.size)),
        name=name,
    )(core, left, right, gain)


def attend_back_kernel(
    frame_len,
    core_ref,
    proj_ref,
    token_ref,
    expo_ref,
    grad_mixed_ref,
    delta_ref,
    x_ref,
    branch_ref,
    message_ref,
    gain_ref,
    w_ref,
    grad_in_ref,
    class_ref,
    message_grad_ref,
    send_0_ref,
    send_1_ref,
    keep_0_ref,
    keep_1_ref,
    scores_ref,
    grad_proj_ref,
    total_ref,
    gain_grad_ref,
):
    pad = expo_ref.shape[2]
    width = grad_mixed_ref.shape[1]
    pairs = width // PAIR
    step = pl.program_id(0)

    @pl.when(step == 0)
    def _():
        total_ref[...] = jnp.zeros_like(total_ref)
        gain_grad_ref[...] = jnp.zeros_like(gain_grad_ref)

    def at(part, j):
        return pl.ds(part * width + j * PAIR, PAIR)

    def weigh(f, j):
        rows = pl.ds(f * pad, pad)
        value = token_in(proj_ref[rows, at(2, j)], token_ref[f, :, at(1, j)], frame_len)
        grad = grad_mixed_ref[rows, at(0, j)]
        for h in range(2):
            head = 2 * j + h
            grad_prob = dot_nt(one_head(value, h), grad) - delta_ref[f, head : head + 1, :]
            scores_ref[f, head] = expo_ref[f, head] * grad_prob.astype(BFLOAT)

    def mix(f, j):
        rows = pl.ds(f * pad, pad)
        query = proj_ref[rows, at(0, j)]
        key = token_in(proj_ref[rows, at(1, j)], token_ref[f, :, at(0, j)], frame_len)
        grad = grad_mixed_ref[rows, at(0, j)]
        key_t = key.astype(FLOAT).T.astype(BFLOAT)
        grad_query, grad_key, grad_value = [], [], []
        for h in range(2):
            scores = scores_ref[f, 2 * j + h]
            grad_value.append(dot(expo_ref[f, 2 * j + h], one_head(grad, h)))
            grad_key.append(dot(scores, one_head(query, h)))
            grad_query.append(dot(key_t[h * HD : (h + 1) * HD], scores))
        grad_query = jnp.concatenate(grad_query, axis=0).T * 0.125
        grad_proj_ref[rows, at(0, j)] = grad_query.astype(BFLOAT)
        grad_key = (grad_key[0] + grad_key[1]) * 0.125
        grad_proj_ref[rows, at(1, j)] = grad_key.astype(BFLOAT)
        grad_value = grad_value[0] + grad_value[1]
        grad_proj_ref[rows, at(2, j)] = grad_value.astype(BFLOAT)

    units = [(f, j) for j in range(pairs) for f in range(GROUP)]
    for i in range(len(units) + 2):
        if i < len(units):
            weigh(*units[i])
        if i >= 2:
            mix(*units[i - 2])

    values = load_rows(x_ref, frame_len)
    values = jnp.concatenate(
        [
            token_in(values[f * pad : (f + 1) * pad], message_ref[f].astype(FLOAT), frame_len)
            for f in range(GROUP)
        ]
    )
    normed, scale_inv = normalize(values)
    hidden = (normed * gain_ref[...]).astype(BFLOAT)
    for part in range(3):
        cols = slice(part * width, (part + 1) * width)
        total_ref[:, cols] += dot_tn(hidden, grad_proj_ref[:, cols])
    grad = dot_nt(grad_proj_ref[...], w_ref[...])
    gain_grad_ref[...] += jnp.sum(grad * normed, axis=0, keepdims=True)
    total = branch_ref[...].astype(FLOAT) + norm_back(grad * gain_ref[...], normed, scale_inv)
    total = total.reshape(GROUP, pad, width)
    grad_in_ref[...] = total.astype(BFLOAT)
    for f in range(GROUP):
        class_ref[f] = total[f, :1]
        message_grad_ref[f] = total[f, frame_len : frame_len + 1].astype(BFLOAT)

    @pl.when(step == pl.num_programs(0) - 1)
    def _():
        store_split(
            core_ref[0],
            total_ref,
            gain_grad_ref[...],
            [send_0_ref, send_1_ref],
            [keep_0_ref, keep_1_ref],
        )


def attend_back(
    core, proj, token_kv, expo, grad_mixed, delta, frames_in, branch, message, gain, qkv, parts
):
    count, heads, pad, _ = expo.shape
    frame_len, width = frames_in.shape[1:]
    block = GROUP * pad
    lanes = -(-3 * width // parts // LANES) * LANES
    first = lanes // (2 * LANES) * LANES + LANES
    sums = [(parts // 2, width, n) for n in (first, lanes - first)] * 2
    shape = jax.ShapeDtypeStruct
    return pl.pallas_call(
        functools.partial(attend_back_kernel, frame_len),
        grid=(count // GROUP,),
        in_specs=[
            pl.BlockSpec(memory_space=pltpu.SMEM),
            rows_of(block, 3 * width),
            frames_of(1, 2 * width),
            pl.BlockSpec((GROUP, heads, pad, pad), lambda i: (i, 0, 0, 0)),
            rows_of(block, width),
            pl.BlockSpec((GROUP, heads, pad), lambda i: (i, 0, 0)),
            frames_of(pad, width),
            rows_of(block, width),
            frames_of(1, width),
            whole((width,)),
            whole(qkv.shape),
        ],
        out_specs=[frames_of(pad, width), frames_of(1, width), frames_of(1, width)]
        + [whole(s) for s in sums],
        out_shape=[
            shape((count, frame_len, width), BFLOAT),
            shape((count, 1, width), FLOAT),
            shape((count, 1, width), BFLOAT),
        ]
        + [shape(s, BFLOAT) for s in sums],
        scratch_shapes=[
            pltpu.VMEM((GROUP, heads, pad, pad), BFLOAT),
            pltpu.VMEM((block, 3 * width), BFLOAT),
            pltpu.VMEM((width, 3 * width), FLOAT),
            pltpu.VMEM((1, width), FLOAT),
        ],
        compiler_params=params(),
        cost_estimate=cost(45e9, 50e6),
        name="attend_back",
    )(core, proj, token_kv, expo, grad_mixed, delta, frames_in, branch, message, gain, qkv)


def in_turn(count, slots, first, second):
    if slots > 256:

        def both(j, carry):
            first(j)
            second(j)
            return carry

        lax.fori_loop(0, count, both, 0)
        return
    for j in range(count + 2):
        if j < count:
            first(j)
        if j >= 2:
            second(j - 2)


def message_kernel(
    own,
    pieces,
    *refs,
):
    gathered = jnp.concatenate([ref[...] for ref in refs[:pieces]])
    message_body(own, gathered, *refs[pieces:])


def message_body(
    own,
    gathered,
    weight_ref,
    gain_ref,
    qkv_ref,
    out_w_ref,
    attn_gain_ref,
    key_w_ref,
    value_w_ref,
    class_ref,
    start_ref,
    hidden_ref,
    proj_ref,
    prob_ref,
    mixed_ref,
    message_ref,
    token_kv_ref,
):
    width = weight_ref.shape[0]
    class_ref[...] = gathered[:, :width]
    start = dot(gathered[:, :width], weight_ref[...]).astype(BFLOAT)
    start_ref[...] = start
    normed, _ = normalize(start.astype(FLOAT))
    hidden = (normed * gain_ref[...]).astype(BFLOAT)
    hidden_ref[...] = hidden
    proj_ref[...] = dot(hidden, qkv_ref[...]).astype(BFLOAT)
    digits = gathered[:, width:].astype(FLOAT)
    lane = lax.broadcasted_iota(jnp.int32, digits.shape, 1)
    weights = jnp.where(lane == 0, 1.0, jnp.where(lane == 1, BASE, BASE * BASE))
    digits = jnp.where(lane < DIGITS, digits * weights, 0.0)
    id_col = jnp.sum(digits, axis=1, keepdims=True)
    id_row = jnp.sum(digits.T, axis=0, keepdims=True)
    visible = id_col == id_row

    def at(part, j):
        start = part * width + j * PAIR
        return pl.ds(start if isinstance(j, int) else pl.multiple_of(start, PAIR), PAIR)

    def weigh(j):
        query = proj_ref[:, at(0, j)] * 0.125
        for h in range(2):
            scores = jnp.where(visible, dot_nt(proj_ref[:, at(1, j)], one_head(query, h)), NEG)
            expo = jnp.exp(scores - jnp.max(scores, axis=0, keepdims=True))
            prob = expo * (1.0 / jnp.sum(expo, axis=0, keepdims=True))
            prob_ref[2 * j + h] = prob.astype(BFLOAT)

    def mix(j):
        value_t = proj_ref[:, at(2, j)].astype(FLOAT).T.astype(BFLOAT)
        outs = [dot(value_t[h * HD : (h + 1) * HD], prob_ref[2 * j + h]) for h in range(2)]
        mixed_ref[:, at(0, j)] = jnp.concatenate(outs, axis=0).T.astype(BFLOAT)

    in_turn(width // PAIR, start.shape[0], weigh, mix)
    message = start[:own].astype(FLOAT) + dot(mixed_ref[:own, :], out_w_ref[...])
    message = message.astype(BFLOAT)
    message_ref[...] = message
    normed, _ = normalize(message.astype(FLOAT))
    token_hidden = (normed * attn_gain_ref[...]).astype(BFLOAT)
    token_kv_ref[:, :width] = dot(token_hidden, key_w_ref[...]).astype(BFLOAT)
    token_kv_ref[:, width:] = dot(token_hidden, value_w_ref[...]).astype(BFLOAT)


def message_forward(class_parts, own, weight, gain, qkv, out_w, attn_gain, attn_qkv):
    slots = sum(part.shape[0] for part in class_parts)
    width = weight.shape[0]
    heads = width // HD
    shape = jax.ShapeDtypeStruct
    part = lambda index: pl.BlockSpec((width, width), lambda i, index=index: (0, index))
    return pl.pallas_call(
        functools.partial(message_kernel, own, len(class_parts)),
        grid=(1,),
        in_specs=[whole(p.shape) for p in class_parts]
        + [
            whole(weight.shape),
            whole((width,)),
            whole(qkv.shape),
            whole(out_w.shape),
            whole((width,)),
            part(1),
            part(2),
        ],
        out_specs=[
            whole((slots, width)),
            whole((slots, width)),
            whole((slots, width)),
            whole((slots, 3 * width)),
            whole((heads, slots, slots)),
            whole((slots, width)),
            whole((own, width)),
            whole((own, 2 * width)),
        ],
        out_shape=[
            shape((slots, width), BFLOAT),
            shape((slots, width), BFLOAT),
            shape((slots, width), BFLOAT),
            shape((slots, 3 * width), BFLOAT),
            shape((heads, slots, slots), BFLOAT),
            shape((slots, width), BFLOAT),
            shape((own, width), BFLOAT),
            shape((own, 2 * width), BFLOAT),
        ],
        compiler_params=params(),
        cost_estimate=cost(7e9, 9e6),
        name="message_forward",
    )(
        *class_parts,
        weight,
        gain,
        qkv,
        out_w,
        attn_gain,
        attn_qkv,
        attn_qkv,
    )


def message_back_kernel(
    own,
    parts,
    together,
    pieces,
    block_ref,
    *refs,
):
    grad = jnp.concatenate([ref[...] for ref in refs[:pieces]])
    message_back_body(own, parts, together, block_ref, grad, *refs[pieces:])


def message_back_body(
    own,
    parts,
    together,
    block_ref,
    grad,
    class_ref,
    start_ref,
    hidden_ref,
    proj_ref,
    prob_ref,
    mixed_ref,
    weight_ref,
    gain_ref,
    qkv_ref,
    out_w_ref,
    class_grad_ref,
    sums_ref,
    grad_mixed_ref,
    grad_proj_ref,
    scores_ref,
):
    width = weight_ref.shape[0]
    j = pl.program_id(0)

    @pl.when(j == 0)
    def _():
        grad_mixed_ref[...] = dot_nt(grad, out_w_ref[...]).astype(BFLOAT)

    def finish():
        grad_proj = grad_proj_ref[...]
        grad_hidden = dot_nt(grad_proj, qkv_ref[...])
        normed, scale_inv = normalize(start_ref[...].astype(FLOAT))
        gain_grad = jnp.sum(grad_hidden * normed, axis=0, keepdims=True)
        back = norm_back(grad_hidden * gain_ref[...], normed, scale_inv)
        start_grad = (grad.astype(FLOAT) + back).astype(BFLOAT)
        class_grad_ref[...] = dot_nt(start_grad[:own], weight_ref[...])
        size = sums_ref.shape[1]
        row = lax.broadcasted_iota(jnp.int32, (size, width), 0)
        column = lax.broadcasted_iota(jnp.int32, (size, width), 1)
        mine = column == row + block_ref[0] * size
        pick = mine.astype(BFLOAT)
        gain_grad = jnp.sum(jnp.where(mine, gain_grad, 0.0), axis=1, keepdims=True)
        lanes = sums_ref.shape[2] - 5 * width // parts
        for part in range(parts):
            sums_ref[part, :, 5 * width // parts :] = jnp.broadcast_to(
                gain_grad, (size, lanes)
            ).astype(BFLOAT)
        offset = 0
        for left, right in (
            (hidden_ref[...], grad_proj),
            (class_ref[:, :width], start_grad),
            (mixed_ref[...], grad),
        ):
            total = dot(dot_nt(pick, left).astype(BFLOAT), right).astype(BFLOAT)
            columns = total.shape[1] // parts
            for part in range(parts):
                sums_ref[part, :, offset : offset + columns] = total[
                    :, part * columns : (part + 1) * columns
                ]
            offset += columns

    def at(part, k):
        if together == 1:
            return pl.ds(pl.multiple_of(part * width + j * PAIR, PAIR), PAIR)
        return pl.ds(part * width + k * PAIR, PAIR)

    def weigh(k):
        value = proj_ref[:, at(2, k)]
        for h in range(2):
            grad_prob = dot_nt(value, one_head(grad_mixed_ref[:, at(0, k)], h))
            prob = prob_ref[2 * k + h].astype(FLOAT)
            part = prob * grad_prob
            scores = part - prob * jnp.sum(part, axis=0, keepdims=True)
            scores_ref[2 * k + h] = scores.astype(BFLOAT)

    def mix(k):
        query, key, grad_m = proj_ref[:, at(0, k)], proj_ref[:, at(1, k)], grad_mixed_ref[:, at(0, k)]
        key_t = key.astype(FLOAT).T.astype(BFLOAT)
        grad_query, grad_key, grad_value = [], [], []
        for h in range(2):
            scores = scores_ref[2 * k + h]
            grad_value.append(dot(prob_ref[2 * k + h], one_head(grad_m, h)))
            grad_key.append(dot(scores, one_head(query, h)))
            grad_query.append(dot(key_t[h * HD : (h + 1) * HD], scores))
        grad_query = jnp.concatenate(grad_query, axis=0).T * 0.125
        grad_proj_ref[:, at(0, k)] = grad_query.astype(BFLOAT)
        grad_proj_ref[:, at(1, k)] = ((grad_key[0] + grad_key[1]) * 0.125).astype(BFLOAT)
        grad_proj_ref[:, at(2, k)] = (grad_value[0] + grad_value[1]).astype(BFLOAT)

    if together == 1:
        weigh(0)
        mix(0)
    else:
        in_turn(together, grad.shape[0], weigh, mix)

    @pl.when(j == pl.num_programs(0) - 1)
    def _():
        finish()


def message_back(block, parts, size, own, grad_parts, saved, weight, gain, qkv, out_w):
    class_all, start, hidden, proj, prob, mixed = saved
    slots, width = class_all.shape
    shape = jax.ShapeDtypeStruct
    sums = (parts, size, -(-(5 * width // parts + 1) // LANES) * LANES)
    together = width // PAIR if slots <= 256 else 1
    args = (*grad_parts, class_all, start, hidden, proj, prob, mixed, weight, gain, qkv, out_w)
    return pl.pallas_call(
        functools.partial(message_back_kernel, own, parts, together, len(grad_parts)),
        grid=(width // PAIR // together,),
        in_specs=[pl.BlockSpec(memory_space=pltpu.SMEM)]
        + [pl.BlockSpec((2 * together, slots, slots), lambda j: (j, 0, 0)) if a is prob else whole(a.shape) for a in args],
        out_specs=[whole((own, width)), whole(sums)],
        out_shape=[shape((own, width), FLOAT), shape(sums, BFLOAT)],
        scratch_shapes=[
            pltpu.VMEM((slots, width), BFLOAT),
            pltpu.VMEM((slots, 3 * width), BFLOAT),
            pltpu.VMEM((2 * together, slots, slots), BFLOAT),
        ],
        compiler_params=params(),
        cost_estimate=cost(8e9, 9e6),
        name="message_back",
    )(block, *args)


def swap(values, axis, distance):
    return lax.ppermute(values, axis, [(i, i ^ distance) for i in range(lax.axis_size(axis))])


def tied(values, *others):
    return lax.optimization_barrier((values, others))[0]


def meet(outputs, *transfers):
    outputs, got = lax.optimization_barrier((outputs, [transfer.got for transfer in transfers]))
    for transfer, values in zip(transfers, got):
        transfer.got = values
    return outputs


def pick(values, index, axis=0, window=None):
    starts, sizes = [0] * values.ndim, list(values.shape)
    starts[axis], sizes[axis] = index, 1
    if window is not None:
        starts[window[0]], sizes[window[0]] = window[1:]
    return lax.squeeze(lax.dynamic_slice(values, starts, sizes), (axis,))


def add(*terms):
    total = terms[0].astype(FLOAT)
    for term in terms[1:]:
        total = total + term.astype(FLOAT)
    return total


class Gather:
    def __init__(self, axis, values):
        self.axis, self.values = axis, values
        self.distance, self.left = 1, lax.axis_size(axis)

    def begin(self, direct=True):
        while self.left > 8:
            self.finish(self.start(2))
        self.got = self.start(self.left if direct and self.left < 8 else 2)

    def start(self, size):
        got = [swap(self.values, self.axis, d * self.distance) for d in range(1, size)]
        self.distance, self.left = self.distance * size, self.left // size
        return got

    def finish(self, got):
        self.pieces = [self.values, *got]
        self.values = jnp.concatenate(self.pieces)

    def end(self):
        self.finish(self.got)
        return self.values


class Sum:
    def __init__(self, terms):
        self.terms = terms

    @classmethod
    def of_cores(cls, sent, kept):
        self = cls([kept])
        self.sent = sent
        self.got = [swap(sent, "rows", 1)]
        return self

    def part(self, index):
        return Sum([term[index] for term in self.terms])

    def total(self):
        return add(*self.terms)

    def begin(self, axis, distance, dim, window=None):
        bit = (lax.axis_index(axis) // distance) % 2
        sent = add(*(pick(term, 1 - bit, dim, window) for term in self.terms)).astype(BFLOAT)
        self.terms = [pick(term, bit, dim, window) for term in self.terms]
        self.got = [swap(sent, axis, distance)]
        return sent

    def end(self, apart=False):
        self.terms = self.got + self.terms
        if not apart:
            self.terms = [self.total().astype(BFLOAT)]

    def begin_frames(self, dim=0):
        self.left, self.distance, self.dim = lax.axis_size("frames"), 1, dim
        shape = self.terms[0].shape
        if len(shape) == 2 + dim:
            shape = (*shape[:dim], self.left, -1, shape[-1])
            self.terms = [term.reshape(shape) for term in self.terms]
        while self.left > 8:
            self.step_frames()
            self.end()
        return self.step_frames()

    def step_frames(self):
        shape, dim = self.terms[0].shape, self.dim
        shape = (*shape[:dim], self.left // 2, 2, *shape[dim + 1 :])
        self.terms = [term.reshape(shape) for term in self.terms]
        sent = self.begin("frames", self.distance, dim + 1)
        self.left, self.distance = self.left // 2, self.distance * 2
        return sent

    def begin_last(self):
        index = lax.axis_index("frames") // self.distance
        sent = [
            add(*(pick(term, index ^ d) for term in self.terms)).astype(BFLOAT)
            for d in range(1, self.left)
        ]
        self.terms = [pick(term, index) for term in self.terms]
        self.got = [
            swap(block, "frames", (d + 1) * self.distance) for d, block in enumerate(sent)
        ]
        return sent


def joined(first, second, axis):
    self = Sum([jnp.concatenate([first.total(), second.total()], axis=axis).astype(BFLOAT)])
    if hasattr(first, "left"):
        self.left, self.distance, self.dim = first.left, first.distance, first.dim
    return self


def per_device(
    frames_in,
    cotangent,
    video_ids,
    frame_device,
    msg_weight,
    msg_gain,
    msg_qkv,
    msg_out,
    attn_gain,
    attn_qkv,
    attn_out,
    mlp_gain,
    up_weight,
    down_weight,
):
    count, frame_len, width = frames_in.shape
    owners, parts = lax.axis_size("frames"), lax.axis_size("rows")
    hidden_width = up_weight.shape[1]
    own = -(-count // 16) * 16
    steps = count // GROUP
    block_index = lax.axis_index("frames").astype(jnp.int32).reshape(1)
    extra = ((0, own - count), (0, 0))

    ids = (video_ids * owners + frame_device)[:, None]
    base = int(BASE)
    digits = jnp.concatenate([ids % base, ids // base % base, ids // (base * base)], axis=1)
    digits = jnp.pad(digits, ((0, own - count), (0, LANES - DIGITS)), constant_values=-1)
    payload = jnp.concatenate([jnp.pad(frames_in[:, 0, :], extra), digits.astype(BFLOAT)], axis=1)
    gather = Gather("frames", payload)
    gather.begin()
    frames = tied(frames_in, payload)
    early = steps // 2
    projected = meet(project(frames, attn_gain, attn_qkv, 0, early, None), gather)
    gather.end()
    gather.begin()
    (proj,) = project(
        tied(frames, gather.values), attn_gain, attn_qkv, early, steps - early, projected
    )
    proj = meet(proj, gather)
    gather.end()

    *saved, message, token_kv = message_forward(
        gather.pieces, own, msg_weight, msg_gain, msg_qkv, msg_out, attn_gain, attn_qkv
    )
    token_kv = token_kv[:count, None]
    message = message[:count, None]
    expo, mixed, scale, residual = attend(frames_in, proj, token_kv, attn_out)
    cot, second, act, grad_up, branch, grad_mixed, delta, mlp_gain_grad = mlp(
        residual, cotangent, mlp_gain, up_weight, down_weight, attn_out, mixed, scale
    )

    core = (lax.axis_index("rows") % 2).astype(jnp.int32).reshape(1)
    tile = 3 * LANES
    tiles = hidden_width // tile
    down = Sum.of_cores(*down_grad(core, cot, act, parts, tile))
    lanes = hidden_width // parts
    out_lanes = -(-width // parts // LANES) * LANES
    shape = (parts // 2, width, lanes + out_lanes)
    out_sums = split_grad(
        core,
        tied(mixed, down.sent),
        branch,
        mlp_gain_grad,
        256,
        parts,
        shape,
        lanes // out_lanes,
        "grad_attn_out",
    )
    out_sums = meet(out_sums, down)
    down.end(apart=True)
    split = tiles * 3 // 4
    down_a, down_b = Sum(down.terms), Sum(down.terms)
    sent = down_a.begin("rows", 2, 0, (1, 0, split))
    up_sums = up_grad(core, tied(second, sent), grad_up, parts, out_sums)
    up = Sum.of_cores(*meet(up_sums, down_a))

    def finish_output(first, number, prior, *others):
        return mlp_output(
            tied(residual, *others), act, down_weight, frames_in.shape, first, number, prior
        )

    pieces = (2, steps - 4, 2)
    down_a.end(apart=True)
    sent = [up.sent, down_b.begin("rows", 2, 0, (1, split, tiles - split))]
    output = meet(finish_output(0, pieces[0], None, sent), down_b, up)
    down_b.end(apart=True)
    down = joined(down_a, down_b, 0)
    if tiles != owners:
        moved = jnp.swapaxes(down.terms[0], 0, 1).reshape(width // parts, owners, -1)
        down.terms = [jnp.swapaxes(moved, 0, 1)]
    up.end(apart=True)
    split = shape[-1] // 2
    up_a, up_b = up.part(np.s_[..., :split]), up.part(np.s_[..., split:])
    sent = [down.begin_frames(), up_a.begin("rows", 2, 0), up_b.begin_frames(1)]
    grads = attend_back(
        core,
        proj,
        token_kv,
        expo,
        tied(grad_mixed, sent),
        delta,
        frames_in,
        branch,
        message,
        attn_gain,
        attn_qkv,
        parts,
    )
    grad_in, class_rows, message_grad, *qkv_sums = meet(grads, down, up_a, up_b)
    message_grad = jnp.pad(message_grad.reshape(count, width), extra)
    gather = Gather("frames", message_grad)
    gather.begin()
    qkv_a, qkv_b = (Sum.of_cores(qkv_sums[i], qkv_sums[2 + i]) for i in range(2))
    for one in (down, up_a, up_b):
        one.end()
    gather.got = tied(gather.got, up_a.terms, up_b.terms, down.terms)
    gather.end()
    gather.begin(direct=False)
    sent = [gather.values, down.step_frames(), up_a.begin_frames(), up_b.begin("rows", 2, 0)]
    sent = meet(sent, qkv_a, qkv_b)
    qkv_a.end()
    qkv_b.end()
    sent = [sent, qkv_a.begin("rows", 2, 0), qkv_b.begin_frames(1)]
    output = finish_output(pieces[0], pieces[1], output, sent)
    output = meet(output, gather, down, up_a, up_b, qkv_a, qkv_b)
    gather.end()
    gather.begin(direct=False)
    down.end(apart=True)
    up_a.end(apart=True)
    up_b.end(apart=True)
    up = joined(up_a, up_b, 2)
    qkv_a.end()
    qkv_b.end()
    sent = [
        gather.values,
        down.begin_last(),
        up.step_frames(),
        qkv_a.begin_frames(),
        qkv_b.begin("rows", 2, 0),
    ]
    output = finish_output(sum(pieces[:2]), pieces[2], output, sent)
    output = meet(output, gather, down, up, qkv_a, qkv_b)
    gather.end()
    up.end(apart=True)
    qkv_a.end(apart=True)
    qkv_b.end(apart=True)
    qkv = joined(qkv_a, qkv_b, 2)
    down.end(apart=True)
    grad_down = down.total().T
    sent = [up.begin_last(), qkv.begin_last(), grad_down]
    grads = message_back(
        block_index,
        parts,
        width // owners,
        own,
        tied(gather.pieces, sent),
        saved,
        msg_weight,
        msg_gain,
        msg_qkv,
        msg_out,
    )
    class_grad, msg_sums = meet(grads, qkv)
    msg = Sum([msg_sums.reshape(2, 2, *msg_sums.shape[1:])])
    msg.begin("rows", 1, 1)
    msg.end()
    sent = msg.begin("rows", 2, 0)
    class_grad, qkv.got = tied((class_grad, qkv.got), sent)
    class_rows = (class_rows[:, 0] + class_grad[:count]).astype(BFLOAT)
    grad_in = lax.dynamic_update_slice(grad_in, class_rows[:, None], (0, 0, 0))
    for one in (up, qkv, msg):
        one.end(apart=True)
    grad_up, grad_qkv, msg_total = up.total(), qkv.total(), msg.total()
    third, fourth, fifth = (n * width // parts for n in (3, 4, 5))
    return (
        output[0],
        grad_in,
        msg_total[:, third:fourth],
        msg_total[:, fifth],
        msg_total[:, :third],
        msg_total[:, fourth:fifth],
        grad_qkv[:, third],
        grad_qkv[:, :third],
        grad_up[:, lanes : lanes + width // parts],
        grad_up[:, lanes + width // parts],
        grad_up[:, :lanes],
        grad_down,
    )


def solution(mesh):
    split = P(("frames", "rows"))
    matrix = P("frames", "rows")
    gain = P("frames")
    return jax.shard_map(
        per_device,
        mesh=mesh,
        in_specs=(split, split, split, split) + (P(),) * 10,
        out_specs=(
            split,
            split,
            matrix,
            gain,
            matrix,
            matrix,
            gain,
            matrix,
            matrix,
            gain,
            matrix,
            matrix,
        ),
        check_vma=False,
    )
```

```python
import functools

import jax
import jax.numpy as jnp
import numpy as np
from jax import lax
from jax.experimental import pallas as pl
from jax.experimental.pallas import tpu as pltpu
from jax.sharding import PartitionSpec as P

H = 12
HD = 64
PAIR = 2 * HD
GROUP = 2
EPS = 1e-05
NEG = -1e30
BASE = 128.0
DIGITS = 3
LANES = 128
FLOAT = jnp.float32
BFLOAT = jnp.bfloat16
VMEM_BYTES = 60 * 1024 * 1024


def params(**kw):
    return pltpu.CompilerParams(vmem_limit_bytes=VMEM_BYTES, **kw)


def cost(flops, moved):
    return pl.CostEstimate(flops=int(flops / 100), transcendentals=0, bytes_accessed=int(moved / 100))


def padded_len(frame_len):
    return -(-(frame_len + 1) // 8) * 8


def whole(shape):
    return pl.BlockSpec(shape, lambda *_: (0,) * len(shape), pipeline_mode=pl.Buffered(1))


def rows_of(height, width, first=0):
    return pl.BlockSpec((height, width), lambda i: (i + first, 0))


def frames_of(pad, width, first=0):
    return pl.BlockSpec((GROUP, pad, width), lambda i: (i + first, 0, 0))


def normalize(values):
    center = values - jnp.mean(values, axis=-1, keepdims=True)
    spread = jnp.mean(center * center, axis=-1, keepdims=True)
    scale_inv = lax.rsqrt(spread + EPS)
    return (center * scale_inv, scale_inv)


def norm_back(grad_normed, normed, scale_inv):
    return scale_inv * (
        grad_normed
        - jnp.mean(grad_normed, axis=-1, keepdims=True)
        - normed * jnp.mean(grad_normed * normed, axis=-1, keepdims=True)
    )


def dot(a, b):
    return jnp.dot(a, b, preferred_element_type=FLOAT)


def dot_nt(a, b):
    return lax.dot_general(a, b, (((1,), (1,)), ((), ())), preferred_element_type=FLOAT)


def dot_tn(a, b):
    return lax.dot_general(a, b, (((0,), (0,)), ((), ())), preferred_element_type=FLOAT)


def load_rows(ref, frame_len):
    values = ref[...].astype(FLOAT)
    count, pad, width = values.shape
    row = lax.broadcasted_iota(jnp.int32, values.shape, 1)
    return jnp.where(row < frame_len, values, 0.0).reshape(count * pad, width)


def project_kernel(frame_len, x_ref, gain_ref, w_ref, proj_ref):
    normed, _ = normalize(load_rows(x_ref, frame_len))
    hidden = (normed * gain_ref[...]).astype(BFLOAT)
    width = hidden.shape[1]
    for part in range(3):
        cols = slice(part * width, (part + 1) * width)
        proj_ref[:, cols] = dot(hidden, w_ref[:, cols]).astype(BFLOAT)


def alias_call(
    kernel, grid, in_specs, args, prior, out_specs, out_shape, name, flops, moved, scratch=()
):
    extra = [] if prior is None else list(prior)

    def body(*refs):
        kernel(*refs[: len(args)], *refs[len(args) + len(extra) :])

    return pl.pallas_call(
        body,
        grid=grid,
        in_specs=in_specs + [pl.BlockSpec(memory_space=pl.ANY)] * len(extra),
        out_specs=out_specs,
        out_shape=out_shape,
        input_output_aliases={len(args) + i: i for i in range(len(extra))},
        scratch_shapes=list(scratch),
        compiler_params=params(),
        cost_estimate=cost(flops, moved),
        name=name,
    )(*args, *extra)


def project(frames_in, gain, qkv, first, steps, prior):
    count, frame_len, width = frames_in.shape
    pad = padded_len(frame_len)
    block = GROUP * pad
    return alias_call(
        functools.partial(project_kernel, frame_len),
        (steps,),
        [frames_of(pad, width, first), whole((width,)), whole(qkv.shape)],
        (frames_in, gain, qkv),
        prior,
        [rows_of(block, 3 * width, first)],
        [jax.ShapeDtypeStruct((count * pad, 3 * width), BFLOAT)],
        "project",
        6 * steps * block * width * width,
        8 * steps * block * width,
    )


def last_rows(rows, change):
    cut = rows.shape[0] - 8
    return jnp.concatenate([rows[:cut], change(rows[cut:], cut)], axis=0)


def token_in(rows, token, frame_len):
    def change(tail, cut):
        row = lax.broadcasted_iota(jnp.int32, tail.shape, 0)
        return jnp.where(row == frame_len - cut, token, tail)

    return last_rows(rows, change)


def one_head(pair, h):
    lane = lax.broadcasted_iota(jnp.int32, pair.shape, 1)
    return jnp.where((lane >= HD) == (h == 1), pair, jnp.zeros_like(pair))


def attend_kernel(
    frame_len, x_ref, proj_ref, token_ref, out_w_ref, expo_ref, mixed_ref, scale_ref, res_ref
):
    width = x_ref.shape[2]
    pad = x_ref.shape[1]
    pairs = width // PAIR

    def hide(tail, cut):
        row = lax.broadcasted_iota(jnp.int32, tail.shape, 0)
        return jnp.where(row <= frame_len - cut, tail, NEG)

    def at(part, j):
        return pl.ds(part * width + j * PAIR, PAIR)

    def weigh(f, j):
        rows = pl.ds(f * pad, pad)
        query = proj_ref[rows, at(0, j)] * 0.125
        key = token_in(proj_ref[rows, at(1, j)], token_ref[f, :, at(0, j)], frame_len)
        for h in range(2):
            scores = last_rows(dot_nt(one_head(key, h), query), hide)
            expo = jnp.exp(scores - jnp.max(scores, axis=0, keepdims=True)).astype(BFLOAT)
            expo_ref[f, 2 * j + h] = expo

    def mix(f, j):
        rows = pl.ds(f * pad, pad)
        value = token_in(proj_ref[rows, at(2, j)], token_ref[f, :, at(1, j)], frame_len)
        value_t = value.astype(FLOAT).T.astype(BFLOAT)
        outs = []
        for h in range(2):
            ones = jnp.ones((8, pad), BFLOAT)
            out = dot(jnp.concatenate([value_t[h * HD : (h + 1) * HD], ones]), expo_ref[f, 2 * j + h])
            scale = 1.0 / out[HD : HD + 1]
            outs.append(out[:HD] * scale)
            scale_ref[f, 2 * j + h : 2 * j + h + 1, :] = scale
        mixed_ref[rows, at(0, j)] = jnp.concatenate(outs, axis=0).T.astype(BFLOAT)

    units = [(f, j) for j in range(pairs) for f in range(GROUP)]
    for i in range(len(units) + 2):
        if i < len(units):
            weigh(*units[i])
        if i >= 2:
            mix(*units[i - 2])
    residual = load_rows(x_ref, frame_len) + dot(mixed_ref[...], out_w_ref[...])
    res_ref[...] = residual.astype(BFLOAT)


def attend(frames_in, proj, token_kv, out_w):
    count, frame_len, width = frames_in.shape
    pad = padded_len(frame_len)
    block = GROUP * pad
    heads = width // HD
    return pl.pallas_call(
        functools.partial(attend_kernel, frame_len),
        grid=(count // GROUP,),
        in_specs=[
            frames_of(pad, width),
            rows_of(block, 3 * width),
            frames_of(1, 2 * width),
            whole(out_w.shape),
        ],
        out_specs=[
            pl.BlockSpec((GROUP, heads, pad, pad), lambda i: (i, 0, 0, 0)),
            rows_of(block, width),
            frames_of(heads, pad),
            rows_of(block, width),
        ],
        out_shape=[
            jax.ShapeDtypeStruct((count, heads, pad, pad), BFLOAT),
            jax.ShapeDtypeStruct((count * pad, width), BFLOAT),
            jax.ShapeDtypeStruct((count, heads, pad), FLOAT),
            jax.ShapeDtypeStruct((count * pad, width), BFLOAT),
        ],
        compiler_params=params(),
        cost_estimate=cost(25e9, 50e6),
        name="attend",
    )(frames_in, proj, token_kv, out_w)


def mlp_kernel(
    frame_len,
    parts,
    res_ref,
    cot_ref,
    gain_ref,
    up_ref,
    down_ref,
    out_w_ref,
    mixed_ref,
    scale_ref,
    cot_rows_ref,
    second_ref,
    act_ref,
    grad_up_ref,
    branch_ref,
    grad_mixed_ref,
    delta_ref,
    gain_grad_ref,
):
    residual = res_ref[...].astype(FLOAT)
    width = residual.shape[1]
    normed, scale_inv = normalize(residual)
    gain = gain_ref[...]
    second = (normed * gain).astype(BFLOAT)
    second_ref[...] = second
    cot = load_rows(cot_ref, frame_len)
    cot_bf = cot.astype(BFLOAT)
    cot_rows_ref[...] = cot_bf
    grad_second = jnp.zeros_like(residual)
    size = up_ref.shape[1] // parts
    for part in range(parts):
        cols = slice(part * size, (part + 1) * size)
        up_part = dot(second, up_ref[:, cols])
        sigma = 0.5 * jnp.tanh(0.851 * up_part) + 0.5
        gated = up_part * sigma
        act = gated.astype(BFLOAT)
        act_ref[:, cols] = act
        grad_act = dot_nt(cot_bf, down_ref[cols, :])
        grad_up = (grad_act * (sigma + 1.702 * gated * (1.0 - sigma))).astype(BFLOAT)
        grad_up_ref[:, cols] = grad_up
        grad_second = grad_second + dot_nt(grad_up, up_ref[:, cols])
    gain_grad = jnp.sum(grad_second * normed, axis=0, keepdims=True)
    step = pl.program_id(0)
    gain_grad_ref[...] = jnp.where(step == 0, 0.0, gain_grad_ref[...]) + gain_grad
    branch = (cot + norm_back(grad_second * gain, normed, scale_inv)).astype(BFLOAT)
    branch_ref[...] = branch
    heads, pad = delta_ref.shape[1:]
    head = lax.broadcasted_iota(jnp.int32, (heads, width), 0)
    lane = lax.broadcasted_iota(jnp.int32, (heads, width), 1)
    of_head = (lane // HD == head).astype(FLOAT)
    scales = []
    for f in range(GROUP):
        high = scale_ref[f].astype(BFLOAT).astype(FLOAT)
        rows = jnp.concatenate([high, scale_ref[f] - high]).astype(BFLOAT)
        scales.append(dot_tn(rows, jnp.concatenate([of_head, of_head]).astype(BFLOAT)))
    of_head = of_head.astype(BFLOAT)
    grad_mixed = dot_nt(branch, out_w_ref[...]) * jnp.concatenate(scales)
    grad_mixed = grad_mixed.astype(BFLOAT)
    grad_mixed_ref[...] = grad_mixed
    product = grad_mixed * mixed_ref[...]
    for f in range(GROUP):
        delta_ref[f] = dot_nt(of_head, product[f * pad : (f + 1) * pad])


def mlp(residual, cotangent, gain, up, down, out_w, mixed, scale):
    count, frame_len, width = cotangent.shape
    pad = padded_len(frame_len)
    block = GROUP * pad
    rows = count * pad
    heads = width // HD
    hidden = up.shape[1]
    shape = jax.ShapeDtypeStruct
    return pl.pallas_call(
        functools.partial(mlp_kernel, frame_len, 4),
        grid=(count // GROUP,),
        in_specs=[
            rows_of(block, width),
            frames_of(pad, width),
            whole((width,)),
            whole(up.shape),
            whole(down.shape),
            whole(out_w.shape),
            rows_of(block, width),
            frames_of(heads, pad),
        ],
        out_specs=[
            rows_of(block, width),
            rows_of(block, width),
            rows_of(block, hidden),
            rows_of(block, hidden),
            rows_of(block, width),
            rows_of(block, width),
            pl.BlockSpec((GROUP, heads, pad), lambda i: (i, 0, 0)),
            pl.BlockSpec((1, width), lambda i: (0, 0)),
        ],
        out_shape=[
            shape((rows, width), BFLOAT),
            shape((rows, width), BFLOAT),
            shape((rows, hidden), BFLOAT),
            shape((rows, hidden), BFLOAT),
            shape((rows, width), BFLOAT),
            shape((rows, width), BFLOAT),
            shape((count, heads, pad), FLOAT),
            shape((1, width), FLOAT),
        ],
        compiler_params=params(),
        cost_estimate=cost(6 * rows * width * hidden, 60e6),
        name="mlp",
    )(residual, cotangent, gain, up, down, out_w, mixed, scale)


def output_kernel(res_ref, act_ref, down_ref, output_ref):
    out = res_ref[...].astype(FLOAT) + dot(act_ref[...], down_ref[...])
    output_ref[...] = out.astype(BFLOAT).reshape(output_ref.shape)


def mlp_output(residual, act, down, shape, first, steps, prior):
    count, frame_len, width = shape
    pad = padded_len(frame_len)
    block = GROUP * pad
    hidden = down.shape[0]
    return alias_call(
        output_kernel,
        (steps,),
        [rows_of(block, width, first), rows_of(block, hidden, first), whole(down.shape)],
        (residual, act, down),
        prior,
        [frames_of(pad, width, first)],
        [jax.ShapeDtypeStruct(shape, BFLOAT)],
        "mlp_output",
        2 * steps * block * width * hidden,
        8 * steps * block * width,
    )


def weight_grad_kernel(core_ref, left_ref, right_ref, *refs):
    send_ref, keep_ref = refs[-2:]
    total = dot_tn(left_ref[...], right_ref[...]).astype(BFLOAT)
    step = pl.program_id(0)

    @pl.when(step < 2)
    def _():
        send_ref[0] = total

    @pl.when(step >= 2)
    def _():
        keep_ref[0] = total


def up_grad(core, left, right, parts, prior):
    rows, width = left.shape
    lanes = right.shape[1] // parts

    def block(i, core_ref):
        return 2 * (i % 2) + jnp.where(i < 2, 1 - core_ref[0], core_ref[0])

    return pl.pallas_call(
        weight_grad_kernel,
        grid_spec=pltpu.PrefetchScalarGridSpec(
            num_scalar_prefetch=1,
            grid=(parts,),
            in_specs=[
                pl.BlockSpec(left.shape, lambda i, c: (0, 0), pipeline_mode=pl.Buffered(1)),
                pl.BlockSpec((rows, lanes), lambda i, c: (0, block(i, c))),
                pl.BlockSpec(memory_space=pl.ANY),
                pl.BlockSpec(memory_space=pl.ANY),
            ],
            out_specs=[
                pl.BlockSpec((1, width, lanes), lambda i, c: (jnp.minimum(i, 1), 0, 0)),
                pl.BlockSpec((1, width, lanes), lambda i, c: (jnp.maximum(i - 2, 0), 0, 0)),
            ],
        ),
        out_shape=[jax.ShapeDtypeStruct(p.shape, BFLOAT) for p in prior],
        input_output_aliases={3: 0, 4: 1},
        compiler_params=params(),
        cost_estimate=cost(2 * left.size * right.shape[1], 2 * (left.size + right.size)),
        name="grad_up",
    )(core, left, right, *prior)


def by_core(core, blocks):
    pairs = [(blocks[2 * y], blocks[2 * y + 1]) for y in range(len(blocks) // 2)]
    first = core == 0
    send = [jnp.where(first, odd, even) for even, odd in pairs]
    return send, [jnp.where(first, even, odd) for even, odd in pairs]


def down_grad_kernel(core_ref, left_ref, right_ref, send_ref, keep_ref):
    total = dot_tn(left_ref[...], right_ref[...]).astype(BFLOAT)
    parts, pieces, height, columns = 2 * send_ref.shape[0], *send_ref.shape[1:]
    for piece in range(pieces):
        cols = slice(piece * columns, (piece + 1) * columns)
        blocks = [total[part * height : (part + 1) * height, cols] for part in range(parts)]
        for ref, values in zip((send_ref, keep_ref), by_core(core_ref[0], blocks)):
            for y, value in enumerate(values):
                ref[y, piece] = value


def down_grad(core, left, right, parts, tile):
    rows, width = left.shape
    tiles = right.shape[1] // tile
    shape = (parts // 2, tiles, width // parts, tile)
    spec = pl.BlockSpec((parts // 2, 2, width // parts, tile), lambda i: (0, i, 0, 0))
    return pl.pallas_call(
        down_grad_kernel,
        grid=(tiles // 2,),
        in_specs=[
            pl.BlockSpec(memory_space=pltpu.SMEM),
            whole(left.shape),
            pl.BlockSpec((rows, 2 * tile), lambda i: (0, i)),
        ],
        out_specs=[spec, spec],
        out_shape=[jax.ShapeDtypeStruct(shape, BFLOAT)] * 2,
        compiler_params=params(),
        cost_estimate=cost(2 * left.size * right.shape[1], 2 * (left.size + right.size)),
        name="grad_down",
    )(core, left, right)


def with_gain(block, gain, lanes):
    column = jnp.broadcast_to(gain, (8, gain.shape[1])).T.astype(BFLOAT)
    blank = jnp.zeros((block.shape[0], lanes - block.shape[1] - 8), BFLOAT)
    return jnp.concatenate([block, column, blank], axis=1)


def store_split(core, total_ref, gain, send_refs, keep_refs):
    halves = send_refs[0].shape[0]
    parts = 2 * halves
    size = total_ref.shape[1] // parts
    lanes = sum(ref.shape[2] for ref in send_refs)
    for y in range(halves):
        blocks = [
            with_gain(total_ref[:, part * size : (part + 1) * size].astype(BFLOAT), gain, lanes)
            for part in (2 * y, 2 * y + 1)
        ]
        for refs, (value,) in zip((send_refs, keep_refs), by_core(core, blocks)):
            offset = 0
            for ref in refs:
                ref[y] = value[:, offset : offset + ref.shape[2]]
                offset += ref.shape[2]


def split_grad_kernel(core_ref, left_ref, right_ref, gain_ref, send_ref, keep_ref, all_ref):
    step = pl.program_id(0)
    tile = right_ref.shape[1]
    all_ref[:, pl.ds(pl.multiple_of(step * tile, tile), tile)] = dot_tn(
        left_ref[...], right_ref[...]
    ).astype(BFLOAT)

    @pl.when(step == pl.num_programs(0) - 1)
    def _():
        store_split(core_ref[0], all_ref, gain_ref[...], [send_ref], [keep_ref])


def split_grad(core, left, right, gain, tile, parts, shape, index, name):
    rows, width = left.shape
    columns = right.shape[1]
    size = -(-columns // parts // LANES) * LANES
    spec = pl.BlockSpec((parts // 2, width, size), lambda i: (0, 0, index))
    return pl.pallas_call(
        split_grad_kernel,
        grid=(columns // tile,),
        in_specs=[
            pl.BlockSpec(memory_space=pltpu.SMEM),
            whole(left.shape),
            pl.BlockSpec((rows, tile), lambda i: (0, i)),
            whole(gain.shape),
        ],
        out_specs=[spec, spec],
        out_shape=[jax.ShapeDtypeStruct(shape, BFLOAT)] * 2,
        scratch_shapes=[pltpu.VMEM((width, columns), BFLOAT)],
        compiler_params=params(),
        cost_estimate=cost(2 * left.size * columns, 2 * (left.size + right.size)),
        name=name,
    )(core, left, right, gain)


def attend_back_kernel(
    frame_len,
    core_ref,
    proj_ref,
    token_ref,
    expo_ref,
    grad_mixed_ref,
    delta_ref,
    x_ref,
    branch_ref,
    message_ref,
    gain_ref,
    w_ref,
    grad_in_ref,
    class_ref,
    message_grad_ref,
    send_0_ref,
    send_1_ref,
    keep_0_ref,
    keep_1_ref,
    scores_ref,
    grad_proj_ref,
    total_ref,
    gain_grad_ref,
):
    pad = expo_ref.shape[2]
    width = grad_mixed_ref.shape[1]
    pairs = width // PAIR
    step = pl.program_id(0)

    @pl.when(step == 0)
    def _():
        total_ref[...] = jnp.zeros_like(total_ref)
        gain_grad_ref[...] = jnp.zeros_like(gain_grad_ref)

    def at(part, j):
        return pl.ds(part * width + j * PAIR, PAIR)

    def weigh(f, j):
        rows = pl.ds(f * pad, pad)
        value = token_in(proj_ref[rows, at(2, j)], token_ref[f, :, at(1, j)], frame_len)
        grad = grad_mixed_ref[rows, at(0, j)]
        for h in range(2):
            head = 2 * j + h
            grad_prob = dot_nt(one_head(value, h), grad) - delta_ref[f, head : head + 1, :]
            scores_ref[f, head] = expo_ref[f, head] * grad_prob.astype(BFLOAT)

    def mix(f, j):
        rows = pl.ds(f * pad, pad)
        query = proj_ref[rows, at(0, j)]
        key = token_in(proj_ref[rows, at(1, j)], token_ref[f, :, at(0, j)], frame_len)
        grad = grad_mixed_ref[rows, at(0, j)]
        key_t = key.astype(FLOAT).T.astype(BFLOAT)
        grad_query, grad_key, grad_value = [], [], []
        for h in range(2):
            scores = scores_ref[f, 2 * j + h]
            grad_value.append(dot(expo_ref[f, 2 * j + h], one_head(grad, h)))
            grad_key.append(dot(scores, one_head(query, h)))
            grad_query.append(dot(key_t[h * HD : (h + 1) * HD], scores))
        grad_query = jnp.concatenate(grad_query, axis=0).T * 0.125
        grad_proj_ref[rows, at(0, j)] = grad_query.astype(BFLOAT)
        grad_key = (grad_key[0] + grad_key[1]) * 0.125
        grad_proj_ref[rows, at(1, j)] = grad_key.astype(BFLOAT)
        grad_value = grad_value[0] + grad_value[1]
        grad_proj_ref[rows, at(2, j)] = grad_value.astype(BFLOAT)

    units = [(f, j) for j in range(pairs) for f in range(GROUP)]
    for i in range(len(units) + 2):
        if i < len(units):
            weigh(*units[i])
        if i >= 2:
            mix(*units[i - 2])

    values = load_rows(x_ref, frame_len)
    values = jnp.concatenate(
        [
            token_in(values[f * pad : (f + 1) * pad], message_ref[f].astype(FLOAT), frame_len)
            for f in range(GROUP)
        ]
    )
    normed, scale_inv = normalize(values)
    hidden = (normed * gain_ref[...]).astype(BFLOAT)
    for part in range(3):
        cols = slice(part * width, (part + 1) * width)
        total_ref[:, cols] += dot_tn(hidden, grad_proj_ref[:, cols])
    grad = dot_nt(grad_proj_ref[...], w_ref[...])
    gain_grad_ref[...] += jnp.sum(grad * normed, axis=0, keepdims=True)
    total = branch_ref[...].astype(FLOAT) + norm_back(grad * gain_ref[...], normed, scale_inv)
    total = total.reshape(GROUP, pad, width)
    grad_in_ref[...] = total.astype(BFLOAT)
    for f in range(GROUP):
        class_ref[f] = total[f, :1]
        message_grad_ref[f] = total[f, frame_len : frame_len + 1].astype(BFLOAT)

    @pl.when(step == pl.num_programs(0) - 1)
    def _():
        store_split(
            core_ref[0],
            total_ref,
            gain_grad_ref[...],
            [send_0_ref, send_1_ref],
            [keep_0_ref, keep_1_ref],
        )


def attend_back(
    core, proj, token_kv, expo, grad_mixed, delta, frames_in, branch, message, gain, qkv, parts
):
    count, heads, pad, _ = expo.shape
    frame_len, width = frames_in.shape[1:]
    block = GROUP * pad
    lanes = -(-3 * width // parts // LANES) * LANES
    first = lanes // (2 * LANES) * LANES + LANES
    sums = [(parts // 2, width, n) for n in (first, lanes - first)] * 2
    shape = jax.ShapeDtypeStruct
    return pl.pallas_call(
        functools.partial(attend_back_kernel, frame_len),
        grid=(count // GROUP,),
        in_specs=[
            pl.BlockSpec(memory_space=pltpu.SMEM),
            rows_of(block, 3 * width),
            frames_of(1, 2 * width),
            pl.BlockSpec((GROUP, heads, pad, pad), lambda i: (i, 0, 0, 0)),
            rows_of(block, width),
            pl.BlockSpec((GROUP, heads, pad), lambda i: (i, 0, 0)),
            frames_of(pad, width),
            rows_of(block, width),
            frames_of(1, width),
            whole((width,)),
            whole(qkv.shape),
        ],
        out_specs=[frames_of(pad, width), frames_of(1, width), frames_of(1, width)]
        + [whole(s) for s in sums],
        out_shape=[
            shape((count, frame_len, width), BFLOAT),
            shape((count, 1, width), FLOAT),
            shape((count, 1, width), BFLOAT),
        ]
        + [shape(s, BFLOAT) for s in sums],
        scratch_shapes=[
            pltpu.VMEM((GROUP, heads, pad, pad), BFLOAT),
            pltpu.VMEM((block, 3 * width), BFLOAT),
            pltpu.VMEM((width, 3 * width), FLOAT),
            pltpu.VMEM((1, width), FLOAT),
        ],
        compiler_params=params(),
        cost_estimate=cost(45e9, 50e6),
        name="attend_back",
    )(core, proj, token_kv, expo, grad_mixed, delta, frames_in, branch, message, gain, qkv)


def in_turn(count, slots, first, second):
    if slots > 256:

        def both(j, carry):
            first(j)
            second(j)
            return carry

        lax.fori_loop(0, count, both, 0)
        return
    for j in range(count + 2):
        if j < count:
            first(j)
        if j >= 2:
            second(j - 2)


def message_kernel(
    own,
    pieces,
    *refs,
):
    gathered = jnp.concatenate([ref[...] for ref in refs[:pieces]])
    message_body(own, gathered, *refs[pieces:])


def message_body(
    own,
    gathered,
    weight_ref,
    gain_ref,
    qkv_ref,
    out_w_ref,
    attn_gain_ref,
    key_w_ref,
    value_w_ref,
    class_ref,
    start_ref,
    hidden_ref,
    proj_ref,
    prob_ref,
    mixed_ref,
    message_ref,
    token_kv_ref,
):
    width = weight_ref.shape[0]
    class_ref[...] = gathered[:, :width]
    start = dot(gathered[:, :width], weight_ref[...]).astype(BFLOAT)
    start_ref[...] = start
    normed, _ = normalize(start.astype(FLOAT))
    hidden = (normed * gain_ref[...]).astype(BFLOAT)
    hidden_ref[...] = hidden
    proj_ref[...] = dot(hidden, qkv_ref[...]).astype(BFLOAT)
    digits = gathered[:, width:].astype(FLOAT)
    lane = lax.broadcasted_iota(jnp.int32, digits.shape, 1)
    weights = jnp.where(lane == 0, 1.0, jnp.where(lane == 1, BASE, BASE * BASE))
    digits = jnp.where(lane < DIGITS, digits * weights, 0.0)
    id_col = jnp.sum(digits, axis=1, keepdims=True)
    id_row = jnp.sum(digits.T, axis=0, keepdims=True)
    visible = id_col == id_row

    def at(part, j):
        start = part * width + j * PAIR
        return pl.ds(start if isinstance(j, int) else pl.multiple_of(start, PAIR), PAIR)

    def weigh(j):
        query = proj_ref[:, at(0, j)] * 0.125
        for h in range(2):
            scores = jnp.where(visible, dot_nt(proj_ref[:, at(1, j)], one_head(query, h)), NEG)
            expo = jnp.exp(scores - jnp.max(scores, axis=0, keepdims=True))
            prob = expo * (1.0 / jnp.sum(expo, axis=0, keepdims=True))
            prob_ref[2 * j + h] = prob.astype(BFLOAT)

    def mix(j):
        value_t = proj_ref[:, at(2, j)].astype(FLOAT).T.astype(BFLOAT)
        outs = [dot(value_t[h * HD : (h + 1) * HD], prob_ref[2 * j + h]) for h in range(2)]
        mixed_ref[:, at(0, j)] = jnp.concatenate(outs, axis=0).T.astype(BFLOAT)

    in_turn(width // PAIR, start.shape[0], weigh, mix)
    message = start[:own].astype(FLOAT) + dot(mixed_ref[:own, :], out_w_ref[...])
    message = message.astype(BFLOAT)
    message_ref[...] = message
    normed, _ = normalize(message.astype(FLOAT))
    token_hidden = (normed * attn_gain_ref[...]).astype(BFLOAT)
    token_kv_ref[:, :width] = dot(token_hidden, key_w_ref[...]).astype(BFLOAT)
    token_kv_ref[:, width:] = dot(token_hidden, value_w_ref[...]).astype(BFLOAT)


def message_forward(class_parts, own, weight, gain, qkv, out_w, attn_gain, attn_qkv):
    slots = sum(part.shape[0] for part in class_parts)
    width = weight.shape[0]
    heads = width // HD
    shape = jax.ShapeDtypeStruct
    part = lambda index: pl.BlockSpec((width, width), lambda i, index=index: (0, index))
    return pl.pallas_call(
        functools.partial(message_kernel, own, len(class_parts)),
        grid=(1,),
        in_specs=[whole(p.shape) for p in class_parts]
        + [
            whole(weight.shape),
            whole((width,)),
            whole(qkv.shape),
            whole(out_w.shape),
            whole((width,)),
            part(1),
            part(2),
        ],
        out_specs=[
            whole((slots, width)),
            whole((slots, width)),
            whole((slots, width)),
            whole((slots, 3 * width)),
            whole((heads, slots, slots)),
            whole((slots, width)),
            whole((own, width)),
            whole((own, 2 * width)),
        ],
        out_shape=[
            shape((slots, width), BFLOAT),
            shape((slots, width), BFLOAT),
            shape((slots, width), BFLOAT),
            shape((slots, 3 * width), BFLOAT),
            shape((heads, slots, slots), BFLOAT),
            shape((slots, width), BFLOAT),
            shape((own, width), BFLOAT),
            shape((own, 2 * width), BFLOAT),
        ],
        compiler_params=params(),
        cost_estimate=cost(7e9, 9e6),
        name="message_forward",
    )(
        *class_parts,
        weight,
        gain,
        qkv,
        out_w,
        attn_gain,
        attn_qkv,
        attn_qkv,
    )


def message_back_kernel(
    own,
    parts,
    together,
    pieces,
    block_ref,
    *refs,
):
    grad = jnp.concatenate([ref[...] for ref in refs[:pieces]])
    message_back_body(own, parts, together, block_ref, grad, *refs[pieces:])


def message_back_body(
    own,
    parts,
    together,
    block_ref,
    grad,
    class_ref,
    start_ref,
    hidden_ref,
    proj_ref,
    prob_ref,
    mixed_ref,
    weight_ref,
    gain_ref,
    qkv_ref,
    out_w_ref,
    class_grad_ref,
    sums_ref,
    grad_mixed_ref,
    grad_proj_ref,
    scores_ref,
):
    width = weight_ref.shape[0]
    j = pl.program_id(0)

    @pl.when(j == 0)
    def _():
        grad_mixed_ref[...] = dot_nt(grad, out_w_ref[...]).astype(BFLOAT)

    def finish():
        grad_proj = grad_proj_ref[...]
        grad_hidden = dot_nt(grad_proj, qkv_ref[...])
        normed, scale_inv = normalize(start_ref[...].astype(FLOAT))
        gain_grad = jnp.sum(grad_hidden * normed, axis=0, keepdims=True)
        back = norm_back(grad_hidden * gain_ref[...], normed, scale_inv)
        start_grad = (grad.astype(FLOAT) + back).astype(BFLOAT)
        class_grad_ref[...] = dot_nt(start_grad[:own], weight_ref[...])
        size = sums_ref.shape[1]
        row = lax.broadcasted_iota(jnp.int32, (size, width), 0)
        column = lax.broadcasted_iota(jnp.int32, (size, width), 1)
        mine = column == row + block_ref[0] * size
        pick = mine.astype(BFLOAT)
        gain_grad = jnp.sum(jnp.where(mine, gain_grad, 0.0), axis=1, keepdims=True)
        lanes = sums_ref.shape[2] - 5 * width // parts
        for part in range(parts):
            sums_ref[part, :, 5 * width // parts :] = jnp.broadcast_to(
                gain_grad, (size, lanes)
            ).astype(BFLOAT)
        offset = 0
        for left, right in (
            (hidden_ref[...], grad_proj),
            (class_ref[:, :width], start_grad),
            (mixed_ref[...], grad),
        ):
            total = dot(dot_nt(pick, left).astype(BFLOAT), right).astype(BFLOAT)
            columns = total.shape[1] // parts
            for part in range(parts):
                sums_ref[part, :, offset : offset + columns] = total[
                    :, part * columns : (part + 1) * columns
                ]
            offset += columns

    def at(part, k):
        if together == 1:
            return pl.ds(pl.multiple_of(part * width + j * PAIR, PAIR), PAIR)
        return pl.ds(part * width + k * PAIR, PAIR)

    def weigh(k):
        value = proj_ref[:, at(2, k)]
        for h in range(2):
            grad_prob = dot_nt(value, one_head(grad_mixed_ref[:, at(0, k)], h))
            prob = prob_ref[2 * k + h].astype(FLOAT)
            part = prob * grad_prob
            scores = part - prob * jnp.sum(part, axis=0, keepdims=True)
            scores_ref[2 * k + h] = scores.astype(BFLOAT)

    def mix(k):
        query, key, grad_m = proj_ref[:, at(0, k)], proj_ref[:, at(1, k)], grad_mixed_ref[:, at(0, k)]
        key_t = key.astype(FLOAT).T.astype(BFLOAT)
        grad_query, grad_key, grad_value = [], [], []
        for h in range(2):
            scores = scores_ref[2 * k + h]
            grad_value.append(dot(prob_ref[2 * k + h], one_head(grad_m, h)))
            grad_key.append(dot(scores, one_head(query, h)))
            grad_query.append(dot(key_t[h * HD : (h + 1) * HD], scores))
        grad_query = jnp.concatenate(grad_query, axis=0).T * 0.125
        grad_proj_ref[:, at(0, k)] = grad_query.astype(BFLOAT)
        grad_proj_ref[:, at(1, k)] = ((grad_key[0] + grad_key[1]) * 0.125).astype(BFLOAT)
        grad_proj_ref[:, at(2, k)] = (grad_value[0] + grad_value[1]).astype(BFLOAT)

    if together == 1:
        weigh(0)
        mix(0)
    else:
        in_turn(together, grad.shape[0], weigh, mix)

    @pl.when(j == pl.num_programs(0) - 1)
    def _():
        finish()


def message_back(block, parts, size, own, grad_parts, saved, weight, gain, qkv, out_w):
    class_all, start, hidden, proj, prob, mixed = saved
    slots, width = class_all.shape
    shape = jax.ShapeDtypeStruct
    sums = (parts, size, -(-(5 * width // parts + 1) // LANES) * LANES)
    together = width // PAIR if slots <= 256 else 1
    args = (*grad_parts, class_all, start, hidden, proj, prob, mixed, weight, gain, qkv, out_w)
    return pl.pallas_call(
        functools.partial(message_back_kernel, own, parts, together, len(grad_parts)),
        grid=(width // PAIR // together,),
        in_specs=[pl.BlockSpec(memory_space=pltpu.SMEM)]
        + [pl.BlockSpec((2 * together, slots, slots), lambda j: (j, 0, 0)) if a is prob else whole(a.shape) for a in args],
        out_specs=[whole((own, width)), whole(sums)],
        out_shape=[shape((own, width), FLOAT), shape(sums, BFLOAT)],
        scratch_shapes=[
            pltpu.VMEM((slots, width), BFLOAT),
            pltpu.VMEM((slots, 3 * width), BFLOAT),
            pltpu.VMEM((2 * together, slots, slots), BFLOAT),
        ],
        compiler_params=params(),
        cost_estimate=cost(8e9, 9e6),
        name="message_back",
    )(block, *args)


def swap(values, axis, distance):
    return lax.ppermute(values, axis, [(i, i ^ distance) for i in range(lax.axis_size(axis))])


def tied(values, *others):
    return lax.optimization_barrier((values, others))[0]


def meet(outputs, *transfers):
    outputs, got = lax.optimization_barrier((outputs, [transfer.got for transfer in transfers]))
    for transfer, values in zip(transfers, got):
        transfer.got = values
    return outputs


def pick(values, index, axis=0, window=None):
    starts, sizes = [0] * values.ndim, list(values.shape)
    starts[axis], sizes[axis] = index, 1
    if window is not None:
        starts[window[0]], sizes[window[0]] = window[1:]
    return lax.squeeze(lax.dynamic_slice(values, starts, sizes), (axis,))


def add(*terms):
    total = terms[0].astype(FLOAT)
    for term in terms[1:]:
        total = total + term.astype(FLOAT)
    return total


class Gather:
    def __init__(self, axis, values):
        self.axis, self.values = axis, values
        self.distance, self.left = 1, lax.axis_size(axis)

    def begin(self, direct=True):
        while self.left > 8:
            self.finish(self.start(2))
        self.got = self.start(self.left if direct and self.left < 8 else 2)

    def start(self, size):
        got = [swap(self.values, self.axis, d * self.distance) for d in range(1, size)]
        self.distance, self.left = self.distance * size, self.left // size
        return got

    def finish(self, got):
        self.pieces = [self.values, *got]
        self.values = jnp.concatenate(self.pieces)

    def end(self):
        self.finish(self.got)
        return self.values


class Sum:
    def __init__(self, terms):
        self.terms = terms

    @classmethod
    def of_cores(cls, sent, kept):
        self = cls([kept])
        self.sent = sent
        self.got = [swap(sent, "rows", 1)]
        return self

    def part(self, index):
        return Sum([term[index] for term in self.terms])

    def total(self):
        return add(*self.terms)

    def begin(self, axis, distance, dim, window=None):
        bit = (lax.axis_index(axis) // distance) % 2
        sent = add(*(pick(term, 1 - bit, dim, window) for term in self.terms)).astype(BFLOAT)
        self.terms = [pick(term, bit, dim, window) for term in self.terms]
        self.got = [swap(sent, axis, distance)]
        return sent

    def end(self, apart=False):
        self.terms = self.got + self.terms
        if not apart:
            self.terms = [self.total().astype(BFLOAT)]

    def begin_frames(self, dim=0):
        self.left, self.distance, self.dim = lax.axis_size("frames"), 1, dim
        shape = self.terms[0].shape
        if len(shape) == 2 + dim:
            shape = (*shape[:dim], self.left, -1, shape[-1])
            self.terms = [term.reshape(shape) for term in self.terms]
        while self.left > 8:
            self.step_frames()
            self.end()
        return self.step_frames()

    def step_frames(self):
        shape, dim = self.terms[0].shape, self.dim
        shape = (*shape[:dim], self.left // 2, 2, *shape[dim + 1 :])
        self.terms = [term.reshape(shape) for term in self.terms]
        sent = self.begin("frames", self.distance, dim + 1)
        self.left, self.distance = self.left // 2, self.distance * 2
        return sent

    def begin_last(self):
        index = lax.axis_index("frames") // self.distance
        sent = [
            add(*(pick(term, index ^ d) for term in self.terms)).astype(BFLOAT)
            for d in range(1, self.left)
        ]
        self.terms = [pick(term, index) for term in self.terms]
        self.got = [
            swap(block, "frames", (d + 1) * self.distance) for d, block in enumerate(sent)
        ]
        return sent


def joined(first, second, axis):
    self = Sum([jnp.concatenate([first.total(), second.total()], axis=axis).astype(BFLOAT)])
    if hasattr(first, "left"):
        self.left, self.distance, self.dim = first.left, first.distance, first.dim
    return self


def per_device(
    frames_in,
    cotangent,
    video_ids,
    frame_device,
    msg_weight,
    msg_gain,
    msg_qkv,
    msg_out,
    attn_gain,
    attn_qkv,
    attn_out,
    mlp_gain,
    up_weight,
    down_weight,
):
    count, frame_len, width = frames_in.shape
    owners, parts = lax.axis_size("frames"), lax.axis_size("rows")
    hidden_width = up_weight.shape[1]
    own = -(-count // 16) * 16
    steps = count // GROUP
    block_index = lax.axis_index("frames").astype(jnp.int32).reshape(1)
    extra = ((0, own - count), (0, 0))

    ids = (video_ids * owners + frame_device)[:, None]
    base = int(BASE)
    digits = jnp.concatenate([ids % base, ids // base % base, ids // (base * base)], axis=1)
    digits = jnp.pad(digits, ((0, own - count), (0, LANES - DIGITS)), constant_values=-1)
    payload = jnp.concatenate([jnp.pad(frames_in[:, 0, :], extra), digits.astype(BFLOAT)], axis=1)
    gather = Gather("frames", payload)
    gather.begin()
    frames = tied(frames_in, payload)
    early = steps // 2
    projected = meet(project(frames, attn_gain, attn_qkv, 0, early, None), gather)
    gather.end()
    gather.begin()
    (proj,) = project(
        tied(frames, gather.values), attn_gain, attn_qkv, early, steps - early, projected
    )
    proj = meet(proj, gather)
    gather.end()

    *saved, message, token_kv = message_forward(
        gather.pieces, own, msg_weight, msg_gain, msg_qkv, msg_out, attn_gain, attn_qkv
    )
    token_kv = token_kv[:count, None]
    message = message[:count, None]
    expo, mixed, scale, residual = attend(frames_in, proj, token_kv, attn_out)
    cot, second, act, grad_up, branch, grad_mixed, delta, mlp_gain_grad = mlp(
        residual, cotangent, mlp_gain, up_weight, down_weight, attn_out, mixed, scale
    )

    core = (lax.axis_index("rows") % 2).astype(jnp.int32).reshape(1)
    tile = 3 * LANES
    tiles = hidden_width // tile
    down = Sum.of_cores(*down_grad(core, cot, act, parts, tile))
    lanes = hidden_width // parts
    out_lanes = -(-width // parts // LANES) * LANES
    shape = (parts // 2, width, lanes + out_lanes)
    out_sums = split_grad(
        core,
        tied(mixed, down.sent),
        branch,
        mlp_gain_grad,
        256,
        parts,
        shape,
        lanes // out_lanes,
        "grad_attn_out",
    )
    out_sums = meet(out_sums, down)
    down.end(apart=True)
    split = tiles * 3 // 4
    down_a, down_b = Sum(down.terms), Sum(down.terms)
    sent = down_a.begin("rows", 2, 0, (1, 0, split))
    up_sums = up_grad(core, tied(second, sent), grad_up, parts, out_sums)
    up = Sum.of_cores(*meet(up_sums, down_a))

    def finish_output(first, number, prior, *others):
        return mlp_output(
            tied(residual, *others), act, down_weight, frames_in.shape, first, number, prior
        )

    pieces = (2, steps - 4, 2)
    down_a.end(apart=True)
    sent = [up.sent, down_b.begin("rows", 2, 0, (1, split, tiles - split))]
    output = meet(finish_output(0, pieces[0], None, sent), down_b, up)
    down_b.end(apart=True)
    down = joined(down_a, down_b, 0)
    if tiles != owners:
        moved = jnp.swapaxes(down.terms[0], 0, 1).reshape(width // parts, owners, -1)
        down.terms = [jnp.swapaxes(moved, 0, 1)]
    up.end(apart=True)
    split = shape[-1] // 2
    up_a, up_b = up.part(np.s_[..., :split]), up.part(np.s_[..., split:])
    sent = [down.begin_frames(), up_a.begin("rows", 2, 0), up_b.begin_frames(1)]
    grads = attend_back(
        core,
        proj,
        token_kv,
        expo,
        tied(grad_mixed, sent),
        delta,
        frames_in,
        branch,
        message,
        attn_gain,
        attn_qkv,
        parts,
    )
    grad_in, class_rows, message_grad, *qkv_sums = meet(grads, down, up_a, up_b)
    message_grad = jnp.pad(message_grad.reshape(count, width), extra)
    gather = Gather("frames", message_grad)
    gather.begin()
    qkv_a, qkv_b = (Sum.of_cores(qkv_sums[i], qkv_sums[2 + i]) for i in range(2))
    for one in (down, up_a, up_b):
        one.end()
    gather.end()
    gather.begin(direct=False)
    for one in (down, up_a, up_b):
        one.terms = tied(one.terms, gather.got)
    sent = [gather.values, down.step_frames(), up_a.begin_frames(), up_b.begin("rows", 2, 0)]
    sent = meet(sent, qkv_a, qkv_b)
    qkv_a.end()
    qkv_b.end()
    sent = [sent, qkv_a.begin("rows", 2, 0), qkv_b.begin_frames(1)]
    output = finish_output(pieces[0], pieces[1], output, sent)
    output = meet(output, gather, down, up_a, up_b, qkv_a, qkv_b)
    gather.end()
    gather.begin(direct=False)
    down.end(apart=True)
    up_a.end(apart=True)
    up_b.end(apart=True)
    up = joined(up_a, up_b, 2)
    qkv_a.end()
    qkv_b.end()
    sent = [
        gather.values,
        down.begin_last(),
        up.step_frames(),
        qkv_a.begin_frames(),
        qkv_b.begin("rows", 2, 0),
    ]
    output = finish_output(sum(pieces[:2]), pieces[2], output, sent)
    output = meet(output, gather, down, up, qkv_a, qkv_b)
    gather.end()
    up.end(apart=True)
    qkv_a.end(apart=True)
    qkv_b.end(apart=True)
    qkv = joined(qkv_a, qkv_b, 2)
    down.end(apart=True)
    grad_down = down.total().T
    sent = [up.begin_last(), qkv.begin_last(), grad_down]
    grads = message_back(
        block_index,
        parts,
        width // owners,
        own,
        tied(gather.pieces, sent),
        saved,
        msg_weight,
        msg_gain,
        msg_qkv,
        msg_out,
    )
    class_grad, msg_sums = meet(grads, qkv)
    msg = Sum([msg_sums.reshape(2, 2, *msg_sums.shape[1:])])
    msg.begin("rows", 1, 1)
    msg.end()
    sent = msg.begin("rows", 2, 0)
    class_grad, qkv.got = tied((class_grad, qkv.got), sent)
    class_rows = (class_rows[:, 0] + class_grad[:count]).astype(BFLOAT)
    grad_in = lax.dynamic_update_slice(grad_in, class_rows[:, None], (0, 0, 0))
    for one in (up, qkv, msg):
        one.end(apart=True)
    grad_up, grad_qkv, msg_total = up.total(), qkv.total(), msg.total()
    third, fourth, fifth = (n * width // parts for n in (3, 4, 5))
    return (
        output[0],
        grad_in,
        msg_total[:, third:fourth],
        msg_total[:, fifth],
        msg_total[:, :third],
        msg_total[:, fourth:fifth],
        grad_qkv[:, third],
        grad_qkv[:, :third],
        grad_up[:, lanes : lanes + width // parts],
        grad_up[:, lanes + width // parts],
        grad_up[:, :lanes],
        grad_down,
    )


def solution(mesh):
    split = P(("frames", "rows"))
    matrix = P("frames", "rows")
    gain = P("frames")
    return jax.shard_map(
        per_device,
        mesh=mesh,
        in_specs=(split, split, split, split) + (P(),) * 10,
        out_specs=(
            split,
            split,
            matrix,
            gain,
            matrix,
            matrix,
            gain,
            matrix,
            matrix,
            gain,
            matrix,
            matrix,
        ),
        check_vma=False,
    )
```
